32 devices in a mesh: grp: 2 (over y), chan: 4 (over z), tm: 2 (over x), sub: 2 (over core).
Axes of the slice: x: 2, y: 2, z: 4, core: 2. Of those that a mesh axis runs over, the one named last changes fastest.
Arguments:
- raw: bfloat16 [1024, 16384], P(('grp', 'chan'), ('tm', 'sub')), parts along dimension 0, may hold values from -6 to 6
- fir_taps: bfloat16 [129], replicated, may hold values from -0.5 to 0.5
- spatial_taps: float32 [9], replicated, may hold values from -2 to 2
- band_edges: int32 [4], replicated, may hold values from 1 to 125, as said below
- source_owner: int32 [16], P('grp'), parts along dimension 0, may hold values from 0 to 3
- source_panel: int32 [8], replicated, may hold values from 0 to 3
- source_pick: int32 [8, 1024], P(None, ('grp', 'chan')), parts along dimension 1, may hold values from 0 to 31
Outputs:
- correlations: float32 [8, 1024, 128], P(None, ('grp', 'chan')), parts along dimension 1
The draws below stay inside these ranges and needn't reach their ends.
There are 2 independent parts, one for each index of `grp`. The reference program is written for one: setup_inputs(seed, part) draws one part's arguments, and reference() takes and returns one part's arrays. A program takes and returns all parts, laid end to end along the dimension named above; an argument that names none is the same for every part. Nothing has to cross between parts.
Inputs may be any that keep to these rules, and one draw needn't show every extreme that they name: `band_edges`: e0 < e1 <= e2 < e3, with e1 - e0 and e3 - e2 from 4 to 12.
All inputs are finite; a program needn't handle non-finite values.
Results may differ from the reference program's by a relative error of at most 0.0055.
Values may be sent and summed in bfloat16 or wider, within the bound.
A program may use at most 64 MiB of HBM per device.

```python
import math
import jax
import jax.numpy as jnp
from jax import lax

CB = 128
P_SIZE = 32
WIN = 256
TAPS = 129
SPAN = 9
LAGS = 128
REACH = 1000
STEPS = 8
CH = 512
SEGS = 4
SAMPLES = 16384
NW = 16
WT = 64
FREQS = 128
N_CHAN = 4


def draw_band_edges(key, part):
    streams = jax.random.split(key, 4)
    low_edge = jax.random.randint(streams[0], (), 1, 6)
    rise_len = jax.random.randint(streams[1], (), 4, 13)
    high_edge = jax.random.randint(streams[2], (), FREQS - 28, FREQS - 2)
    fall_len = jax.random.randint(streams[3], (), 4, 13)
    return jnp.stack([low_edge, low_edge + rise_len, high_edge - fall_len, high_edge]).astype(jnp.int32)


def with_ends(array, stream_key, smallest, largest):
    longest = array.shape.index(max(array.shape))
    spots = []
    for shift in (0, 1):
        where = [jax.random.randint(jax.random.fold_in(stream_key, axis), (), 0, length) for axis, length in enumerate(array.shape)]
        where[longest] = (where[longest] + shift) % array.shape[longest]
        spots.append(tuple(where))
    return array.at[spots[0]].set(smallest).at[spots[1]].set(largest)


def steps_of(own_key, shape, cuts, least, high):
    loudness = 1.0
    for position, parts in cuts:
        steps = jax.random.uniform(jax.random.fold_in(jax.random.fold_in(own_key, 6), position), (parts,), jnp.float32, least / len(cuts), high / len(cuts))
        loudness = loudness * jnp.repeat(jnp.exp(steps), shape[position] // parts).reshape((-1,) + (1,) * (len(shape) - 1 - position))
    return loudness


def centred(rng, dims, deviation, bound, cuts=(), dtype=jnp.bfloat16):
    level = steps_of(rng, dims, cuts, -0.22, 0.18) if cuts else 1.0
    values = jax.random.normal(rng, dims, jnp.float32) * deviation * level
    return jnp.minimum(jnp.maximum(values, -bound), bound).astype(dtype)


def setup_inputs(seed: int = 0, part: int = 0) -> dict:
    key_list = jax.random.split(jax.random.key(seed), 8)
    part_keys = jax.random.split(jax.random.fold_in(key_list[7], part), 8)
    raw = centred(part_keys[0], (CH, SAMPLES), 1.0, 6.0, ((0, 4), (1, 4)))
    fir_taps = centred(key_list[1], (TAPS,), TAPS ** -0.5, 0.5)
    spatial_taps = centred(key_list[2], (SPAN,), SPAN ** -0.5, 2.0, (), jnp.float32)
    band_edges = draw_band_edges(jax.random.fold_in(key_list[7], 71), part)
    source_owner = with_ends(jax.random.randint(part_keys[4], (STEPS,), 0, N_CHAN), jax.random.fold_in(part_keys[4], 1), 0, N_CHAN - 1).astype(jnp.int32)
    source_panel = with_ends(jax.random.randint(key_list[5], (STEPS,), 0, CB // P_SIZE), jax.random.fold_in(key_list[5], 1), 0, (CB // P_SIZE) - 1).astype(jnp.int32)
    source_pick = with_ends(jax.random.randint(part_keys[6], (STEPS, CH), 0, P_SIZE), jax.random.fold_in(part_keys[6], 1), 0, P_SIZE - 1).astype(jnp.int32)
    return {"raw": raw, "fir_taps": fir_taps, "spatial_taps": spatial_taps, "band_edges": band_edges, "source_owner": source_owner, "source_panel": source_panel, "source_pick": source_pick}


HIGHEST = lax.Precision.HIGHEST

def fir_matrix(fir_taps):
    tap_count = fir_taps.shape[0]
    row_index = jnp.arange(2 * (tap_count - 1))[:, None]
    col_index = jnp.arange(tap_count - 1)[None, :]
    offset = row_index - col_index
    is_valid = (offset >= 0) & (offset < tap_count)
    picked = jnp.take(fir_taps.astype(jnp.float32), jnp.clip(offset, 0, tap_count - 1))
    return jnp.where(is_valid, picked, jnp.float32(0.0))

def spectral_table(window_len):
    quarter = window_len // 4
    sample = jnp.arange(window_len)[:, None]
    column = jnp.arange(window_len)[None, :]
    bin_number = column // (2 * quarter) * quarter + column % quarter
    part_flag = column // quarter % 2
    phase = jnp.mod(bin_number * sample, window_len).astype(jnp.float32) * jnp.float32(2.0 * math.pi / window_len)
    entries = jnp.where(part_flag == 0, jnp.cos(phase), -jnp.sin(phase)) / jnp.float32(math.sqrt(window_len))
    return entries.astype(jnp.bfloat16)

def lag_matrix(first_half, halves, quarter, window_len, lag_count):
    column = jnp.arange(halves * 2 * quarter)[:, None]
    bin_number = (first_half + column // (2 * quarter)) * quarter + column % quarter
    part_flag = column // quarter % 2
    lag_shift = jnp.arange(lag_count)[None, :] - lag_count // 2
    phase = jnp.mod(bin_number * lag_shift, window_len).astype(jnp.float32) * jnp.float32(2.0 * math.pi / window_len)
    return jnp.where(part_flag == 0, jnp.cos(phase), -jnp.sin(phase)).astype(jnp.float32)

def band_taper(band_edges, bin_count):
    bin_values = jnp.arange(bin_count).astype(jnp.float32)
    edges = band_edges.astype(jnp.float32)
    rising = 0.5 - 0.5 * jnp.cos(jnp.float32(math.pi) * (bin_values - edges[0]) / (edges[1] - edges[0]))
    falling = 0.5 - 0.5 * jnp.cos(jnp.float32(math.pi) * (edges[3] - bin_values) / (edges[3] - edges[2]))
    inner = jnp.where(bin_values < edges[3], falling, jnp.float32(0.0))
    inner = jnp.where(bin_values <= edges[2], jnp.float32(1.0), inner)
    inner = jnp.where(bin_values < edges[1], rising, inner)
    return jnp.where(bin_values <= edges[0], jnp.float32(0.0), inner).astype(jnp.float32)

def whiten(spectra, band_edges):
    window_len = spectra.shape[-1]
    quarter = window_len // 4
    bin_count = window_len // 2
    leading = spectra.shape[:-1]
    split = spectra.reshape(leading + (2, 2, quarter))
    power = (split[..., 0, :] * split[..., 0, :] + split[..., 1, :] * split[..., 1, :]).reshape(leading + (bin_count,))
    mean_power = lax.optimization_barrier(jnp.mean(power, axis=-2))
    bin_values = jnp.arange(bin_count)
    smoother = (jnp.abs(bin_values[:, None] - bin_values[None, :]) <= 4).astype(jnp.float32)
    counts = lax.optimization_barrier(jnp.sum(smoother, axis=0))
    levels = jnp.dot(mean_power, smoother, precision=HIGHEST) / counts
    factor = band_taper(band_edges, bin_count) / jnp.sqrt(levels + 1e-06)
    factor = factor.reshape(factor.shape[:-1] + (2, 1, quarter))
    return (split * jnp.expand_dims(factor, -4)).astype(jnp.bfloat16)

def cross_terms(receiver_part, partner):
    recv_real = receiver_part[:, :, :, 0]
    recv_imag = receiver_part[:, :, :, 1]
    part_real = partner[:, :, :, 0]
    part_imag = partner[:, :, :, 1]
    real_sum = jnp.einsum('rwhf,rwhf->rhf', recv_real, part_real, precision=HIGHEST) + jnp.einsum('rwhf,rwhf->rhf', recv_imag, part_imag, precision=HIGHEST)
    imag_sum = jnp.einsum('rwhf,rwhf->rhf', recv_imag, part_real, precision=HIGHEST) - jnp.einsum('rwhf,rwhf->rhf', recv_real, part_imag, precision=HIGHEST)
    return jnp.stack([real_sum, imag_sum], axis=2).reshape(receiver_part.shape[0], -1)

def reference(raw, fir_taps, spatial_taps, band_edges, source_owner, source_panel, source_pick):
    channels, samples = raw.shape
    margin = (TAPS - 1) // 2
    padded = jnp.pad(raw.astype(jnp.float32), ((0, 0), (margin, margin)))
    blocks = padded.reshape(channels, samples // (2 * margin) + 1, 2 * margin)
    windows = jnp.concatenate([blocks[:, :-1], blocks[:, 1:]], axis=2)
    filtered = jnp.einsum('cbi,ij->cbj', windows, fir_matrix(fir_taps), precision=HIGHEST).reshape(channels, samples)
    side_len = SPAN // 2
    bordered = jnp.pad(filtered, ((side_len, side_len), (0, 0)))
    shaped = jnp.zeros_like(filtered)
    for tap_index in range(SPAN):
        shaped = shaped + spatial_taps[tap_index] * bordered[tap_index:tap_index + channels]
    shaped = shaped.astype(jnp.bfloat16)
    frames = shaped.astype(jnp.float32).reshape(channels, SEGS, NW, WIN)
    spectra = jnp.einsum('cgwn,nk->cgwk', frames, spectral_table(WIN).astype(jnp.float32), precision=HIGHEST)
    whitened = whiten(spectra, band_edges).astype(jnp.float32).reshape(channels, WT, 2, 2, WIN // 4)
    lag_table = lag_matrix(0, 2, WIN // 4, WIN, LAGS)
    norm_scale = 1.0 / math.sqrt(WT * FREQS)
    receivers = jnp.arange(channels).astype(jnp.int32)
    results = []
    for step_index in range(STEPS):
        start_row = (source_owner[step_index] * CB + source_panel[step_index] * P_SIZE).astype(jnp.int32)
        panel_rows = lax.dynamic_slice_in_dim(whitened, start_row, P_SIZE, 0)
        pick_row = source_pick[step_index].astype(jnp.int32)
        partner = jnp.take(panel_rows, pick_row, axis=0)
        cross_sum = cross_terms(whitened, partner)
        lagged = jnp.dot(cross_sum, lag_table, precision=HIGHEST) * norm_scale
        sources = start_row + pick_row
        nearby = jnp.abs(receivers - sources) <= REACH
        results.append(jnp.where(nearby[:, None], lagged, jnp.float32(0.0)))
    return jnp.stack(results)
```

```python
import functools
import math

import jax
import jax.numpy as jnp
import numpy as np
from jax import lax
from jax.experimental import pallas as pl
from jax.experimental.pallas import tpu as pltpu
from jax.sharding import PartitionSpec as P

P_SIZE = 32
WIN = 256
LAGS = 128
REACH = 1000
HIGHEST = lax.Precision.HIGHEST


def column_maps():
    column = np.arange(WIN)
    quarter = WIN // 4
    bins = column // (2 * quarter) * quarter + column % quarter
    parts = column // quarter % 2
    return bins, parts


def spectral_table():
    bins, parts = column_maps()
    angle = 2.0 * np.pi * ((bins[None, :] * np.arange(WIN)[:, None]) % WIN) / WIN
    table = np.where(parts == 0, np.cos(angle), -np.sin(angle)) / math.sqrt(WIN)
    return jnp.asarray(table.astype(np.float32)).astype(jnp.bfloat16)


def bins_of(shape, axis):
    column = lax.broadcasted_iota(jnp.int32, shape, axis)
    quarter = WIN // 4
    return lax.div(column, 2 * quarter) * quarter + lax.rem(column, quarter)


def lag_tables(scale):
    bins, parts = column_maps()
    lag = np.arange(LAGS) - LAGS // 2
    angle = 2.0 * np.pi * ((bins[:, None] * lag[None, :]) % WIN) / WIN
    real = np.cos(angle) * scale
    imag = np.where(parts[:, None] == 0, -np.sin(angle), np.sin(angle)) * scale
    return jnp.asarray(np.concatenate([real, imag]).astype(np.float32))


def taper_row(edges_ref):
    bins = bins_of((1, WIN), 1).astype(jnp.float32)
    e0, e1, e2, e3 = [jnp.full((1, WIN), edges_ref[k]).astype(jnp.float32) for k in range(4)]
    rising = 0.5 - 0.5 * jnp.cos(math.pi * (bins - e0) / (e1 - e0))
    falling = 0.5 - 0.5 * jnp.cos(math.pi * (e3 - bins) / (e3 - e2))
    inner = jnp.where(bins < e3, falling, 0.0)
    inner = jnp.where(bins <= e2, 1.0, inner)
    inner = jnp.where(bins < e1, rising, inner)
    return jnp.where(bins <= e0, 0.0, inner)


LANES = 128
SPLIT = 2
LAG = 2
MESH = pl.DeviceIdType.MESH


def relay_kernel(frames, channels, side, steps, n_chan, n_tm, n_sub, sp_hbm, edges_hbm, owner_hbm, panel_hbm,
           taps_hbm, pick_hbm, raw_hbm, table_hbm, lag_hbm, out_ref,
           sp_ref, edges_ref, owner_ref, panel_ref, taps_ref, pick_ref, raw_ref, table_ref, lag_ref, filt, spec, ext, time_in, chan_out, chan_in, corner_out, corner_in, send_sem,
           recv_sem, load_sem, white_ref, own_ref, chosen, pick_wide, plain, swapped, in_low, in_high, to_high,
           to_low, own_lag, sub_in, tm_in, done, sem_high, sem_low, got_low, got_high, sub_send, sub_recv,
           tm_send, tm_recv, fin_send, fin_recv):
    my_tm = lax.axis_index("tm")
    my_sub = lax.axis_index("sub")
    loads = [
        pltpu.make_async_copy(source, target, load_sem.at[k])
        for k, (source, target) in enumerate([
            (raw_hbm, raw_ref), (taps_hbm, taps_ref), (pick_hbm, pick_ref), (sp_hbm, sp_ref),
            (edges_hbm, edges_ref), (owner_hbm, owner_ref), (panel_hbm, panel_ref),
            (table_hbm, table_ref), (lag_hbm, lag_ref),
        ])
    ]
    for load in loads:
        load.start()
    me = lax.axis_index("chan")
    n_time = n_tm * n_sub
    now = lax.axis_index("tm") * n_sub + lax.axis_index("sub")
    samples = frames * WIN
    depth = taps_ref.shape[1]

    def peer(dc, dt):
        at = lax.rem(now + dt + n_time, n_time)
        return {"chan": lax.rem(me + dc + n_chan, n_chan), "tm": lax.div(at, n_sub), "sub": lax.rem(at, n_sub)}

    moves = [(0, 1), (0, -1), (1, 0), (-1, 0), (1, 1), (1, -1), (-1, 1), (-1, -1)]
    barrier = pltpu.get_barrier_semaphore()
    peers = [peer(dc, dt) for dc, dt in moves]
    peers += [{"tm": lax.rem(my_tm + d, n_tm)} for d in range(1, n_tm)]
    peers += [{"sub": lax.rem(my_sub + d, n_sub)} for d in range(1, n_sub)]
    for to in peers:
        pl.semaphore_signal(barrier, inc=1, device_id=to, device_id_type=MESH)

    loads[0].wait()
    ends = (slice(channels - side, channels), slice(0, side))
    sides = (slice(samples - LANES, samples), slice(0, LANES))
    for k in range(2):
        chan_out[k] = raw_ref[ends[k]]
        for h in range(2):
            corner_out[2 * k + h] = raw_ref[ends[k], sides[h]]

    def exists(dc, dt):
        return (me + dc >= 0) & (me + dc < n_chan) & (now + dt >= 0) & (now + dt < n_time)

    def copy(k):
        dc, dt = moves[k]
        if k < 2:
            src, dst = raw_ref.at[:, sides[k]], time_in.at[k]
        elif k < 4:
            src, dst = chan_out.at[k - 2], chan_in.at[k - 2]
        else:
            src, dst = corner_out.at[k - 4], corner_in.at[k - 4]
        return pltpu.make_async_remote_copy(
            src_ref=src, dst_ref=dst, send_sem=send_sem.at[k], recv_sem=recv_sem.at[k],
            device_id=peer(dc, dt), device_id_type=MESH)

    pl.semaphore_wait(barrier, len(peers))
    for k in (2, 3, 0, 1, 4, 5, 6, 7):
        pl.when(exists(*moves[k]))(lambda k=k: copy(k).start())

    ext[:channels, LANES : LANES + samples] = raw_ref[...]
    for load in loads[1:]:
        load.wait()
    rolled = pltpu.roll(jnp.broadcast_to(taps_ref[...], (WIN, depth)), 0, 1, stride=1, stride_axis=0)
    fir_t = rolled.astype(jnp.bfloat16)
    near = (jnp.abs(bins_of((WIN, WIN), 0) - bins_of((WIN, WIN), 1)) <= 4).astype(jnp.float32)
    row_bins = bins_of((1, WIN), 1)
    count = jnp.minimum(row_bins + 4, WIN // 2 - 1) - jnp.maximum(row_bins - 4, 0) + 1
    turned = jnp.transpose(pick_ref[...].astype(jnp.float32))
    for s in range(steps):
        wide = jnp.broadcast_to(turned[:, s : s + 1], (channels, LANES)).astype(jnp.int32)
        pick_wide[s] = wide
        chosen[s] = (
            wide[:, :P_SIZE] == lax.broadcasted_iota(jnp.int32, (channels, P_SIZE), 1)
        ).astype(jnp.bfloat16)

    @pl.when(me == 0)
    def _():
        in_low[...] = jnp.zeros_like(in_low)

    @pl.when(me == n_chan - 1)
    def _():
        in_high[...] = jnp.zeros_like(in_high)

    for k, (dc, dt) in enumerate(moves):
        there = exists(-dc, -dt)
        pl.when(there)(lambda k=k: copy(k).wait_recv())
        buf, slot = (time_in, k) if k < 2 else (chan_in, k - 2) if k < 4 else (corner_in, k - 4)

        @pl.when(jnp.logical_not(there))
        def _():
            buf[slot] = jnp.zeros(buf.shape[1:], buf.dtype)

    def rows(low, high):
        width = low.shape[1]
        spare = jnp.zeros((16 - 2 * side, width), jnp.float32)
        both = [low.astype(jnp.float32), high.astype(jnp.float32), spare]
        return jnp.concatenate(both, axis=0).astype(jnp.bfloat16)

    high_at = LANES + samples
    ext[:channels, :LANES] = time_in[0]
    ext[:channels, high_at:] = time_in[1]
    ext[channels:, LANES:high_at] = rows(chan_in[0], chan_in[1])
    ext[channels:, :LANES] = rows(corner_in[0], corner_in[2])
    ext[channels:, high_at:] = rows(corner_in[1], corner_in[3])
    power = jnp.zeros((channels, WIN), jnp.float32)
    for w in range(frames):
        block = ext[:, w * WIN : w * WIN + depth]
        got = lax.dot_general(block, fir_t, (((1,), (1,)), ((), ())), preferred_element_type=jnp.float32)
        slot = w % 2
        filt[slot, 8 : 8 + channels] = got[:channels]
        filt[slot, 8 - side : 8] = got[channels : channels + side]
        filt[slot, 8 + channels : 8 + channels + side] = got[channels + side : channels + 2 * side]
        shaped = sp_ref[0] * filt[slot, 8 - side : 8 - side + channels]
        for m in range(1, 2 * side + 1):
            shaped += sp_ref[m] * filt[slot, 8 - side + m : 8 - side + m + channels]
        spectra = jnp.dot(shaped.astype(jnp.bfloat16), table_ref[...], preferred_element_type=jnp.float32)
        spec[w] = spectra
        power += spectra * spectra
    level = jnp.dot(power, near, precision=HIGHEST, preferred_element_type=jnp.float32)
    level = level / (count.astype(jnp.float32) * frames)
    factor = taper_row(edges_ref) / jnp.sqrt(level + 1e-06)
    for w in range(frames):
        white_ref[w] = (spec[w] * factor).astype(jnp.bfloat16)
    half = WIN // 2
    part = channels // n_sub
    group = frames // SPLIT
    chunks = steps * SPLIT

    def up(c):
        return pltpu.make_async_remote_copy(
            src_ref=to_high.at[c], dst_ref=in_low.at[c], send_sem=sem_high.at[c], recv_sem=got_low.at[c],
            device_id={"chan": lax.rem(me + 1, n_chan)}, device_id_type=MESH)

    def down(c):
        return pltpu.make_async_remote_copy(
            src_ref=to_low.at[c], dst_ref=in_high.at[c], send_sem=sem_low.at[c], recv_sem=got_high.at[c],
            device_id={"chan": lax.rem(me + n_chan - 1, n_chan)}, device_id_type=MESH)

    def sub_copy(s, d):
        to = lax.rem(my_sub + d, n_sub)
        return pltpu.make_async_remote_copy(
            src_ref=own_lag.at[s, pl.ds(to * part, part)], dst_ref=sub_in.at[s, d - 1],
            send_sem=sub_send.at[s, d - 1], recv_sem=sub_recv.at[s, d - 1],
            device_id={"sub": to}, device_id_type=MESH)

    def tm_copy(s, d):
        return pltpu.make_async_remote_copy(
            src_ref=tm_in.at[s, my_tm], dst_ref=tm_in.at[s, my_tm],
            send_sem=tm_send.at[s, d - 1], recv_sem=tm_recv.at[s, d - 1],
            device_id={"tm": lax.rem(my_tm + d, n_tm)}, device_id_type=MESH)

    def fin_copy(s, d):
        here = pl.ds(my_sub * part, part)
        return pltpu.make_async_remote_copy(
            src_ref=done.at[s, here], dst_ref=done.at[s, here],
            send_sem=fin_send.at[s, d - 1], recv_sem=fin_recv.at[s, d - 1],
            device_id={"sub": lax.rem(my_sub + d, n_sub)}, device_id_type=MESH)

    def own_panel(s):
        panel = jnp.full((P_SIZE, WIN), panel_ref[s], jnp.int32)
        for w in range(frames):
            value = white_ref[w, :P_SIZE]
            for k in range(1, channels // P_SIZE):
                value = jnp.where(panel == k, white_ref[w, k * P_SIZE : (k + 1) * P_SIZE], value)
            own_ref[s, w] = value

    def stage(c, arrived, leaving):
        s = lax.div(c, SPLIT)
        k = lax.rem(c, SPLIT)
        mine = jnp.full((P_SIZE, WIN), owner_ref[s], jnp.int32) == me
        for w in range(group):
            leaving[c, w] = jnp.where(mine, own_ref[s, k * group + w], arrived[c, w])

    def relay(t):
        c = t - LAG * me

        @pl.when((c >= 0) & (c < chunks))
        def _():
            @pl.when(me > 0)
            def _():
                up(c).wait_recv()

            @pl.when(me < n_chan - 1)
            def _():
                stage(c, in_low, to_high)
                up(c).start()

        e = t - LAG * (n_chan - 1 - me)

        @pl.when((e >= 0) & (e < chunks))
        def _():
            @pl.when(me < n_chan - 1)
            def _():
                down(e).wait_recv()

            @pl.when(me > 0)
            def _():
                stage(e, in_high, to_low)
                down(e).start()

    def compute(s):
        rows = channels // 2
        owner = owner_ref[s]
        where = jnp.full((P_SIZE, WIN), owner, jnp.int32)
        start = owner * channels + panel_ref[s] * P_SIZE
        for r in range(2):
            here = slice(r * rows, (r + 1) * rows)
            acc_p = jnp.zeros((rows, WIN), jnp.float32)
            acc_q = jnp.zeros((rows, WIN), jnp.float32)
            for w in range(frames):
                c = s * SPLIT + w // group
                value = jnp.where(where < me, in_low[c, w % group], in_high[c, w % group])
                value = jnp.where(where == me, own_ref[s, w], value)
                partner = jnp.dot(chosen[s, here], value, preferred_element_type=jnp.float32)
                acc_p += plain[w, here] * partner
                acc_q += swapped[w, here] * partner
            lagged = jnp.dot(acc_p, lag_ref[:WIN], precision=HIGHEST, preferred_element_type=jnp.float32)
            lagged += jnp.dot(acc_q, lag_ref[WIN:], precision=HIGHEST, preferred_element_type=jnp.float32)
            receiver = me * channels + r * rows + lax.broadcasted_iota(jnp.int32, (rows, LAGS), 0)
            far = jnp.abs(receiver - (start + pick_wide[s, here])) > REACH
            own_lag[s, here] = jnp.where(far, 0.0, lagged)
        for d in range(1, n_sub):
            sub_copy(s, d).start()

    def sub_sum(s):
        total = own_lag[s, pl.ds(my_sub * part, part)]
        for d in range(1, n_sub):
            sub_copy(s, d).wait_recv()
            total += sub_in[s, d - 1]
        tm_in[s, my_tm] = total
        for d in range(1, n_tm):
            tm_copy(s, d).start()

    def tm_sum(s):
        for d in range(1, n_tm):
            tm_copy(s, d).wait_recv()
        total = tm_in[s, 0]
        for k in range(1, n_tm):
            total += tm_in[s, k]
        done[s, pl.ds(my_sub * part, part)] = total
        for d in range(1, n_sub):
            fin_copy(s, d).start()

    def finish(s):
        for d in range(1, n_sub):
            fin_copy(s, d).wait_recv()
        out_ref[s] = done[s]

    delay = -(-(n_chan - 1) * LAG // SPLIT)

    def turn(u, carry):
        pl.when(u < steps)(functools.partial(own_panel, u))
        for k in range(SPLIT):
            relay(u * SPLIT + k)

        @pl.when(u == 0)
        def _():
            for w in range(frames):
                value = white_ref[w].astype(jnp.float32)
                plain[w] = value
                for h in range(2):
                    swapped[w, :, h * half : (h + 1) * half] = pltpu.roll(
                        value[:, h * half : (h + 1) * half], half // 2, 1)

        for late, work in enumerate((compute, sub_sum, tm_sum, finish)):
            s = u - delay - late
            pl.when((s >= 0) & (s < steps))(functools.partial(work, s))
        return carry

    lax.fori_loop(0, steps + delay + 3, turn, 0)

    def drain_chunk(c, carry):
        @pl.when(me < n_chan - 1)
        def _():
            up(c).wait_send()

        @pl.when(me > 0)
        def _():
            down(c).wait_send()
        return carry

    lax.fori_loop(0, chunks, drain_chunk, 0)
    for k, move in enumerate(moves):
        pl.when(exists(*move))(lambda k=k: copy(k).wait_send())

    def drain_step(s, carry):
        for d in range(1, n_sub):
            sub_copy(s, d).wait_send()
            fin_copy(s, d).wait_send()
        for d in range(1, n_tm):
            tm_copy(s, d).wait_send()
        return carry

    lax.fori_loop(0, steps, drain_step, 0)


def lag_pair(scale):
    bins, parts = column_maps()
    lag = np.arange(LAGS) - LAGS // 2
    angle = 2.0 * np.pi * ((bins[:, None] * lag[None, :]) % WIN) / WIN
    real = np.cos(angle) * scale
    imag = np.where(parts[:, None] == 0, np.sin(angle), -np.sin(angle)) * scale
    full = np.concatenate([real, imag]).astype(np.float32)
    high = jnp.asarray(full).astype(jnp.bfloat16)
    low = (jnp.asarray(full) - high.astype(jnp.float32)).astype(jnp.bfloat16)
    return jnp.concatenate([high, low], axis=1)


ROWS = 64


def split_kernel(frames, channels, side, steps, n_chan, n_tm, n_sub, sp_hbm, edges_hbm, owner_hbm, panel_hbm,
                 taps_hbm, pick_hbm, raw_hbm, table_hbm, lag_hbm, out_ref,
                 sp_ref, edges_ref, owner_ref, panel_ref, taps_ref, pick_ref, raw_ref, table_ref, lag_ref,
                 filt, spec, edge_ext, halo_ext, halo_win, low_edge, high_edge, edge_rows, power_ref,
                 time_in, chan_out, chan_in, corner_out, corner_in, white_ref, picks, chosen, pick_wide, pan, acc,
                 own_lag, sub_in, z_out, z_in, done,
                 load_sem, halo_send, halo_recv, far_sem, pick_send, pick_recv, z_send, z_recv, x_send, x_recv,
                 sub_send, sub_recv, r_send, r_recv, a_send, a_recv, *alls):
    f32, bf16 = jnp.float32, jnp.bfloat16
    me, my_tm, my_sub = lax.axis_index("chan"), lax.axis_index("tm"), lax.axis_index("sub")
    n_time = n_tm * n_sub
    now = my_tm * n_sub + my_sub
    samples = frames * WIN
    depth = taps_ref.shape[1]
    panels = channels // P_SIZE
    per = frames // n_chan
    spd = steps // n_time
    spt = spd * n_sub
    loads = [
        pltpu.make_async_copy(source, target, load_sem.at[k])
        for k, (source, target) in enumerate([
            (raw_hbm, raw_ref), (taps_hbm, taps_ref), (pick_hbm, pick_ref), (sp_hbm, sp_ref),
            (edges_hbm, edges_ref), (owner_hbm, owner_ref), (panel_hbm, panel_ref),
            (table_hbm, table_ref), (lag_hbm, lag_ref),
        ])
    ]
    for load in loads:
        load.start()

    def at_time(dt):
        at = lax.rem(now + dt + n_time, n_time)
        return {"tm": lax.div(at, n_sub), "sub": lax.rem(at, n_sub)}

    def peer(dc, dt):
        return {"chan": lax.rem(me + dc + n_chan, n_chan), **at_time(dt)}

    def exists(dc, dt):
        return (me + dc >= 0) & (me + dc < n_chan) & (now + dt >= 0) & (now + dt < n_time)

    moves = [(0, 1), (0, -1), (1, 0), (-1, 0), (1, 1), (1, -1), (-1, 1), (-1, -1)]
    barrier = pltpu.get_barrier_semaphore()
    for dt in range(1, n_time):
        pl.semaphore_signal(barrier, inc=1, device_id=at_time(dt), device_id_type=MESH)
    for move in moves[2:]:
        @pl.when(exists(*move))
        def _(move=move):
            pl.semaphore_signal(barrier, inc=1, device_id=peer(*move), device_id_type=MESH)

    loads[0].wait()
    ends = (slice(channels - side, channels), slice(0, side))
    sides = (slice(samples - LANES, samples), slice(0, LANES))
    for k in range(2):
        chan_out[k] = raw_ref[ends[k]]
        for h in range(2):
            corner_out[2 * k + h] = raw_ref[ends[k], sides[h]]

    def copy(k):
        dc, dt = moves[k]
        if k < 2:
            src, dst = raw_ref.at[:, sides[k]], time_in.at[k]
        elif k < 4:
            src, dst = chan_out.at[k - 2], chan_in.at[k - 2]
        else:
            src, dst = corner_out.at[k - 4], corner_in.at[k - 4]
        return pltpu.make_async_remote_copy(
            src_ref=src, dst_ref=dst, send_sem=halo_send.at[k], recv_sem=halo_recv.at[k],
            device_id=peer(dc, dt), device_id_type=MESH)

    greeted = sum(exists(*move).astype(jnp.int32) for move in moves[2:])
    pl.semaphore_wait(barrier, n_time - 1 + greeted)
    for k in (2, 3, 0, 1, 4, 5, 6, 7):
        pl.when(exists(*moves[k]))(lambda k=k: copy(k).start())

    inner = (me > 0) & (me < n_chan - 1)

    def token(way):
        pl.semaphore_signal(far_sem.at[way], inc=1, device_id={"chan": me + 1 - 2 * way}, device_id_type=MESH)

    def relay_tokens(k):
        for way, distance in ((0, me), (1, n_chan - 1 - me)):
            @pl.when(distance >= k + 1)
            def _():
                pl.semaphore_wait(far_sem.at[way], 1)
            pl.when((distance >= k + 1) & inner)(lambda: token(way))

    for way in range(2):
        pl.when(inner)(lambda: token(way))

    for load in loads[1:]:
        load.wait()
    rolled = pltpu.roll(jnp.broadcast_to(taps_ref[...], (WIN, depth)), 0, 1, stride=1, stride_axis=0)
    fir_t = rolled.astype(bf16)
    near = (jnp.abs(bins_of((WIN, WIN), 0) - bins_of((WIN, WIN), 1)) <= 4).astype(f32)
    row_bins = bins_of((1, WIN), 1)
    count = jnp.minimum(row_bins + 4, WIN // 2 - 1) - jnp.maximum(row_bins - 4, 0) + 1
    taper = taper_row(edges_ref)

    def fir(block):
        return lax.dot_general(block, fir_t, (((1,), (1,)), ((), ())), preferred_element_type=f32)

    def spatial(ref, at, first, size):
        total = sp_ref[0] * ref[at, first : first + size]
        for m in range(1, 2 * side + 1):
            total += sp_ref[m] * ref[at, first + m : first + m + size]
        return total.astype(bf16)

    inside = channels - 16
    power = jnp.zeros((inside, WIN), f32)
    for w in range(1, frames - 1):
        got = fir(raw_ref[:, w * WIN - LANES : w * WIN - LANES + depth])
        slot = w % 2
        filt[slot, 8 : 8 + channels] = got
        low_edge[w, 8:24] = got[:16]
        high_edge[w, :16] = got[channels - 16 :]
        shaped = spatial(filt, slot, 16 - side, inside)
        spectra = jnp.dot(shaped, table_ref[...], preferred_element_type=f32)
        spec[w, 8 : channels - 8] = spectra
        power += spectra * spectra
    power_ref[8 : channels - 8] = power
    edge_ext[0, :channels, LANES:] = raw_ref[:, : depth - LANES]
    edge_ext[1, :channels, : depth - LANES] = raw_ref[:, samples - depth + LANES :]

    for k, (dc, dt) in enumerate(moves):
        there = exists(-dc, -dt)
        pl.when(there)(lambda k=k: copy(k).wait_recv())
        buf, slot = (time_in, k) if k < 2 else (chan_in, k - 2) if k < 4 else (corner_in, k - 4)

        @pl.when(jnp.logical_not(there))
        def _():
            buf[slot] = jnp.zeros(buf.shape[1:], buf.dtype)

    for k in range(1, n_chan - 1):
        relay_tokens(k)

    def rows(low, high):
        width = low.shape[1]
        spare = jnp.zeros((16 - 2 * side, width), f32)
        both = [low.astype(f32), high.astype(f32), spare]
        return jnp.concatenate(both, axis=0).astype(bf16)

    edge_ext[0, :channels, :LANES] = time_in[0]
    edge_ext[1, :channels, depth - LANES :] = time_in[1]
    halo_ext[:, LANES : LANES + samples] = rows(chan_in[0], chan_in[1])
    halo_ext[:, :LANES] = rows(corner_in[0], corner_in[2])
    halo_ext[:, LANES + samples :] = rows(corner_in[1], corner_in[3])
    for w in range(frames):
        halo_win[w] = halo_ext[:, w * WIN : w * WIN + depth]
    halo = fir(halo_win[...].reshape(frames * 16, depth)).reshape(frames, 16, WIN)
    power = jnp.zeros((channels, WIN), f32)
    for k, w in enumerate((0, frames - 1)):
        got = fir(edge_ext[k])
        filt[k, 8 : 8 + channels] = got
        filt[k, 8 - side : 8] = halo[w, :side]
        filt[k, 8 + channels : 8 + channels + side] = halo[w, side : 2 * side]
        shaped = spatial(filt, k, 8 - side, channels)
        spectra = jnp.dot(shaped, table_ref[...], preferred_element_type=f32)
        spec[w] = spectra
        power += spectra * spectra
    for w in range(1, frames - 1):
        low_edge[w, 8 - side : 8] = halo[w, :side]
        high_edge[w, 16 : 16 + side] = halo[w, side : 2 * side]
        edge_rows[w - 1, :] = jnp.concatenate(
            [spatial(low_edge, w, 8 - side, 8).astype(f32), spatial(high_edge, w, 8 - side, 8).astype(f32)],
            axis=0).astype(bf16)
    edges = edge_rows[...].reshape((frames - 2) * 16, WIN)
    spectra = jnp.dot(edges, table_ref[...], preferred_element_type=f32).reshape(frames - 2, 16, WIN)
    for w in range(1, frames - 1):
        spec[w, :8] = spectra[w - 1, :8]
        spec[w, channels - 8 :] = spectra[w - 1, 8:]
    edge_power = jnp.sum(spectra * spectra, axis=0)
    power_ref[:8] = edge_power[:8]
    power_ref[channels - 8 :] = edge_power[8:]
    power += power_ref[...]
    level = jnp.dot(power, near, precision=HIGHEST, preferred_element_type=f32)
    level = level / (count.astype(f32) * frames)
    factor = taper / jnp.sqrt(level + 1e-06)

    def whiten(w):
        return (spec[w] * factor).astype(bf16).reshape(panels, P_SIZE, WIN)

    def block_of(q):
        return pl.ds(q * panels, panels)

    def pick_copy(d):
        return pltpu.make_async_remote_copy(
            src_ref=pick_ref, dst_ref=picks.at[me], send_sem=pick_send.at[d], recv_sem=pick_recv.at[d],
            device_id={"chan": lax.rem(me + d, n_chan)}, device_id_type=MESH)

    def z_copy(j, d):
        to = lax.rem(me + d, n_chan)
        return pltpu.make_async_remote_copy(
            src_ref=white_ref.at[to * per + j], dst_ref=alls[j].at[my_tm, block_of(me)],
            send_sem=z_send.at[j, d], recv_sem=z_recv.at[j, d],
            device_id={"chan": to}, device_id_type=MESH)

    def x_copy(j, e, d):
        here = alls[j].at[my_tm, block_of(lax.rem(me - e + n_chan, n_chan))]
        return pltpu.make_async_remote_copy(
            src_ref=here, dst_ref=here, send_sem=x_send.at[j, e, d], recv_sem=x_recv.at[j, e, d],
            device_id={"tm": lax.rem(my_tm + d, n_tm)}, device_id_type=MESH)

    near_first = sorted(range(1, n_chan), key=lambda d: (min(d, n_chan - d), d))
    far_first = near_first[::-1]
    for j in range(per):
        for d in far_first:
            w = lax.rem(me + d, n_chan) * per + j
            white_ref[w] = whiten(w)
            z_copy(j, d).start()
        alls[j][my_tm, block_of(me)] = whiten(me * per + j)
        for d in range(1, n_tm):
            x_copy(j, 0, d).start()
        if j == 0:
            for d in range(1, n_chan):
                pick_copy(d).start()
    picks[me] = pick_ref[...]
    turned = jnp.transpose(pick_ref[...].astype(f32))
    for s in range(steps):
        pick_wide[s] = jnp.broadcast_to(turned[:, s : s + 1], (channels, LANES)).astype(jnp.int32)
    for d in range(1, n_chan):
        pick_copy(d).wait_recv()
    for q in range(n_chan):
        turned = jnp.transpose(picks[q].astype(f32))
        for s in range(steps):
            wide = jnp.broadcast_to(turned[:, s : s + 1], (channels, LANES)).astype(jnp.int32)
            chosen[s, q * channels : (q + 1) * channels] = (
                wide[:, :P_SIZE] == lax.broadcasted_iota(jnp.int32, (channels, P_SIZE), 1)
            ).astype(bf16)

    half = WIN // 2

    def gather(j):
        for i in range(spt):
            s = my_tm * spt + i
            at = owner_ref[s] * panels + panel_ref[s]
            for t in range(n_tm):
                value = alls[j][t, at]
                wide = value.astype(f32)
                turn = [pltpu.roll(wide[:, h * half : (h + 1) * half], half // 2, 1) for h in range(2)]
                pan[i, t, :, :WIN] = value
                pan[i, t, :, WIN:] = jnp.concatenate(turn, axis=1).astype(bf16)

    def plain(j, r):
        blocks = pl.ds(r * (ROWS // P_SIZE), ROWS // P_SIZE)
        return [alls[j][t, blocks].reshape(ROWS, WIN).astype(f32) for t in range(n_tm)]

    def products(j, i, here, values):
        pick = chosen[my_tm * spt + i, here]
        p = q = None
        for t in range(n_tm):
            partner = jnp.dot(pick, pan[i, t], preferred_element_type=f32)
            dp, dq = values[t] * partner[:, :WIN], values[t] * partner[:, WIN:]
            p, q = (dp, dq) if t == 0 else (p + dp, q + dq)
        if j > 0:
            p += acc[i, 0, here]
            q += acc[i, 1, here]
        return p, q

    tiles = n_chan * channels // ROWS

    def accumulate(j):
        gather(j)

        def tile(r, carry):
            here = pl.ds(pl.multiple_of(r * ROWS, ROWS), ROWS)
            values = plain(j, r)
            for i in range(spt):
                p, q = products(j, i, here, values)
                acc[i, 0, here] = p
                acc[i, 1, here] = q
            return carry

        lax.fori_loop(0, tiles, tile, 0)

    def forward(j):
        for d in near_first:
            z_copy(j, d).wait_recv()
            for k in range(1, n_tm):
                x_copy(j, d, k).start()

    def arrive(j):
        for e in [0] + near_first:
            for k in range(1, n_tm):
                x_copy(j, e, k).wait_recv()

    last = per - 1
    for j in range(per):
        forward(j)
        if j > 0:
            arrive(j - 1)
            accumulate(j - 1)
    arrive(last)
    gather(last)

    def lagged(i):
        def tile(r, carry):
            here = pl.ds(pl.multiple_of(r * ROWS, ROWS), ROWS)
            p, q = products(last, i, here, plain(last, r))
            both = jnp.dot(p.astype(bf16), lag_ref[:WIN], preferred_element_type=f32)
            both += jnp.dot(q.astype(bf16), lag_ref[WIN:], preferred_element_type=f32)
            own_lag[i, here] = both[:, :LAGS] + both[:, LAGS:]
            return carry

        lax.fori_loop(0, tiles, tile, 0)

    def sub_copy(k, d):
        to = lax.rem(my_sub + d, n_sub)
        return pltpu.make_async_remote_copy(
            src_ref=own_lag.at[to * spd + k], dst_ref=sub_in.at[k, d - 1],
            send_sem=sub_send.at[k, d - 1], recv_sem=sub_recv.at[k, d - 1],
            device_id={"sub": to}, device_id_type=MESH)

    def r_copy(k, d):
        to = lax.rem(me + d, n_chan)
        return pltpu.make_async_remote_copy(
            src_ref=z_out.at[k, to], dst_ref=z_in.at[k, d], send_sem=r_send.at[k, d], recv_sem=r_recv.at[k, d],
            device_id={"chan": to}, device_id_type=MESH)

    def a_copy(k, d):
        here = done.at[now * spd + k]
        return pltpu.make_async_remote_copy(
            src_ref=here, dst_ref=here, send_sem=a_send.at[k, d], recv_sem=a_recv.at[k, d],
            device_id=at_time(d), device_id_type=MESH)

    for d in range(1, n_sub):
        for k in range(spd):
            lagged(lax.rem(my_sub + d, n_sub) * spd + k)
            sub_copy(k, d).start()
    kept = []
    for k in range(spd):
        mine = my_sub * spd + k
        lagged(mine)
        for d in range(1, n_sub):
            sub_copy(k, d).wait_recv()

        def summed(q, mine=mine, k=k):
            here = pl.ds(q * channels, channels)
            total = own_lag[mine, here]
            for d in range(1, n_sub):
                total += sub_in[k, d - 1, here]
            return total

        for d in far_first:
            to = lax.rem(me + d, n_chan)
            z_out[k, to] = summed(to).astype(bf16)
            r_copy(k, d).start()
        kept.append(summed(me))
    receiver = me * channels + lax.broadcasted_iota(jnp.int32, (channels, LAGS), 0)
    for k in range(spd):
        s = now * spd + k
        total = kept[k]
        for d in near_first:
            r_copy(k, d).wait_recv()
            total += z_in[k, d].astype(f32)
        start = owner_ref[s] * channels + panel_ref[s] * P_SIZE
        far = jnp.abs(receiver - (start + pick_wide[s])) > REACH
        total = jnp.where(far, 0.0, total)
        done[s] = total.astype(done.dtype)
        for d in range(1, n_time):
            a_copy(k, d).start()
        out_ref[s] = total
    for k in range(spd):
        for d in range(1, n_time):
            a_copy(k, d).wait_recv()
            s = lax.rem(now - d + n_time, n_time) * spd + k
            out_ref[s] = done[s].astype(f32)

    for k, move in enumerate(moves):
        pl.when(exists(*move))(lambda k=k: copy(k).wait_send())
    for d in range(1, n_chan):
        pick_copy(d).wait_send()
        for j in range(per):
            z_copy(j, d).wait_send()
        for k in range(spd):
            r_copy(k, d).wait_send()
    for d in range(1, n_tm):
        for j in range(per):
            for e in range(n_chan):
                x_copy(j, e, d).wait_send()
    for k in range(spd):
        for d in range(1, n_sub):
            sub_copy(k, d).wait_send()
        for d in range(1, n_time):
            a_copy(k, d).wait_send()


VMEM = pl.BlockSpec(memory_space=pltpu.VMEM)


def relay(raw, fir_taps, spatial_taps, band_edges, source_owner, source_panel, source_pick):
    channels, samples = raw.shape
    margin = (fir_taps.shape[0] - 1) // 2
    side = spatial_taps.shape[0] // 2
    frames = samples // WIN
    steps = source_owner.shape[0]
    times = ("tm", "sub")
    count = lax.axis_size(times)
    n_chan = lax.axis_size("chan")
    n_tm, n_sub = lax.axis_size("tm"), lax.axis_size("sub")
    depth = WIN + 2 * LANES
    first = LANES - margin
    taps = jnp.pad(fir_taps.astype(jnp.float32), (first, depth - first - fir_taps.shape[0]))[None, :]
    total = frames * n_tm * n_sub
    lag_table = lag_tables(1.0 / math.sqrt(total * (WIN // 2)))
    chunks = steps * SPLIT
    flow = pltpu.VMEM((chunks, frames // SPLIT, P_SIZE, WIN), jnp.bfloat16)
    part = channels // n_sub
    dma = pltpu.SemaphoreType.DMA
    any_space = pl.BlockSpec(memory_space=pltpu.HBM)
    bf16, f32 = jnp.bfloat16, jnp.float32
    return pl.pallas_call(
        functools.partial(relay_kernel, frames, channels, side, steps, n_chan, n_tm, n_sub),
        out_shape=jax.ShapeDtypeStruct((steps, channels, LAGS), f32),
        in_specs=[any_space] * 9,
        out_specs=VMEM,
        scratch_shapes=[
            pltpu.SMEM(spatial_taps.shape, f32),
            pltpu.SMEM(band_edges.shape, jnp.int32),
            pltpu.SMEM(source_owner.shape, jnp.int32),
            pltpu.SMEM(source_panel.shape, jnp.int32),
            pltpu.VMEM(taps.shape, f32),
            pltpu.VMEM(source_pick.shape, jnp.int32),
            pltpu.VMEM(raw.shape, bf16),
            pltpu.VMEM((WIN, WIN), bf16),
            pltpu.VMEM((2 * WIN, LAGS), f32),
            pltpu.VMEM((2, channels + 16, WIN), f32),
            pltpu.VMEM((frames, channels, WIN), f32),
            pltpu.VMEM((channels + 16, samples + 2 * LANES), bf16),
            pltpu.VMEM((2, channels, LANES), bf16),
            pltpu.VMEM((2, side, samples), bf16),
            pltpu.VMEM((2, side, samples), bf16),
            pltpu.VMEM((4, side, LANES), bf16),
            pltpu.VMEM((4, side, LANES), bf16),
            dma((8,)), dma((8,)), dma((9,)),
            pltpu.VMEM((frames, channels, WIN), bf16),
            pltpu.VMEM((steps, frames, P_SIZE, WIN), bf16),
            pltpu.VMEM((steps, channels, P_SIZE), bf16),
            pltpu.VMEM((steps, channels, LANES), jnp.int32),
            pltpu.VMEM((frames, channels, WIN), f32),
            pltpu.VMEM((frames, channels, WIN), f32),
            flow, flow, flow, flow,
            pltpu.VMEM((steps, channels, LAGS), f32),
            pltpu.VMEM((steps, n_sub - 1, part, LAGS), f32),
            pltpu.VMEM((steps, n_tm, part, LAGS), f32),
            pltpu.VMEM((steps, channels, LAGS), f32),
            dma((chunks,)), dma((chunks,)), dma((chunks,)), dma((chunks,)),
            dma((steps, n_sub - 1)), dma((steps, n_sub - 1)),
            dma((steps, n_tm - 1)), dma((steps, n_tm - 1)),
            dma((steps, n_sub - 1)), dma((steps, n_sub - 1)),
        ],
        compiler_params=pltpu.CompilerParams(
            vmem_limit_bytes=64 * 2**20, collective_id=0, has_side_effects=True),
        name="correlate",
    )(spatial_taps, band_edges, source_owner, source_panel, taps, source_pick, raw, spectral_table(), lag_table)


def split(raw, fir_taps, spatial_taps, band_edges, source_owner, source_panel, source_pick):
    channels, samples = raw.shape
    margin = (fir_taps.shape[0] - 1) // 2
    side = spatial_taps.shape[0] // 2
    frames = samples // WIN
    steps = source_owner.shape[0]
    n_chan, n_tm, n_sub = lax.axis_size("chan"), lax.axis_size("tm"), lax.axis_size("sub")
    n_time = n_tm * n_sub
    depth = WIN + 2 * LANES
    first = LANES - margin
    taps = jnp.pad(fir_taps.astype(jnp.float32), (first, depth - first - fir_taps.shape[0]))[None, :]
    lag_table = lag_pair(1.0 / math.sqrt(frames * n_time * (WIN // 2)))
    per, spd = frames // n_chan, steps // n_time
    spt = spd * n_sub
    panels, everyone = channels // P_SIZE, n_chan * channels
    dma, any_space = pltpu.SemaphoreType.DMA, pl.BlockSpec(memory_space=pltpu.HBM)
    bf16, f32 = jnp.bfloat16, jnp.float32
    return pl.pallas_call(
        functools.partial(split_kernel, frames, channels, side, steps, n_chan, n_tm, n_sub),
        out_shape=jax.ShapeDtypeStruct((steps, channels, LAGS), f32),
        in_specs=[any_space] * 9,
        out_specs=VMEM,
        scratch_shapes=[
            pltpu.SMEM(spatial_taps.shape, f32),
            pltpu.SMEM(band_edges.shape, jnp.int32),
            pltpu.SMEM(source_owner.shape, jnp.int32),
            pltpu.SMEM(source_panel.shape, jnp.int32),
            pltpu.VMEM(taps.shape, f32),
            pltpu.VMEM(source_pick.shape, jnp.int32),
            pltpu.VMEM(raw.shape, bf16),
            pltpu.VMEM((WIN, WIN), bf16),
            pltpu.VMEM(lag_table.shape, bf16),
            pltpu.VMEM((2, channels + 16, WIN), f32),
            pltpu.VMEM((frames, channels, WIN), f32),
            pltpu.VMEM((2, channels, depth), bf16),
            pltpu.VMEM((16, samples + 2 * LANES), bf16),
            pltpu.VMEM((frames, 16, depth), bf16),
            pltpu.VMEM((frames, 24, WIN), f32),
            pltpu.VMEM((frames, 24, WIN), f32),
            pltpu.VMEM((frames - 2, 16, WIN), bf16),
            pltpu.VMEM((channels, WIN), f32),
            pltpu.VMEM((2, channels, LANES), bf16),
            pltpu.VMEM((2, side, samples), bf16),
            pltpu.VMEM((2, side, samples), bf16),
            pltpu.VMEM((4, side, LANES), bf16),
            pltpu.VMEM((4, side, LANES), bf16),
            pltpu.VMEM((frames, panels, P_SIZE, WIN), bf16),
            pltpu.VMEM((n_chan, *source_pick.shape), jnp.int32),
            pltpu.VMEM((steps, everyone, P_SIZE), bf16),
            pltpu.VMEM((steps, channels, LANES), jnp.int32),
            pltpu.VMEM((spt, n_tm, P_SIZE, 2 * WIN), bf16),
            pltpu.VMEM((spt, 2, everyone, WIN), f32),
            pltpu.VMEM((spt, everyone, LAGS), f32),
            pltpu.VMEM((spd, max(n_sub - 1, 1), everyone, LAGS), f32),
            pltpu.VMEM((spd, n_chan, channels, LAGS), bf16),
            pltpu.VMEM((spd, n_chan, channels, LAGS), bf16),
            pltpu.VMEM((steps, channels, LAGS), f32),
            dma((9,)), dma((8,)), dma((8,)), pltpu.SemaphoreType.REGULAR((2,)),
            dma((n_chan,)), dma((n_chan,)),
            dma((per, n_chan)), dma((per, n_chan)),
            dma((per, n_chan, n_tm)), dma((per, n_chan, n_tm)),
            dma((spd, n_sub)), dma((spd, n_sub)),
            dma((spd, n_chan)), dma((spd, n_chan)),
            dma((spd, n_time)), dma((spd, n_time)),
        ] + [pltpu.VMEM((n_tm, n_chan * panels, P_SIZE, WIN), bf16)] * per,
        compiler_params=pltpu.CompilerParams(
            vmem_limit_bytes=60 * 2**20, collective_id=0, has_side_effects=True),
        name="correlate",
    )(spatial_taps, band_edges, source_owner, source_panel, taps, source_pick, raw, spectral_table(), lag_table)


def shards(*blocks):
    frames, steps = blocks[0].shape[1] // WIN, blocks[4].shape[0]
    even = frames % lax.axis_size("chan") == 0 and steps % lax.axis_size(("tm", "sub")) == 0
    return (split if even else relay)(*blocks)


def solution(mesh):
    placed = (
        P(("grp", "chan"), ("tm", "sub")),
        P(),
        P(),
        P(),
        P("grp"),
        P(),
        P(None, ("grp", "chan")),
    )
    return jax.shard_map(
        shards,
        mesh=mesh,
        in_specs=placed,
        out_specs=P(None, ("grp", "chan"), None),
        check_vma=False,
    )
```

```python
import functools
import math

import jax
import jax.numpy as jnp
import numpy as np
from jax import lax
from jax.experimental import pallas as pl
from jax.experimental.pallas import tpu as pltpu
from jax.sharding import PartitionSpec as P

P_SIZE = 32
WIN = 256
LAGS = 128
REACH = 1000
HIGHEST = lax.Precision.HIGHEST


def column_maps():
    column = np.arange(WIN)
    quarter = WIN // 4
    bins = column // (2 * quarter) * quarter + column % quarter
    parts = column // quarter % 2
    return bins, parts


def spectral_table():
    bins, parts = column_maps()
    angle = 2.0 * np.pi * ((bins[None, :] * np.arange(WIN)[:, None]) % WIN) / WIN
    table = np.where(parts == 0, np.cos(angle), -np.sin(angle)) / math.sqrt(WIN)
    return jnp.asarray(table.astype(np.float32)).astype(jnp.bfloat16)


def bins_of(shape, axis):
    column = lax.broadcasted_iota(jnp.int32, shape, axis)
    quarter = WIN // 4
    return lax.div(column, 2 * quarter) * quarter + lax.rem(column, quarter)


def lag_tables(scale):
    bins, parts = column_maps()
    lag = np.arange(LAGS) - LAGS // 2
    angle = 2.0 * np.pi * ((bins[:, None] * lag[None, :]) % WIN) / WIN
    real = np.cos(angle) * scale
    imag = np.where(parts[:, None] == 0, -np.sin(angle), np.sin(angle)) * scale
    return jnp.asarray(np.concatenate([real, imag]).astype(np.float32))


def taper_row(edges_ref):
    bins = bins_of((1, WIN), 1).astype(jnp.float32)
    e0, e1, e2, e3 = [jnp.full((1, WIN), edges_ref[k]).astype(jnp.float32) for k in range(4)]
    rising = 0.5 - 0.5 * jnp.cos(math.pi * (bins - e0) / (e1 - e0))
    falling = 0.5 - 0.5 * jnp.cos(math.pi * (e3 - bins) / (e3 - e2))
    inner = jnp.where(bins < e3, falling, 0.0)
    inner = jnp.where(bins <= e2, 1.0, inner)
    inner = jnp.where(bins < e1, rising, inner)
    return jnp.where(bins <= e0, 0.0, inner)


LANES = 128
SPLIT = 2
LAG = 2
MESH = pl.DeviceIdType.MESH


def relay_kernel(frames, channels, side, steps, n_chan, n_tm, n_sub, sp_hbm, edges_hbm, owner_hbm, panel_hbm,
           taps_hbm, pick_hbm, raw_hbm, table_hbm, lag_hbm, out_ref,
           sp_ref, edges_ref, owner_ref, panel_ref, taps_ref, pick_ref, raw_ref, table_ref, lag_ref, filt, spec, ext, time_in, chan_out, chan_in, corner_out, corner_in, send_sem,
           recv_sem, load_sem, white_ref, own_ref, chosen, pick_wide, plain, swapped, in_low, in_high, to_high,
           to_low, own_lag, sub_in, tm_in, done, sem_high, sem_low, got_low, got_high, sub_send, sub_recv,
           tm_send, tm_recv, fin_send, fin_recv):
    my_tm = lax.axis_index("tm")
    my_sub = lax.axis_index("sub")
    loads = [
        pltpu.make_async_copy(source, target, load_sem.at[k])
        for k, (source, target) in enumerate([
            (raw_hbm, raw_ref), (taps_hbm, taps_ref), (pick_hbm, pick_ref), (sp_hbm, sp_ref),
            (edges_hbm, edges_ref), (owner_hbm, owner_ref), (panel_hbm, panel_ref),
            (table_hbm, table_ref), (lag_hbm, lag_ref),
        ])
    ]
    for load in loads:
        load.start()
    me = lax.axis_index("chan")
    n_time = n_tm * n_sub
    now = lax.axis_index("tm") * n_sub + lax.axis_index("sub")
    samples = frames * WIN
    depth = taps_ref.shape[1]

    def peer(dc, dt):
        at = lax.rem(now + dt + n_time, n_time)
        return {"chan": lax.rem(me + dc + n_chan, n_chan), "tm": lax.div(at, n_sub), "sub": lax.rem(at, n_sub)}

    moves = [(0, 1), (0, -1), (1, 0), (-1, 0), (1, 1), (1, -1), (-1, 1), (-1, -1)]
    barrier = pltpu.get_barrier_semaphore()
    peers = [peer(dc, dt) for dc, dt in moves]
    peers += [{"tm": lax.rem(my_tm + d, n_tm)} for d in range(1, n_tm)]
    peers += [{"sub": lax.rem(my_sub + d, n_sub)} for d in range(1, n_sub)]
    for to in peers:
        pl.semaphore_signal(barrier, inc=1, device_id=to, device_id_type=MESH)

    loads[0].wait()
    ends = (slice(channels - side, channels), slice(0, side))
    sides = (slice(samples - LANES, samples), slice(0, LANES))
    for k in range(2):
        chan_out[k] = raw_ref[ends[k]]
        for h in range(2):
            corner_out[2 * k + h] = raw_ref[ends[k], sides[h]]

    def exists(dc, dt):
        return (me + dc >= 0) & (me + dc < n_chan) & (now + dt >= 0) & (now + dt < n_time)

    def copy(k):
        dc, dt = moves[k]
        if k < 2:
            src, dst = raw_ref.at[:, sides[k]], time_in.at[k]
        elif k < 4:
            src, dst = chan_out.at[k - 2], chan_in.at[k - 2]
        else:
            src, dst = corner_out.at[k - 4], corner_in.at[k - 4]
        return pltpu.make_async_remote_copy(
            src_ref=src, dst_ref=dst, send_sem=send_sem.at[k], recv_sem=recv_sem.at[k],
            device_id=peer(dc, dt), device_id_type=MESH)

    pl.semaphore_wait(barrier, len(peers))
    for k in (2, 3, 0, 1, 4, 5, 6, 7):
        pl.when(exists(*moves[k]))(lambda k=k: copy(k).start())

    ext[:channels, LANES : LANES + samples] = raw_ref[...]
    for load in loads[1:]:
        load.wait()
    rolled = pltpu.roll(jnp.broadcast_to(taps_ref[...], (WIN, depth)), 0, 1, stride=1, stride_axis=0)
    fir_t = rolled.astype(jnp.bfloat16)
    near = (jnp.abs(bins_of((WIN, WIN), 0) - bins_of((WIN, WIN), 1)) <= 4).astype(jnp.float32)
    row_bins = bins_of((1, WIN), 1)
    count = jnp.minimum(row_bins + 4, WIN // 2 - 1) - jnp.maximum(row_bins - 4, 0) + 1
    turned = jnp.transpose(pick_ref[...].astype(jnp.float32))
    for s in range(steps):
        wide = jnp.broadcast_to(turned[:, s : s + 1], (channels, LANES)).astype(jnp.int32)
        pick_wide[s] = wide
        chosen[s] = (
            wide[:, :P_SIZE] == lax.broadcasted_iota(jnp.int32, (channels, P_SIZE), 1)
        ).astype(jnp.bfloat16)

    @pl.when(me == 0)
    def _():
        in_low[...] = jnp.zeros_like(in_low)

    @pl.when(me == n_chan - 1)
    def _():
        in_high[...] = jnp.zeros_like(in_high)

    for k, (dc, dt) in enumerate(moves):
        there = exists(-dc, -dt)
        pl.when(there)(lambda k=k: copy(k).wait_recv())
        buf, slot = (time_in, k) if k < 2 else (chan_in, k - 2) if k < 4 else (corner_in, k - 4)

        @pl.when(jnp.logical_not(there))
        def _():
            buf[slot] = jnp.zeros(buf.shape[1:], buf.dtype)

    def rows(low, high):
        width = low.shape[1]
        spare = jnp.zeros((16 - 2 * side, width), jnp.float32)
        both = [low.astype(jnp.float32), high.astype(jnp.float32), spare]
        return jnp.concatenate(both, axis=0).astype(jnp.bfloat16)

    high_at = LANES + samples
    ext[:channels, :LANES] = time_in[0]
    ext[:channels, high_at:] = time_in[1]
    ext[channels:, LANES:high_at] = rows(chan_in[0], chan_in[1])
    ext[channels:, :LANES] = rows(corner_in[0], corner_in[2])
    ext[channels:, high_at:] = rows(corner_in[1], corner_in[3])
    power = jnp.zeros((channels, WIN), jnp.float32)
    for w in range(frames):
        block = ext[:, w * WIN : w * WIN + depth]
        got = lax.dot_general(block, fir_t, (((1,), (1,)), ((), ())), preferred_element_type=jnp.float32)
        slot = w % 2
        filt[slot, 8 : 8 + channels] = got[:channels]
        filt[slot, 8 - side : 8] = got[channels : channels + side]
        filt[slot, 8 + channels : 8 + channels + side] = got[channels + side : channels + 2 * side]
        shaped = sp_ref[0] * filt[slot, 8 - side : 8 - side + channels]
        for m in range(1, 2 * side + 1):
            shaped += sp_ref[m] * filt[slot, 8 - side + m : 8 - side + m + channels]
        spectra = jnp.dot(shaped.astype(jnp.bfloat16), table_ref[...], preferred_element_type=jnp.float32)
        spec[w] = spectra
        power += spectra * spectra
    level = jnp.dot(power, near, precision=HIGHEST, preferred_element_type=jnp.float32)
    level = level / (count.astype(jnp.float32) * frames)
    factor = taper_row(edges_ref) / jnp.sqrt(level + 1e-06)
    for w in range(frames):
        white_ref[w] = (spec[w] * factor).astype(jnp.bfloat16)
    half = WIN // 2
    part = channels // n_sub
    group = frames // SPLIT
    chunks = steps * SPLIT

    def up(c):
        return pltpu.make_async_remote_copy(
            src_ref=to_high.at[c], dst_ref=in_low.at[c], send_sem=sem_high.at[c], recv_sem=got_low.at[c],
            device_id={"chan": lax.rem(me + 1, n_chan)}, device_id_type=MESH)

    def down(c):
        return pltpu.make_async_remote_copy(
            src_ref=to_low.at[c], dst_ref=in_high.at[c], send_sem=sem_low.at[c], recv_sem=got_high.at[c],
            device_id={"chan": lax.rem(me + n_chan - 1, n_chan)}, device_id_type=MESH)

    def sub_copy(s, d):
        to = lax.rem(my_sub + d, n_sub)
        return pltpu.make_async_remote_copy(
            src_ref=own_lag.at[s, pl.ds(to * part, part)], dst_ref=sub_in.at[s, d - 1],
            send_sem=sub_send.at[s, d - 1], recv_sem=sub_recv.at[s, d - 1],
            device_id={"sub": to}, device_id_type=MESH)

    def tm_copy(s, d):
        return pltpu.make_async_remote_copy(
            src_ref=tm_in.at[s, my_tm], dst_ref=tm_in.at[s, my_tm],
            send_sem=tm_send.at[s, d - 1], recv_sem=tm_recv.at[s, d - 1],
            device_id={"tm": lax.rem(my_tm + d, n_tm)}, device_id_type=MESH)

    def fin_copy(s, d):
        here = pl.ds(my_sub * part, part)
        return pltpu.make_async_remote_copy(
            src_ref=done.at[s, here], dst_ref=done.at[s, here],
            send_sem=fin_send.at[s, d - 1], recv_sem=fin_recv.at[s, d - 1],
            device_id={"sub": lax.rem(my_sub + d, n_sub)}, device_id_type=MESH)

    def own_panel(s):
        panel = jnp.full((P_SIZE, WIN), panel_ref[s], jnp.int32)
        for w in range(frames):
            value = white_ref[w, :P_SIZE]
            for k in range(1, channels // P_SIZE):
                value = jnp.where(panel == k, white_ref[w, k * P_SIZE : (k + 1) * P_SIZE], value)
            own_ref[s, w] = value

    def stage(c, arrived, leaving):
        s = lax.div(c, SPLIT)
        k = lax.rem(c, SPLIT)
        mine = jnp.full((P_SIZE, WIN), owner_ref[s], jnp.int32) == me
        for w in range(group):
            leaving[c, w] = jnp.where(mine, own_ref[s, k * group + w], arrived[c, w])

    def relay(t):
        c = t - LAG * me

        @pl.when((c >= 0) & (c < chunks))
        def _():
            @pl.when(me > 0)
            def _():
                up(c).wait_recv()

            @pl.when(me < n_chan - 1)
            def _():
                stage(c, in_low, to_high)
                up(c).start()

        e = t - LAG * (n_chan - 1 - me)

        @pl.when((e >= 0) & (e < chunks))
        def _():
            @pl.when(me < n_chan - 1)
            def _():
                down(e).wait_recv()

            @pl.when(me > 0)
            def _():
                stage(e, in_high, to_low)
                down(e).start()

    def compute(s):
        rows = channels // 2
        owner = owner_ref[s]
        where = jnp.full((P_SIZE, WIN), owner, jnp.int32)
        start = owner * channels + panel_ref[s] * P_SIZE
        for r in range(2):
            here = slice(r * rows, (r + 1) * rows)
            acc_p = jnp.zeros((rows, WIN), jnp.float32)
            acc_q = jnp.zeros((rows, WIN), jnp.float32)
            for w in range(frames):
                c = s * SPLIT + w // group
                value = jnp.where(where < me, in_low[c, w % group], in_high[c, w % group])
                value = jnp.where(where == me, own_ref[s, w], value)
                partner = jnp.dot(chosen[s, here], value, preferred_element_type=jnp.float32)
                acc_p += plain[w, here] * partner
                acc_q += swapped[w, here] * partner
            lagged = jnp.dot(acc_p, lag_ref[:WIN], precision=HIGHEST, preferred_element_type=jnp.float32)
            lagged += jnp.dot(acc_q, lag_ref[WIN:], precision=HIGHEST, preferred_element_type=jnp.float32)
            receiver = me * channels + r * rows + lax.broadcasted_iota(jnp.int32, (rows, LAGS), 0)
            far = jnp.abs(receiver - (start + pick_wide[s, here])) > REACH
            own_lag[s, here] = jnp.where(far, 0.0, lagged)
        for d in range(1, n_sub):
            sub_copy(s, d).start()

    def sub_sum(s):
        total = own_lag[s, pl.ds(my_sub * part, part)]
        for d in range(1, n_sub):
            sub_copy(s, d).wait_recv()
            total += sub_in[s, d - 1]
        tm_in[s, my_tm] = total
        for d in range(1, n_tm):
            tm_copy(s, d).start()

    def tm_sum(s):
        for d in range(1, n_tm):
            tm_copy(s, d).wait_recv()
        total = tm_in[s, 0]
        for k in range(1, n_tm):
            total += tm_in[s, k]
        done[s, pl.ds(my_sub * part, part)] = total
        for d in range(1, n_sub):
            fin_copy(s, d).start()

    def finish(s):
        for d in range(1, n_sub):
            fin_copy(s, d).wait_recv()
        out_ref[s] = done[s]

    delay = -(-(n_chan - 1) * LAG // SPLIT)

    def turn(u, carry):
        pl.when(u < steps)(functools.partial(own_panel, u))
        for k in range(SPLIT):
            relay(u * SPLIT + k)

        @pl.when(u == 0)
        def _():
            for w in range(frames):
                value = white_ref[w].astype(jnp.float32)
                plain[w] = value
                for h in range(2):
                    swapped[w, :, h * half : (h + 1) * half] = pltpu.roll(
                        value[:, h * half : (h + 1) * half], half // 2, 1)

        for late, work in enumerate((compute, sub_sum, tm_sum, finish)):
            s = u - delay - late
            pl.when((s >= 0) & (s < steps))(functools.partial(work, s))
        return carry

    lax.fori_loop(0, steps + delay + 3, turn, 0)

    def drain_chunk(c, carry):
        @pl.when(me < n_chan - 1)
        def _():
            up(c).wait_send()

        @pl.when(me > 0)
        def _():
            down(c).wait_send()
        return carry

    lax.fori_loop(0, chunks, drain_chunk, 0)
    for k, move in enumerate(moves):
        pl.when(exists(*move))(lambda k=k: copy(k).wait_send())

    def drain_step(s, carry):
        for d in range(1, n_sub):
            sub_copy(s, d).wait_send()
            fin_copy(s, d).wait_send()
        for d in range(1, n_tm):
            tm_copy(s, d).wait_send()
        return carry

    lax.fori_loop(0, steps, drain_step, 0)


def lag_pair(scale):
    bins, parts = column_maps()
    lag = np.arange(LAGS) - LAGS // 2
    angle = 2.0 * np.pi * ((bins[:, None] * lag[None, :]) % WIN) / WIN
    real = np.cos(angle) * scale
    imag = np.where(parts[:, None] == 0, np.sin(angle), -np.sin(angle)) * scale
    full = np.concatenate([real, imag]).astype(np.float32)
    high = jnp.asarray(full).astype(jnp.bfloat16)
    low = (jnp.asarray(full) - high.astype(jnp.float32)).astype(jnp.bfloat16)
    return jnp.concatenate([high, low], axis=1)


GROUP = 4


def split_kernel(frames, channels, side, steps, n_chan, n_tm, n_sub, sp_hbm, edges_hbm, owner_hbm, panel_hbm,
                 taps_hbm, pick_hbm, raw_hbm, table_hbm, lag_hbm, out_hbm,
                 sp_ref, edges_ref, owner_ref, panel_ref, taps_ref, pick_ref, raw_ref, table_ref, lag_ref,
                 spec, mixed, halo_ext, halo_win, ends_ref, rim_ref, power_ref,
                 time_in, chan_out, chan_in, corner_out, corner_in, white_ref, picks, chosen, pan, acc,
                 own_lag, sub_in, z_out, z_in, done,
                 load_sem, halo_send, halo_recv, far_sem, pick_send, pick_recv, z_send, z_recv, x_send, x_recv,
                 sub_send, sub_recv, r_send, r_recv, a_send, a_recv, out_sem, *white_in):
    f32, bf16 = jnp.float32, jnp.bfloat16
    me, my_tm, my_sub = lax.axis_index("chan"), lax.axis_index("tm"), lax.axis_index("sub")
    n_time = n_tm * n_sub
    now = my_tm * n_sub + my_sub
    samples = frames * WIN
    depth = taps_ref.shape[1]
    panels = channels // P_SIZE
    per = frames // n_chan
    spd = steps // n_time
    spt = spd * n_sub
    mine, theirs = white_in[:per], white_in[per:]
    loads = [
        pltpu.make_async_copy(source, target, load_sem.at[k])
        for k, (source, target) in enumerate([
            (raw_hbm, raw_ref), (taps_hbm, taps_ref), (pick_hbm, pick_ref), (sp_hbm, sp_ref),
            (edges_hbm, edges_ref), (owner_hbm, owner_ref), (panel_hbm, panel_ref),
            (table_hbm, table_ref), (lag_hbm, lag_ref),
        ])
    ]
    for load in loads[1:] + loads[:1]:
        load.start()

    def at_time(dt):
        at = lax.rem(now + dt + n_time, n_time)
        return {"tm": lax.div(at, n_sub), "sub": lax.rem(at, n_sub)}

    def peer(dc, dt):
        return {"chan": lax.rem(me + dc + n_chan, n_chan), **at_time(dt)}

    def exists(dc, dt):
        return (me + dc >= 0) & (me + dc < n_chan) & (now + dt >= 0) & (now + dt < n_time)

    moves = [(0, 1), (0, -1), (1, 0), (-1, 0), (1, 1), (1, -1), (-1, 1), (-1, -1)]
    barrier = pltpu.get_barrier_semaphore()
    for dt in range(1, n_time):
        pl.semaphore_signal(barrier, inc=1, device_id=at_time(dt), device_id_type=MESH)
    for move in moves[2:]:
        @pl.when(exists(*move))
        def _(move=move):
            pl.semaphore_signal(barrier, inc=1, device_id=peer(*move), device_id_type=MESH)

    for load in loads[1:]:
        load.wait()
    rolled = pltpu.roll(jnp.broadcast_to(taps_ref[...], (WIN, depth)), 0, 1, stride=1, stride_axis=0)
    fir_w = jnp.transpose(rolled).astype(bf16)
    parts = [fir_w[LANES : LANES + WIN]] * 2 + [fir_w[:LANES], fir_w[LANES + WIN :]] * 2
    fir_pair = jnp.concatenate(parts, axis=0)
    near = (jnp.abs(bins_of((WIN, WIN), 0) - bins_of((WIN, WIN), 1)) <= 4).astype(f32)
    row_bins = bins_of((1, WIN), 1)
    count = jnp.minimum(row_bins + 4, WIN // 2 - 1) - jnp.maximum(row_bins - 4, 0) + 1
    taper = taper_row(edges_ref)

    def fir(block, first=0, last=depth):
        return jnp.dot(block, fir_w[first:last], preferred_element_type=f32)

    def taps_at(offset):
        total = jnp.zeros(offset.shape, f32)
        for m in range(2 * side + 1):
            total = jnp.where(offset == m - side, sp_ref[m], total)
        return total

    def two(value):
        high = value.astype(bf16)
        return high, (value - high.astype(f32)).astype(bf16)

    def across(matrix, value):
        m_high, m_low = matrix
        v_high, v_low = two(value)
        left = jnp.concatenate([m_high, m_low, m_high], axis=1)
        right = jnp.concatenate([v_high, v_high, v_low], axis=0)
        return jnp.dot(left, right, preferred_element_type=f32)

    def iota(shape, axis):
        return lax.broadcasted_iota(jnp.int32, shape, axis)

    square = (channels, channels)
    spatial = two(taps_at(iota(square, 1) - iota(square, 0)))
    rim = channels - 16
    stacked = jnp.concatenate(spatial, axis=0)
    row, column = iota((16, frames * 16), 0), iota((16, frames * 16), 1)
    row_channel = jnp.where(row < 8, row, row + rim)
    spot = lax.rem(column, 16)
    column_channel = jnp.where(spot < side, spot - side, jnp.where(spot < 2 * side, channels + spot - side, 4 * channels))
    base = taps_at(column_channel - row_channel)
    frame_of = lax.div(column, 16)
    rim_matrix = two(jnp.concatenate([jnp.where(frame_of == w, base, 0.0) for w in range(frames)], axis=0))
    for k in range(2):
        for at in (0, frames + 1):
            mixed[k, at] = jnp.zeros((channels, WIN), bf16)
    loads[0].wait()
    ends = (slice(channels - side, channels), slice(0, side))
    sides = (slice(samples - LANES, samples), slice(0, LANES))
    for k in range(2):
        chan_out[k] = raw_ref[ends[k]]
        for h in range(2):
            corner_out[2 * k + h] = raw_ref[ends[k], sides[h]]

    def copy(k):
        dc, dt = moves[k]
        if k < 2:
            src, dst = raw_ref.at[:, sides[k]], time_in.at[k]
        elif k < 4:
            src, dst = chan_out.at[k - 2], chan_in.at[k - 2]
        else:
            src, dst = corner_out.at[k - 4], corner_in.at[k - 4]
        return pltpu.make_async_remote_copy(
            src_ref=src, dst_ref=dst, send_sem=halo_send.at[k], recv_sem=halo_recv.at[k],
            device_id=peer(dc, dt), device_id_type=MESH)

    greeted = sum(exists(*move).astype(jnp.int32) for move in moves[2:])
    pl.semaphore_wait(barrier, n_time - 1 + greeted)
    for k in (2, 3, 0, 1, 4, 5, 6, 7):
        pl.when(exists(*moves[k]))(lambda k=k: copy(k).start())

    inner = (me > 0) & (me < n_chan - 1)

    def token(way):
        pl.semaphore_signal(far_sem.at[way], inc=1, device_id={"chan": me + 1 - 2 * way}, device_id_type=MESH)

    def relay_tokens(k):
        for way, distance in ((0, me), (1, n_chan - 1 - me)):
            @pl.when(distance >= k + 1)
            def _():
                pl.semaphore_wait(far_sem.at[way], 1)
            pl.when((distance >= k + 1) & inner)(lambda: token(way))

    for way in range(2):
        pl.when(inner)(lambda: token(way))

    def pick_copy(d):
        return pltpu.make_async_remote_copy(
            src_ref=pick_ref, dst_ref=picks.at[me], send_sem=pick_send.at[0], recv_sem=pick_recv.at[0],
            device_id={"chan": lax.rem(me + d, n_chan)}, device_id_type=MESH)

    def pick_all():
        rest = picks.at[pl.ds(0, n_chan - 1)]
        return pltpu.make_async_remote_copy(
            src_ref=rest, dst_ref=rest, send_sem=pick_send.at[0], recv_sem=pick_recv.at[0],
            device_id={"chan": lax.rem(me + 1, n_chan)}, device_id_type=MESH)

    for w in range(frames):
        got = jnp.dot(stacked, raw_ref[:, w * WIN : (w + 1) * WIN], preferred_element_type=f32)
        mixed[0, w + 1], mixed[1, w + 1] = two(got[:channels] + got[channels:])

    def filtered(g):
        sides = []
        for k in range(2):
            sides.append(mixed[k, g + 1 : g + 1 + GROUP])
        for k in range(2):
            sides += [mixed[k, g : g + GROUP, :, WIN - LANES :], mixed[k, g + 2 : g + 2 + GROUP, :, :LANES]]
        windows = jnp.concatenate(sides, axis=2).reshape(GROUP * channels, 2 * depth)
        return jnp.dot(windows, fir_pair, preferred_element_type=f32)

    power = jnp.zeros((channels, WIN), f32)
    ready = filtered(0)
    for g in range(0, frames, GROUP):
        part, ready = ready, filtered(g + GROUP) if g + GROUP < frames else None
        spectra = jnp.dot(part.astype(bf16), table_ref[...], preferred_element_type=f32)
        part, spectra = part.reshape(GROUP, channels, WIN), spectra.reshape(GROUP, channels, WIN)
        for k in range(GROUP):
            w = g + k
            if w in (0, frames - 1):
                ends_ref[min(w, 1)] = part[k]
                continue
            rim_ref[w, :8] = part[k, :8]
            rim_ref[w, 8:] = part[k, channels - 8 :]
            spec[w] = spectra[k]
            power += spectra[k] * spectra[k]
    power_ref[...] = power
    relay_tokens(1)

    for k, (dc, dt) in enumerate(moves):
        there = exists(-dc, -dt)
        pl.when(there)(lambda k=k: copy(k).wait_recv())
        buf, slot = (time_in, k) if k < 2 else (chan_in, k - 2) if k < 4 else (corner_in, k - 4)

        @pl.when(jnp.logical_not(there))
        def _():
            buf[slot] = jnp.zeros(buf.shape[1:], buf.dtype)

    def rows(low, high):
        width = low.shape[1]
        spare = jnp.zeros((16 - 2 * side, width), f32)
        both = [low.astype(f32), high.astype(f32), spare]
        return jnp.concatenate(both, axis=0).astype(bf16)

    halo_ext[:, LANES : LANES + samples] = rows(chan_in[0], chan_in[1])
    halo_ext[:, :LANES] = rows(corner_in[0], corner_in[2])
    halo_ext[:, LANES + samples :] = rows(corner_in[1], corner_in[3])
    for w in range(frames):
        halo_win[w] = halo_ext[:, w * WIN : w * WIN + depth]
    halo = fir(halo_win[...].reshape(frames * 16, depth))
    late = [fir(time_in[k], k * (depth - LANES), k * (depth - LANES) + LANES) for k in range(2)]
    rim_part = across(rim_matrix, halo).reshape(frames, 16, WIN)
    late = [across(spatial, value) for value in late]
    blocks = [rim_ref[1 : frames - 1] + rim_part[1 : frames - 1]]
    blocks[0] = blocks[0].reshape((frames - 2) * 16, WIN)
    for k, w in enumerate((0, frames - 1)):
        whole = ends_ref[k] + late[k]
        blocks += [whole[:8] + rim_part[w, :8], whole[8 : channels - 8], whole[channels - 8 :] + rim_part[w, 8:]]
    shaped = jnp.concatenate(blocks, axis=0).astype(bf16)
    spectra = jnp.dot(shaped, table_ref[...], preferred_element_type=f32)
    rims, whole = spectra[: (frames - 2) * 16].reshape(frames - 2, 16, WIN), spectra[(frames - 2) * 16 :]
    whole = whole.reshape(2, channels, WIN)
    for w in range(1, frames - 1):
        spec[w, :8] = rims[w - 1, :8]
        spec[w, channels - 8 :] = rims[w - 1, 8:]
    for k, w in enumerate((0, frames - 1)):
        spec[w] = whole[k]
    rims = jnp.sum(rims * rims, axis=0)
    inside = power_ref[8 : channels - 8]
    power = jnp.concatenate([rims[:8], inside, rims[8:]], axis=0) + jnp.sum(whole * whole, axis=0)
    for k in range(2, n_chan - 1):
        relay_tokens(k)
    for d in range(1, n_chan):
        pick_copy(d).start()
    level = jnp.dot(power, near, precision=HIGHEST, preferred_element_type=f32)
    level = level / (count.astype(f32) * frames)
    factor = taper / jnp.sqrt(level + 1e-06)

    def whiten(w):
        return (spec[w] * factor).astype(bf16).reshape(panels, P_SIZE, WIN)

    def block_of(q):
        return pl.ds(q * panels, panels)

    def z_copy(j, d):
        to = lax.rem(me + d, n_chan)
        return pltpu.make_async_remote_copy(
            src_ref=white_ref.at[to * per + j], dst_ref=mine[j].at[block_of(me)],
            send_sem=z_send.at[0], recv_sem=z_recv.at[j, d - 1],
            device_id={"chan": to}, device_id_type=MESH)

    def z_sent():
        rest = white_ref.at[pl.ds(0, (n_chan - 1) * per)]
        return pltpu.make_async_remote_copy(
            src_ref=rest, dst_ref=rest, send_sem=z_send.at[0], recv_sem=z_recv.at[0, 0],
            device_id={"chan": lax.rem(me + 1, n_chan)}, device_id_type=MESH)

    def x_copy(j, e, k):
        at = slice(None) if e is None else block_of(lax.rem(me - e + n_chan, n_chan))
        return pltpu.make_async_remote_copy(
            src_ref=mine[j].at[at], dst_ref=theirs[j].at[k - 1, at],
            send_sem=x_send.at[j, k - 1], recv_sem=x_recv.at[j, k - 1],
            device_id={"tm": lax.rem(my_tm + k, n_tm)}, device_id_type=MESH)

    near_first = sorted(range(1, n_chan), key=lambda d: (min(d, n_chan - d), d))
    far_first = near_first[::-1]
    for j in range(per):
        for d in far_first:
            w = lax.rem(me + d, n_chan) * per + j
            white_ref[w] = whiten(w)
            z_copy(j, d).start()
        mine[j][block_of(me)] = whiten(me * per + j)
        for k in range(1, n_tm):
            x_copy(j, 0, k).start()
    picks[me] = pick_ref[...]
    pick_all().wait_recv()
    for i in range(spt):
        for q in range(n_chan):
            pick = jnp.broadcast_to(picks[q, pl.ds(my_tm * spt + i, 1)], (P_SIZE, channels))
            hit = (pick == iota((P_SIZE, channels), 0)).astype(f32)
            chosen[i, q * channels : (q + 1) * channels] = jnp.transpose(hit).astype(bf16)

    half = WIN // 2

    def source(unit):
        j, k = unit
        return mine[j] if k == 0 else theirs[j].at[k - 1]

    def gather(units):
        for i in range(spt):
            s = my_tm * spt + i
            at = owner_ref[s] * panels + panel_ref[s]
            for u, unit in enumerate(units):
                value = source(unit)[at]
                wide = value.astype(f32)
                turn = [pltpu.roll(wide[:, h * half : (h + 1) * half], half // 2, 1) for h in range(2)]
                pan[i, u, :, :WIN] = value
                pan[i, u, :, WIN:] = jnp.concatenate(turn, axis=1).astype(bf16)

    everyone = n_chan * channels

    def receivers(unit):
        return source(unit)[...].reshape(everyone, WIN).astype(f32)

    def products(units, i, values):
        p = q = None
        for u, value in enumerate(values):
            partner = jnp.dot(chosen[i], pan[i, u], preferred_element_type=f32)
            dp, dq = value * partner[:, :WIN], value * partner[:, WIN:]
            p, q = (dp, dq) if u == 0 else (p + dp, q + dq)
        return p, q

    def accumulate(units, first):
        gather(units)
        values = [receivers(unit) for unit in units]

        def step(i, carry):
            p, q = products(units, i, values)
            if not first:
                p += acc[i, 0]
                q += acc[i, 1]
            acc[i, 0] = p
            acc[i, 1] = q
            return carry

        for i in range(spt):
            step(i, 0)

    def forward(j):
        for d in near_first:
            z_copy(j, d).wait_recv()
            for k in range(1, n_tm):
                x_copy(j, d, k).start()

    def arrive(j):
        for k in range(1, n_tm):
            x_copy(j, None, k).wait_recv()

    def others(j):
        return [(j, k) for k in range(1, n_tm)]

    last = per - 1
    for j in range(per):
        forward(j)
        units = [(j, 0)]
        if j > 0:
            arrive(j - 1)
            units += others(j - 1)
        accumulate(units, j == 0)
    arrive(last)
    gather(others(last))

    def lagged(i):
        p, q = products(others(last), i, [receivers(unit) for unit in others(last)])
        p, q = p + acc[i, 0], q + acc[i, 1]
        both = jnp.dot(p.astype(bf16), lag_ref[:WIN], preferred_element_type=f32)
        both += jnp.dot(q.astype(bf16), lag_ref[WIN:], preferred_element_type=f32)
        own_lag[i] = both[:, :LAGS] + both[:, LAGS:]

    def sub_copy(k, d):
        to = lax.rem(my_sub + d, n_sub)
        return pltpu.make_async_remote_copy(
            src_ref=own_lag.at[to * spd + k], dst_ref=sub_in.at[k, d - 1],
            send_sem=sub_send.at[k, d - 1], recv_sem=sub_recv.at[k, d - 1],
            device_id={"sub": to}, device_id_type=MESH)

    def r_copy(k, d):
        to = lax.rem(me + d, n_chan)
        return pltpu.make_async_remote_copy(
            src_ref=z_out.at[k, d - 1], dst_ref=z_in.at[k, d - 1], send_sem=r_send.at[k], recv_sem=r_recv.at[k],
            device_id={"chan": to}, device_id_type=MESH)

    def r_all(k):
        return pltpu.make_async_remote_copy(
            src_ref=z_out.at[k], dst_ref=z_in.at[k], send_sem=r_send.at[k], recv_sem=r_recv.at[k],
            device_id={"chan": lax.rem(me + 1, n_chan)}, device_id_type=MESH)

    def a_copy(k, d):
        here = done.at[now * spd + k]
        return pltpu.make_async_remote_copy(
            src_ref=here, dst_ref=here, send_sem=a_send.at[k], recv_sem=a_recv.at[k],
            device_id=at_time(d), device_id_type=MESH)

    def a_all(k):
        rest = done.at[pl.ds(0, n_time - 1)]
        return pltpu.make_async_remote_copy(
            src_ref=rest, dst_ref=rest, send_sem=a_send.at[k], recv_sem=a_recv.at[k],
            device_id=at_time(1), device_id_type=MESH)

    for d in range(1, n_sub):
        for k in range(spd):
            lagged(lax.rem(my_sub + d, n_sub) * spd + k)
            sub_copy(k, d).start()
    kept = []
    for k in range(spd):
        own = my_sub * spd + k
        lagged(own)
        for d in range(1, n_sub):
            sub_copy(k, d).wait_recv()

        def summed(q, own=own, k=k):
            here = pl.ds(q * channels, channels)
            value = own_lag[own, here]
            for d in range(1, n_sub):
                value += sub_in[k, d - 1, here]
            return value

        for d in far_first:
            to = lax.rem(me + d, n_chan)
            z_out[k, d - 1] = summed(to).astype(bf16)
            r_copy(k, d).start()
        kept.append(summed(me))
    picked = []
    for k in range(spd):
        pick = jnp.broadcast_to(pick_ref[pl.ds(now * spd + k, 1)], (LAGS, channels))
        picked.append(jnp.transpose(pick.astype(f32)).astype(jnp.int32))
    receiver = me * channels + lax.broadcasted_iota(jnp.int32, (channels, LAGS), 0)
    for k in range(spd):
        s = now * spd + k
        value = kept[k]
        r_all(k).wait_recv()
        for d in range(1, n_chan):
            value += z_in[k, d - 1].astype(f32)
        start = owner_ref[s] * channels + panel_ref[s] * P_SIZE
        far = jnp.abs(receiver - (start + picked[k])) > REACH
        done[s] = jnp.where(far, 0.0, value).astype(bf16)
        for d in range(1, n_time):
            a_copy(k, d).start()
    for k in range(spd):
        if n_time > 1:
            a_all(k).wait_recv()
    store = pltpu.make_async_copy(done, out_hbm, out_sem.at[0])
    store.start()
    for k, move in enumerate(moves):
        pl.when(exists(*move))(lambda k=k: copy(k).wait_send())
    pick_all().wait_send()
    z_sent().wait_send()
    for k in range(1, n_tm):
        for j in range(per):
            x_copy(j, None, k).wait_send()
    for k in range(spd):
        for d in range(1, n_sub):
            sub_copy(k, d).wait_send()
        r_all(k).wait_send()
        if n_time > 1:
            a_all(k).wait_send()
    store.wait()


VMEM = pl.BlockSpec(memory_space=pltpu.VMEM)


def relay(raw, fir_taps, spatial_taps, band_edges, source_owner, source_panel, source_pick):
    channels, samples = raw.shape
    margin = (fir_taps.shape[0] - 1) // 2
    side = spatial_taps.shape[0] // 2
    frames = samples // WIN
    steps = source_owner.shape[0]
    times = ("tm", "sub")
    count = lax.axis_size(times)
    n_chan = lax.axis_size("chan")
    n_tm, n_sub = lax.axis_size("tm"), lax.axis_size("sub")
    depth = WIN + 2 * LANES
    first = LANES - margin
    taps = jnp.pad(fir_taps.astype(jnp.float32), (first, depth - first - fir_taps.shape[0]))[None, :]
    total = frames * n_tm * n_sub
    lag_table = lag_tables(1.0 / math.sqrt(total * (WIN // 2)))
    chunks = steps * SPLIT
    flow = pltpu.VMEM((chunks, frames // SPLIT, P_SIZE, WIN), jnp.bfloat16)
    part = channels // n_sub
    dma = pltpu.SemaphoreType.DMA
    any_space = pl.BlockSpec(memory_space=pltpu.HBM)
    bf16, f32 = jnp.bfloat16, jnp.float32
    return pl.pallas_call(
        functools.partial(relay_kernel, frames, channels, side, steps, n_chan, n_tm, n_sub),
        out_shape=jax.ShapeDtypeStruct((steps, channels, LAGS), f32),
        in_specs=[any_space] * 9,
        out_specs=VMEM,
        scratch_shapes=[
            pltpu.SMEM(spatial_taps.shape, f32),
            pltpu.SMEM(band_edges.shape, jnp.int32),
            pltpu.SMEM(source_owner.shape, jnp.int32),
            pltpu.SMEM(source_panel.shape, jnp.int32),
            pltpu.VMEM(taps.shape, f32),
            pltpu.VMEM(source_pick.shape, jnp.int32),
            pltpu.VMEM(raw.shape, bf16),
            pltpu.VMEM((WIN, WIN), bf16),
            pltpu.VMEM((2 * WIN, LAGS), f32),
            pltpu.VMEM((2, channels + 16, WIN), f32),
            pltpu.VMEM((frames, channels, WIN), f32),
            pltpu.VMEM((channels + 16, samples + 2 * LANES), bf16),
            pltpu.VMEM((2, channels, LANES), bf16),
            pltpu.VMEM((2, side, samples), bf16),
            pltpu.VMEM((2, side, samples), bf16),
            pltpu.VMEM((4, side, LANES), bf16),
            pltpu.VMEM((4, side, LANES), bf16),
            dma((8,)), dma((8,)), dma((9,)),
            pltpu.VMEM((frames, channels, WIN), bf16),
            pltpu.VMEM((steps, frames, P_SIZE, WIN), bf16),
            pltpu.VMEM((steps, channels, P_SIZE), bf16),
            pltpu.VMEM((steps, channels, LANES), jnp.int32),
            pltpu.VMEM((frames, channels, WIN), f32),
            pltpu.VMEM((frames, channels, WIN), f32),
            flow, flow, flow, flow,
            pltpu.VMEM((steps, channels, LAGS), f32),
            pltpu.VMEM((steps, n_sub - 1, part, LAGS), f32),
            pltpu.VMEM((steps, n_tm, part, LAGS), f32),
            pltpu.VMEM((steps, channels, LAGS), f32),
            dma((chunks,)), dma((chunks,)), dma((chunks,)), dma((chunks,)),
            dma((steps, n_sub - 1)), dma((steps, n_sub - 1)),
            dma((steps, n_tm - 1)), dma((steps, n_tm - 1)),
            dma((steps, n_sub - 1)), dma((steps, n_sub - 1)),
        ],
        compiler_params=pltpu.CompilerParams(
            vmem_limit_bytes=64 * 2**20, collective_id=0, has_side_effects=True),
        name="correlate",
    )(spatial_taps, band_edges, source_owner, source_panel, taps, source_pick, raw, spectral_table(), lag_table)


def split(raw, fir_taps, spatial_taps, band_edges, source_owner, source_panel, source_pick):
    channels, samples = raw.shape
    margin = (fir_taps.shape[0] - 1) // 2
    side = spatial_taps.shape[0] // 2
    frames = samples // WIN
    steps = source_owner.shape[0]
    n_chan, n_tm, n_sub = lax.axis_size("chan"), lax.axis_size("tm"), lax.axis_size("sub")
    n_time = n_tm * n_sub
    depth = WIN + 2 * LANES
    first = LANES - margin
    taps = jnp.pad(fir_taps.astype(jnp.float32), (first, depth - first - fir_taps.shape[0]))[None, :]
    lag_table = lag_pair(1.0 / math.sqrt(frames * n_time * (WIN // 2)))
    per, spd = frames // n_chan, steps // n_time
    spt = spd * n_sub
    panels, everyone = channels // P_SIZE, n_chan * channels
    dma, any_space = pltpu.SemaphoreType.DMA, pl.BlockSpec(memory_space=pltpu.HBM)
    bf16, f32 = jnp.bfloat16, jnp.float32
    return pl.pallas_call(
        functools.partial(split_kernel, frames, channels, side, steps, n_chan, n_tm, n_sub),
        out_shape=jax.ShapeDtypeStruct((steps, channels, LAGS), bf16),
        in_specs=[any_space] * 9,
        out_specs=any_space,
        scratch_shapes=[
            pltpu.SMEM(spatial_taps.shape, f32),
            pltpu.SMEM(band_edges.shape, jnp.int32),
            pltpu.SMEM(source_owner.shape, jnp.int32),
            pltpu.SMEM(source_panel.shape, jnp.int32),
            pltpu.VMEM(taps.shape, f32),
            pltpu.VMEM(source_pick.shape, jnp.int32),
            pltpu.VMEM(raw.shape, bf16),
            pltpu.VMEM((WIN, WIN), bf16),
            pltpu.VMEM(lag_table.shape, bf16),
            pltpu.VMEM((frames, channels, WIN), f32),
            pltpu.VMEM((2, frames + 2, channels, WIN), bf16),
            pltpu.VMEM((16, samples + 2 * LANES), bf16),
            pltpu.VMEM((frames, 16, depth), bf16),
            pltpu.VMEM((2, channels, WIN), f32),
            pltpu.VMEM((frames, 16, WIN), f32),
            pltpu.VMEM((channels, WIN), f32),
            pltpu.VMEM((2, channels, LANES), bf16),
            pltpu.VMEM((2, side, samples), bf16),
            pltpu.VMEM((2, side, samples), bf16),
            pltpu.VMEM((4, side, LANES), bf16),
            pltpu.VMEM((4, side, LANES), bf16),
            pltpu.VMEM((frames, panels, P_SIZE, WIN), bf16),
            pltpu.VMEM((n_chan, *source_pick.shape), jnp.int32),
            pltpu.VMEM((spt, everyone, P_SIZE), bf16),
            pltpu.VMEM((spt, n_tm, P_SIZE, 2 * WIN), bf16),
            pltpu.VMEM((spt, 2, everyone, WIN), f32),
            pltpu.VMEM((spt, everyone, LAGS), f32),
            pltpu.VMEM((spd, max(n_sub - 1, 1), everyone, LAGS), f32),
            pltpu.VMEM((spd, n_chan - 1, channels, LAGS), bf16),
            pltpu.VMEM((spd, n_chan - 1, channels, LAGS), bf16),
            pltpu.VMEM((steps, channels, LAGS), bf16),
            dma((9,)), dma((8,)), dma((8,)), pltpu.SemaphoreType.REGULAR((2,)),
            dma((1,)), dma((1,)), dma((1,)), dma((per, n_chan - 1)),
            dma((per, max(n_tm - 1, 1))), dma((per, max(n_tm - 1, 1))),
            dma((spd, max(n_sub - 1, 1))), dma((spd, max(n_sub - 1, 1))),
            dma((spd,)), dma((spd,)), dma((spd,)), dma((spd,)), dma((1,)),
        ] + [pltpu.VMEM((n_chan * panels, P_SIZE, WIN), bf16)] * per
        + [pltpu.VMEM((max(n_tm - 1, 1), n_chan * panels, P_SIZE, WIN), bf16)] * per,
        compiler_params=pltpu.CompilerParams(
            vmem_limit_bytes=60 * 2**20, collective_id=0, has_side_effects=True),
        name="correlate",
    )(spatial_taps, band_edges, source_owner, source_panel, taps, source_pick, raw, spectral_table(), lag_table).astype(f32)


def shards(*blocks):
    frames, steps = blocks[0].shape[1] // WIN, blocks[4].shape[0]
    chans = lax.axis_size("chan")
    even = chans > 1 and frames % chans == 0 and frames % GROUP == 0 and steps % lax.axis_size(("tm", "sub")) == 0
    return (split if even else relay)(*blocks)


def solution(mesh):
    placed = (
        P(("grp", "chan"), ("tm", "sub")),
        P(),
        P(),
        P(),
        P("grp"),
        P(),
        P(None, ("grp", "chan")),
    )
    return jax.shard_map(
        shards,
        mesh=mesh,
        in_specs=placed,
        out_specs=P(None, ("grp", "chan"), None),
        check_vma=False,
    )
```

```python
import functools
import math

import jax
import jax.numpy as jnp
import numpy as np
from jax import lax
from jax.experimental import pallas as pl
from jax.experimental.pallas import tpu as pltpu
from jax.sharding import PartitionSpec as P

P_SIZE = 32
WIN = 256
LAGS = 128
REACH = 1000
HIGHEST = lax.Precision.HIGHEST


def column_maps():
    column = np.arange(WIN)
    quarter = WIN // 4
    bins = column // (2 * quarter) * quarter + column % quarter
    parts = column // quarter % 2
    return bins, parts


def spectral_table():
    bins, parts = column_maps()
    angle = 2.0 * np.pi * ((bins[None, :] * np.arange(WIN)[:, None]) % WIN) / WIN
    table = np.where(parts == 0, np.cos(angle), -np.sin(angle)) / math.sqrt(WIN)
    return jnp.asarray(table.astype(np.float32)).astype(jnp.bfloat16)


def bins_of(shape, axis):
    column = lax.broadcasted_iota(jnp.int32, shape, axis)
    quarter = WIN // 4
    return lax.div(column, 2 * quarter) * quarter + lax.rem(column, quarter)


def lag_tables(scale):
    bins, parts = column_maps()
    lag = np.arange(LAGS) - LAGS // 2
    angle = 2.0 * np.pi * ((bins[:, None] * lag[None, :]) % WIN) / WIN
    real = np.cos(angle) * scale
    imag = np.where(parts[:, None] == 0, -np.sin(angle), np.sin(angle)) * scale
    return jnp.asarray(np.concatenate([real, imag]).astype(np.float32))


def taper_row(edges_ref):
    bins = bins_of((1, WIN), 1).astype(jnp.float32)
    e0, e1, e2, e3 = [jnp.full((1, WIN), edges_ref[k]).astype(jnp.float32) for k in range(4)]
    rising = 0.5 - 0.5 * jnp.cos(math.pi * (bins - e0) / (e1 - e0))
    falling = 0.5 - 0.5 * jnp.cos(math.pi * (e3 - bins) / (e3 - e2))
    inner = jnp.where(bins < e3, falling, 0.0)
    inner = jnp.where(bins <= e2, 1.0, inner)
    inner = jnp.where(bins < e1, rising, inner)
    return jnp.where(bins <= e0, 0.0, inner)


LANES = 128
SPLIT = 2
LAG = 2
MESH = pl.DeviceIdType.MESH


def relay_kernel(frames, channels, side, steps, n_chan, n_tm, n_sub, sp_hbm, edges_hbm, owner_hbm, panel_hbm,
           taps_hbm, pick_hbm, raw_hbm, table_hbm, lag_hbm, out_ref,
           sp_ref, edges_ref, owner_ref, panel_ref, taps_ref, pick_ref, raw_ref, table_ref, lag_ref, filt, spec, ext, time_in, chan_out, chan_in, corner_out, corner_in, send_sem,
           recv_sem, load_sem, white_ref, own_ref, chosen, pick_wide, plain, swapped, in_low, in_high, to_high,
           to_low, own_lag, sub_in, tm_in, done, sem_high, sem_low, got_low, got_high, sub_send, sub_recv,
           tm_send, tm_recv, fin_send, fin_recv):
    my_tm = lax.axis_index("tm")
    my_sub = lax.axis_index("sub")
    loads = [
        pltpu.make_async_copy(source, target, load_sem.at[k])
        for k, (source, target) in enumerate([
            (raw_hbm, raw_ref), (taps_hbm, taps_ref), (pick_hbm, pick_ref), (sp_hbm, sp_ref),
            (edges_hbm, edges_ref), (owner_hbm, owner_ref), (panel_hbm, panel_ref),
            (table_hbm, table_ref), (lag_hbm, lag_ref),
        ])
    ]
    for load in loads:
        load.start()
    me = lax.axis_index("chan")
    n_time = n_tm * n_sub
    now = lax.axis_index("tm") * n_sub + lax.axis_index("sub")
    samples = frames * WIN
    depth = taps_ref.shape[1]

    def peer(dc, dt):
        at = lax.rem(now + dt + n_time, n_time)
        return {"chan": lax.rem(me + dc + n_chan, n_chan), "tm": lax.div(at, n_sub), "sub": lax.rem(at, n_sub)}

    moves = [(0, 1), (0, -1), (1, 0), (-1, 0), (1, 1), (1, -1), (-1, 1), (-1, -1)]
    barrier = pltpu.get_barrier_semaphore()
    peers = [peer(dc, dt) for dc, dt in moves]
    peers += [{"tm": lax.rem(my_tm + d, n_tm)} for d in range(1, n_tm)]
    peers += [{"sub": lax.rem(my_sub + d, n_sub)} for d in range(1, n_sub)]
    for to in peers:
        pl.semaphore_signal(barrier, inc=1, device_id=to, device_id_type=MESH)

    loads[0].wait()
    ends = (slice(channels - side, channels), slice(0, side))
    sides = (slice(samples - LANES, samples), slice(0, LANES))
    for k in range(2):
        chan_out[k] = raw_ref[ends[k]]
        for h in range(2):
            corner_out[2 * k + h] = raw_ref[ends[k], sides[h]]

    def exists(dc, dt):
        return (me + dc >= 0) & (me + dc < n_chan) & (now + dt >= 0) & (now + dt < n_time)

    def copy(k):
        dc, dt = moves[k]
        if k < 2:
            src, dst = raw_ref.at[:, sides[k]], time_in.at[k]
        elif k < 4:
            src, dst = chan_out.at[k - 2], chan_in.at[k - 2]
        else:
            src, dst = corner_out.at[k - 4], corner_in.at[k - 4]
        return pltpu.make_async_remote_copy(
            src_ref=src, dst_ref=dst, send_sem=send_sem.at[k], recv_sem=recv_sem.at[k],
            device_id=peer(dc, dt), device_id_type=MESH)

    pl.semaphore_wait(barrier, len(peers))
    for k in (2, 3, 0, 1, 4, 5, 6, 7):
        pl.when(exists(*moves[k]))(lambda k=k: copy(k).start())

    ext[:channels, LANES : LANES + samples] = raw_ref[...]
    for load in loads[1:]:
        load.wait()
    rolled = pltpu.roll(jnp.broadcast_to(taps_ref[...], (WIN, depth)), 0, 1, stride=1, stride_axis=0)
    fir_t = rolled.astype(jnp.bfloat16)
    near = (jnp.abs(bins_of((WIN, WIN), 0) - bins_of((WIN, WIN), 1)) <= 4).astype(jnp.float32)
    row_bins = bins_of((1, WIN), 1)
    count = jnp.minimum(row_bins + 4, WIN // 2 - 1) - jnp.maximum(row_bins - 4, 0) + 1
    turned = jnp.transpose(pick_ref[...].astype(jnp.float32))
    for s in range(steps):
        wide = jnp.broadcast_to(turned[:, s : s + 1], (channels, LANES)).astype(jnp.int32)
        pick_wide[s] = wide
        chosen[s] = (
            wide[:, :P_SIZE] == lax.broadcasted_iota(jnp.int32, (channels, P_SIZE), 1)
        ).astype(jnp.bfloat16)

    @pl.when(me == 0)
    def _():
        in_low[...] = jnp.zeros_like(in_low)

    @pl.when(me == n_chan - 1)
    def _():
        in_high[...] = jnp.zeros_like(in_high)

    for k, (dc, dt) in enumerate(moves):
        there = exists(-dc, -dt)
        pl.when(there)(lambda k=k: copy(k).wait_recv())
        buf, slot = (time_in, k) if k < 2 else (chan_in, k - 2) if k < 4 else (corner_in, k - 4)

        @pl.when(jnp.logical_not(there))
        def _():
            buf[slot] = jnp.zeros(buf.shape[1:], buf.dtype)

    def rows(low, high):
        width = low.shape[1]
        spare = jnp.zeros((16 - 2 * side, width), jnp.float32)
        both = [low.astype(jnp.float32), high.astype(jnp.float32), spare]
        return jnp.concatenate(both, axis=0).astype(jnp.bfloat16)

    high_at = LANES + samples
    ext[:channels, :LANES] = time_in[0]
    ext[:channels, high_at:] = time_in[1]
    ext[channels:, LANES:high_at] = rows(chan_in[0], chan_in[1])
    ext[channels:, :LANES] = rows(corner_in[0], corner_in[2])
    ext[channels:, high_at:] = rows(corner_in[1], corner_in[3])
    power = jnp.zeros((channels, WIN), jnp.float32)
    for w in range(frames):
        block = ext[:, w * WIN : w * WIN + depth]
        got = lax.dot_general(block, fir_t, (((1,), (1,)), ((), ())), preferred_element_type=jnp.float32)
        slot = w % 2
        filt[slot, 8 : 8 + channels] = got[:channels]
        filt[slot, 8 - side : 8] = got[channels : channels + side]
        filt[slot, 8 + channels : 8 + channels + side] = got[channels + side : channels + 2 * side]
        shaped = sp_ref[0] * filt[slot, 8 - side : 8 - side + channels]
        for m in range(1, 2 * side + 1):
            shaped += sp_ref[m] * filt[slot, 8 - side + m : 8 - side + m + channels]
        spectra = jnp.dot(shaped.astype(jnp.bfloat16), table_ref[...], preferred_element_type=jnp.float32)
        spec[w] = spectra
        power += spectra * spectra
    level = jnp.dot(power, near, precision=HIGHEST, preferred_element_type=jnp.float32)
    level = level / (count.astype(jnp.float32) * frames)
    factor = taper_row(edges_ref) / jnp.sqrt(level + 1e-06)
    for w in range(frames):
        white_ref[w] = (spec[w] * factor).astype(jnp.bfloat16)
    half = WIN // 2
    part = channels // n_sub
    group = frames // SPLIT
    chunks = steps * SPLIT

    def up(c):
        return pltpu.make_async_remote_copy(
            src_ref=to_high.at[c], dst_ref=in_low.at[c], send_sem=sem_high.at[c], recv_sem=got_low.at[c],
            device_id={"chan": lax.rem(me + 1, n_chan)}, device_id_type=MESH)

    def down(c):
        return pltpu.make_async_remote_copy(
            src_ref=to_low.at[c], dst_ref=in_high.at[c], send_sem=sem_low.at[c], recv_sem=got_high.at[c],
            device_id={"chan": lax.rem(me + n_chan - 1, n_chan)}, device_id_type=MESH)

    def sub_copy(s, d):
        to = lax.rem(my_sub + d, n_sub)
        return pltpu.make_async_remote_copy(
            src_ref=own_lag.at[s, pl.ds(to * part, part)], dst_ref=sub_in.at[s, d - 1],
            send_sem=sub_send.at[s, d - 1], recv_sem=sub_recv.at[s, d - 1],
            device_id={"sub": to}, device_id_type=MESH)

    def tm_copy(s, d):
        return pltpu.make_async_remote_copy(
            src_ref=tm_in.at[s, my_tm], dst_ref=tm_in.at[s, my_tm],
            send_sem=tm_send.at[s, d - 1], recv_sem=tm_recv.at[s, d - 1],
            device_id={"tm": lax.rem(my_tm + d, n_tm)}, device_id_type=MESH)

    def fin_copy(s, d):
        here = pl.ds(my_sub * part, part)
        return pltpu.make_async_remote_copy(
            src_ref=done.at[s, here], dst_ref=done.at[s, here],
            send_sem=fin_send.at[s, d - 1], recv_sem=fin_recv.at[s, d - 1],
            device_id={"sub": lax.rem(my_sub + d, n_sub)}, device_id_type=MESH)

    def own_panel(s):
        panel = jnp.full((P_SIZE, WIN), panel_ref[s], jnp.int32)
        for w in range(frames):
            value = white_ref[w, :P_SIZE]
            for k in range(1, channels // P_SIZE):
                value = jnp.where(panel == k, white_ref[w, k * P_SIZE : (k + 1) * P_SIZE], value)
            own_ref[s, w] = value

    def stage(c, arrived, leaving):
        s = lax.div(c, SPLIT)
        k = lax.rem(c, SPLIT)
        mine = jnp.full((P_SIZE, WIN), owner_ref[s], jnp.int32) == me
        for w in range(group):
            leaving[c, w] = jnp.where(mine, own_ref[s, k * group + w], arrived[c, w])

    def relay(t):
        c = t - LAG * me

        @pl.when((c >= 0) & (c < chunks))
        def _():
            @pl.when(me > 0)
            def _():
                up(c).wait_recv()

            @pl.when(me < n_chan - 1)
            def _():
                stage(c, in_low, to_high)
                up(c).start()

        e = t - LAG * (n_chan - 1 - me)

        @pl.when((e >= 0) & (e < chunks))
        def _():
            @pl.when(me < n_chan - 1)
            def _():
                down(e).wait_recv()

            @pl.when(me > 0)
            def _():
                stage(e, in_high, to_low)
                down(e).start()

    def compute(s):
        rows = channels // 2
        owner = owner_ref[s]
        where = jnp.full((P_SIZE, WIN), owner, jnp.int32)
        start = owner * channels + panel_ref[s] * P_SIZE
        for r in range(2):
            here = slice(r * rows, (r + 1) * rows)
            acc_p = jnp.zeros((rows, WIN), jnp.float32)
            acc_q = jnp.zeros((rows, WIN), jnp.float32)
            for w in range(frames):
                c = s * SPLIT + w // group
                value = jnp.where(where < me, in_low[c, w % group], in_high[c, w % group])
                value = jnp.where(where == me, own_ref[s, w], value)
                partner = jnp.dot(chosen[s, here], value, preferred_element_type=jnp.float32)
                acc_p += plain[w, here] * partner
                acc_q += swapped[w, here] * partner
            lagged = jnp.dot(acc_p, lag_ref[:WIN], precision=HIGHEST, preferred_element_type=jnp.float32)
            lagged += jnp.dot(acc_q, lag_ref[WIN:], precision=HIGHEST, preferred_element_type=jnp.float32)
            receiver = me * channels + r * rows + lax.broadcasted_iota(jnp.int32, (rows, LAGS), 0)
            far = jnp.abs(receiver - (start + pick_wide[s, here])) > REACH
            own_lag[s, here] = jnp.where(far, 0.0, lagged)
        for d in range(1, n_sub):
            sub_copy(s, d).start()

    def sub_sum(s):
        total = own_lag[s, pl.ds(my_sub * part, part)]
        for d in range(1, n_sub):
            sub_copy(s, d).wait_recv()
            total += sub_in[s, d - 1]
        tm_in[s, my_tm] = total
        for d in range(1, n_tm):
            tm_copy(s, d).start()

    def tm_sum(s):
        for d in range(1, n_tm):
            tm_copy(s, d).wait_recv()
        total = tm_in[s, 0]
        for k in range(1, n_tm):
            total += tm_in[s, k]
        done[s, pl.ds(my_sub * part, part)] = total
        for d in range(1, n_sub):
            fin_copy(s, d).start()

    def finish(s):
        for d in range(1, n_sub):
            fin_copy(s, d).wait_recv()
        out_ref[s] = done[s]

    delay = -(-(n_chan - 1) * LAG // SPLIT)

    def turn(u, carry):
        pl.when(u < steps)(functools.partial(own_panel, u))
        for k in range(SPLIT):
            relay(u * SPLIT + k)

        @pl.when(u == 0)
        def _():
            for w in range(frames):
                value = white_ref[w].astype(jnp.float32)
                plain[w] = value
                for h in range(2):
                    swapped[w, :, h * half : (h + 1) * half] = pltpu.roll(
                        value[:, h * half : (h + 1) * half], half // 2, 1)

        for late, work in enumerate((compute, sub_sum, tm_sum, finish)):
            s = u - delay - late
            pl.when((s >= 0) & (s < steps))(functools.partial(work, s))
        return carry

    lax.fori_loop(0, steps + delay + 3, turn, 0)

    def drain_chunk(c, carry):
        @pl.when(me < n_chan - 1)
        def _():
            up(c).wait_send()

        @pl.when(me > 0)
        def _():
            down(c).wait_send()
        return carry

    lax.fori_loop(0, chunks, drain_chunk, 0)
    for k, move in enumerate(moves):
        pl.when(exists(*move))(lambda k=k: copy(k).wait_send())

    def drain_step(s, carry):
        for d in range(1, n_sub):
            sub_copy(s, d).wait_send()
            fin_copy(s, d).wait_send()
        for d in range(1, n_tm):
            tm_copy(s, d).wait_send()
        return carry

    lax.fori_loop(0, steps, drain_step, 0)


def lag_pair(scale):
    bins, parts = column_maps()
    lag = np.arange(LAGS) - LAGS // 2
    angle = 2.0 * np.pi * ((bins[:, None] * lag[None, :]) % WIN) / WIN
    real = np.cos(angle) * scale
    imag = np.where(parts[:, None] == 0, np.sin(angle), -np.sin(angle)) * scale
    full = np.concatenate([real, imag]).astype(np.float32)
    high = jnp.asarray(full).astype(jnp.bfloat16)
    low = (jnp.asarray(full) - high.astype(jnp.float32)).astype(jnp.bfloat16)
    return jnp.concatenate([high, low], axis=1)


GROUP = 4


def split_kernel(frames, channels, side, steps, n_chan, n_tm, n_sub, sp_hbm, edges_hbm, owner_hbm, panel_hbm,
                 taps_hbm, pick_hbm, raw_hbm, table_hbm, lag_hbm, out_hbm,
                 sp_ref, edges_ref, owner_ref, panel_ref, taps_ref, pick_ref, raw_ref, table_ref, lag_ref,
                 spec, mixed, halo_ext, halo_win, ends_ref, rim_ref, power_ref,
                 time_in, chan_out, chan_in, corner_out, corner_in, white_ref, picks, chosen, pan, acc,
                 own_lag, sub_in, z_out, z_in, done,
                 load_sem, halo_send, halo_recv, far_sem, pick_send, pick_recv, z_send, z_recv, x_send, x_recv,
                 sub_send, sub_recv, r_send, r_recv, a_send, a_recv, out_sem, *white_in):
    f32, bf16 = jnp.float32, jnp.bfloat16
    me, my_tm, my_sub = lax.axis_index("chan"), lax.axis_index("tm"), lax.axis_index("sub")
    n_time = n_tm * n_sub
    now = my_tm * n_sub + my_sub
    samples = frames * WIN
    n_taps = taps_ref.shape[0]
    depth = WIN + 2 * LANES
    panels = channels // P_SIZE
    per = frames // n_chan
    spd = steps // n_time
    spt = spd * n_sub
    mine, theirs = white_in[:per], white_in[per:]
    loads = [
        pltpu.make_async_copy(source, target, load_sem.at[k])
        for k, (source, target) in enumerate([
            (raw_hbm, raw_ref), (taps_hbm, taps_ref), (pick_hbm, pick_ref), (sp_hbm, sp_ref),
            (edges_hbm, edges_ref), (owner_hbm, owner_ref), (panel_hbm, panel_ref),
            (table_hbm, table_ref), (lag_hbm, lag_ref),
        ])
    ]
    for load in loads[1:] + loads[:1]:
        load.start()

    def at_time(dt):
        at = lax.rem(now + dt + n_time, n_time)
        return {"tm": lax.div(at, n_sub), "sub": lax.rem(at, n_sub)}

    def peer(dc, dt):
        return {"chan": lax.rem(me + dc + n_chan, n_chan), **at_time(dt)}

    def exists(dc, dt):
        return (me + dc >= 0) & (me + dc < n_chan) & (now + dt >= 0) & (now + dt < n_time)

    moves = [(0, 1), (0, -1), (1, 0), (-1, 0), (1, 1), (1, -1), (-1, 1), (-1, -1)]
    barrier = pltpu.get_barrier_semaphore()
    for dt in range(1, n_time):
        pl.semaphore_signal(barrier, inc=1, device_id=at_time(dt), device_id_type=MESH)
    for move in moves[2:]:
        @pl.when(exists(*move))
        def _(move=move):
            pl.semaphore_signal(barrier, inc=1, device_id=peer(*move), device_id_type=MESH)

    for load in loads[1:]:
        load.wait()
    taps = taps_ref[...].astype(f32).reshape(1, n_taps)
    taps = jnp.concatenate([taps, jnp.zeros((1, depth - n_taps), f32)], axis=1)
    shift = LANES - (n_taps - 1) // 2
    rolled = pltpu.roll(jnp.broadcast_to(taps, (WIN, depth)), shift, 1, stride=1, stride_axis=0)
    fir_w = jnp.transpose(rolled).astype(bf16)
    parts = [fir_w[LANES : LANES + WIN]] * 2 + [fir_w[:LANES], fir_w[LANES + WIN :]] * 2
    fir_pair = jnp.concatenate(parts, axis=0)
    near = (jnp.abs(bins_of((WIN, WIN), 0) - bins_of((WIN, WIN), 1)) <= 4).astype(f32)
    row_bins = bins_of((1, WIN), 1)
    count = jnp.minimum(row_bins + 4, WIN // 2 - 1) - jnp.maximum(row_bins - 4, 0) + 1
    taper = taper_row(edges_ref)

    def fir(block, first=0, last=depth):
        return jnp.dot(block, fir_w[first:last], preferred_element_type=f32)

    def taps_at(offset):
        total = jnp.zeros(offset.shape, f32)
        for m in range(2 * side + 1):
            total = jnp.where(offset == m - side, sp_ref[m], total)
        return total

    def two(value):
        high = value.astype(bf16)
        return high, (value - high.astype(f32)).astype(bf16)

    def across(matrix, value):
        m_high, m_low = matrix
        v_high, v_low = two(value)
        left = jnp.concatenate([m_high, m_low, m_high], axis=1)
        right = jnp.concatenate([v_high, v_high, v_low], axis=0)
        return jnp.dot(left, right, preferred_element_type=f32)

    def iota(shape, axis):
        return lax.broadcasted_iota(jnp.int32, shape, axis)

    square = (channels, channels)
    spatial = two(taps_at(iota(square, 1) - iota(square, 0)))
    rim = channels - 16
    stacked = jnp.concatenate(spatial, axis=0)
    row, column = iota((16, frames * 16), 0), iota((16, frames * 16), 1)
    row_channel = jnp.where(row < 8, row, row + rim)
    spot = lax.rem(column, 16)
    column_channel = jnp.where(spot < side, spot - side, jnp.where(spot < 2 * side, channels + spot - side, 4 * channels))
    base = taps_at(column_channel - row_channel)
    frame_of = lax.div(column, 16)
    rim_matrix = two(jnp.concatenate([jnp.where(frame_of == w, base, 0.0) for w in range(frames)], axis=0))
    for k in range(2):
        for at in (0, frames + 1):
            mixed[k, at] = jnp.zeros((channels, WIN), bf16)
    loads[0].wait()
    ends = (slice(channels - side, channels), slice(0, side))
    sides = (slice(samples - LANES, samples), slice(0, LANES))
    for k in range(2):
        chan_out[k] = raw_ref[ends[k]]
        for h in range(2):
            corner_out[2 * k + h] = raw_ref[ends[k], sides[h]]

    def copy(k):
        dc, dt = moves[k]
        if k < 2:
            src, dst = raw_ref.at[:, sides[k]], time_in.at[k]
        elif k < 4:
            src, dst = chan_out.at[k - 2], chan_in.at[k - 2]
        else:
            src, dst = corner_out.at[k - 4], corner_in.at[k - 4]
        return pltpu.make_async_remote_copy(
            src_ref=src, dst_ref=dst, send_sem=halo_send.at[k], recv_sem=halo_recv.at[k],
            device_id=peer(dc, dt), device_id_type=MESH)

    greeted = sum(exists(*move).astype(jnp.int32) for move in moves[2:])
    pl.semaphore_wait(barrier, n_time - 1 + greeted)
    for k in (2, 3, 0, 1, 4, 5, 6, 7):
        pl.when(exists(*moves[k]))(lambda k=k: copy(k).start())

    inner = (me > 0) & (me < n_chan - 1)

    def token(way):
        pl.semaphore_signal(far_sem.at[way], inc=1, device_id={"chan": me + 1 - 2 * way}, device_id_type=MESH)

    def relay_tokens(k):
        for way, distance in ((0, me), (1, n_chan - 1 - me)):
            @pl.when(distance >= k + 1)
            def _():
                pl.semaphore_wait(far_sem.at[way], 1)
            pl.when((distance >= k + 1) & inner)(lambda: token(way))

    for way in range(2):
        pl.when(inner)(lambda: token(way))

    def pick_copy(d):
        return pltpu.make_async_remote_copy(
            src_ref=pick_ref, dst_ref=picks.at[me], send_sem=pick_send.at[0], recv_sem=pick_recv.at[0],
            device_id={"chan": lax.rem(me + d, n_chan)}, device_id_type=MESH)

    def pick_all():
        rest = picks.at[pl.ds(0, n_chan - 1)]
        return pltpu.make_async_remote_copy(
            src_ref=rest, dst_ref=rest, send_sem=pick_send.at[0], recv_sem=pick_recv.at[0],
            device_id={"chan": lax.rem(me + 1, n_chan)}, device_id_type=MESH)

    for w in range(frames):
        got = jnp.dot(stacked, raw_ref[:, w * WIN : (w + 1) * WIN], preferred_element_type=f32)
        mixed[0, w + 1], mixed[1, w + 1] = two(got[:channels] + got[channels:])

    def filtered(g):
        sides = []
        for k in range(2):
            sides.append(mixed[k, g + 1 : g + 1 + GROUP])
        for k in range(2):
            sides += [mixed[k, g : g + GROUP, :, WIN - LANES :], mixed[k, g + 2 : g + 2 + GROUP, :, :LANES]]
        windows = jnp.concatenate(sides, axis=2).reshape(GROUP * channels, 2 * depth)
        return jnp.dot(windows, fir_pair, preferred_element_type=f32)

    power = jnp.zeros((channels, WIN), f32)
    ready = filtered(0)
    for g in range(0, frames, GROUP):
        part, ready = ready, filtered(g + GROUP) if g + GROUP < frames else None
        spectra = jnp.dot(part.astype(bf16), table_ref[...], preferred_element_type=f32)
        part, spectra = part.reshape(GROUP, channels, WIN), spectra.reshape(GROUP, channels, WIN)
        for k in range(GROUP):
            w = g + k
            if w in (0, frames - 1):
                ends_ref[min(w, 1)] = part[k]
                continue
            rim_ref[w, :8] = part[k, :8]
            rim_ref[w, 8:] = part[k, channels - 8 :]
            spec[w] = spectra[k]
            power += spectra[k] * spectra[k]
    power_ref[...] = power
    relay_tokens(1)

    for k, (dc, dt) in enumerate(moves):
        there = exists(-dc, -dt)
        pl.when(there)(lambda k=k: copy(k).wait_recv())
        buf, slot = (time_in, k) if k < 2 else (chan_in, k - 2) if k < 4 else (corner_in, k - 4)

        @pl.when(jnp.logical_not(there))
        def _():
            buf[slot] = jnp.zeros(buf.shape[1:], buf.dtype)

    def rows(low, high):
        width = low.shape[1]
        spare = jnp.zeros((16 - 2 * side, width), f32)
        both = [low.astype(f32), high.astype(f32), spare]
        return jnp.concatenate(both, axis=0).astype(bf16)

    halo_ext[:, LANES : LANES + samples] = rows(chan_in[0], chan_in[1])
    halo_ext[:, :LANES] = rows(corner_in[0], corner_in[2])
    halo_ext[:, LANES + samples :] = rows(corner_in[1], corner_in[3])
    for w in range(frames):
        halo_win[w] = halo_ext[:, w * WIN : w * WIN + depth]
    halo = fir(halo_win[...].reshape(frames * 16, depth))
    late = [fir(time_in[k], k * (depth - LANES), k * (depth - LANES) + LANES) for k in range(2)]
    rim_part = across(rim_matrix, halo).reshape(frames, 16, WIN)
    late = [across(spatial, value) for value in late]
    blocks = [rim_ref[1 : frames - 1] + rim_part[1 : frames - 1]]
    blocks[0] = blocks[0].reshape((frames - 2) * 16, WIN)
    for k, w in enumerate((0, frames - 1)):
        whole = ends_ref[k] + late[k]
        blocks += [whole[:8] + rim_part[w, :8], whole[8 : channels - 8], whole[channels - 8 :] + rim_part[w, 8:]]
    shaped = jnp.concatenate(blocks, axis=0).astype(bf16)
    spectra = jnp.dot(shaped, table_ref[...], preferred_element_type=f32)
    rims, whole = spectra[: (frames - 2) * 16].reshape(frames - 2, 16, WIN), spectra[(frames - 2) * 16 :]
    whole = whole.reshape(2, channels, WIN)
    for w in range(1, frames - 1):
        spec[w, :8] = rims[w - 1, :8]
        spec[w, channels - 8 :] = rims[w - 1, 8:]
    for k, w in enumerate((0, frames - 1)):
        spec[w] = whole[k]
    rims = jnp.sum(rims * rims, axis=0)
    inside = power_ref[8 : channels - 8]
    power = jnp.concatenate([rims[:8], inside, rims[8:]], axis=0) + jnp.sum(whole * whole, axis=0)
    for k in range(2, n_chan - 1):
        relay_tokens(k)
    for d in range(1, n_chan):
        pick_copy(d).start()
    level = jnp.dot(power, near, precision=HIGHEST, preferred_element_type=f32)
    level = level / (count.astype(f32) * frames)
    factor = taper / jnp.sqrt(level + 1e-06)

    def whiten(w):
        return (spec[w] * factor).astype(bf16).reshape(panels, P_SIZE, WIN)

    def block_of(q):
        return pl.ds(q * panels, panels)

    def z_copy(j, d):
        to = lax.rem(me + d, n_chan)
        return pltpu.make_async_remote_copy(
            src_ref=white_ref.at[to * per + j], dst_ref=mine[j].at[block_of(me)],
            send_sem=z_send.at[d - 1], recv_sem=z_recv.at[j, d - 1],
            device_id={"chan": to}, device_id_type=MESH)

    def x_copy(j, e, k):
        at = slice(None) if e is None else block_of(lax.rem(me - e + n_chan, n_chan))
        return pltpu.make_async_remote_copy(
            src_ref=mine[j].at[at], dst_ref=theirs[j].at[k - 1, at],
            send_sem=x_send.at[j, k - 1], recv_sem=x_recv.at[j, k - 1],
            device_id={"tm": lax.rem(my_tm + k, n_tm)}, device_id_type=MESH)

    near_first = sorted(range(1, n_chan), key=lambda d: (min(d, n_chan - d), d))
    far_first = near_first[::-1]
    for j in range(per):
        for d in far_first:
            w = lax.rem(me + d, n_chan) * per + j
            white_ref[w] = whiten(w)
            if j == 0:
                z_copy(j, d).start()
        mine[j][block_of(me)] = whiten(me * per + j)
        for k in range(1, n_tm):
            x_copy(j, 0, k).start()
    picks[me] = pick_ref[...]
    pick_all().wait_recv()
    for i in range(spt):
        for q in range(n_chan):
            pick = jnp.broadcast_to(picks[q, pl.ds(my_tm * spt + i, 1)], (P_SIZE, channels))
            hit = (pick == iota((P_SIZE, channels), 0)).astype(f32)
            chosen[i, q * channels : (q + 1) * channels] = jnp.transpose(hit).astype(bf16)

    half = WIN // 2

    def source(unit):
        j, k = unit
        return mine[j] if k == 0 else theirs[j].at[k - 1]

    def gather(units):
        for i in range(spt):
            s = my_tm * spt + i
            at = owner_ref[s] * panels + panel_ref[s]
            for u, unit in enumerate(units):
                value = source(unit)[at]
                wide = value.astype(f32)
                turn = [pltpu.roll(wide[:, h * half : (h + 1) * half], half // 2, 1) for h in range(2)]
                pan[i, u, :, :WIN] = value
                pan[i, u, :, WIN:] = jnp.concatenate(turn, axis=1).astype(bf16)

    everyone = n_chan * channels

    def receivers(unit):
        return source(unit)[...].reshape(everyone, WIN).astype(f32)

    def products(units, i, values):
        p = q = None
        for u, value in enumerate(values):
            partner = jnp.dot(chosen[i], pan[i, u], preferred_element_type=f32)
            dp, dq = value * partner[:, :WIN], value * partner[:, WIN:]
            p, q = (dp, dq) if u == 0 else (p + dp, q + dq)
        return p, q

    def accumulate(units, first):
        gather(units)
        values = [receivers(unit) for unit in units]

        def step(i, carry):
            p, q = products(units, i, values)
            if not first:
                p += acc[i, 0]
                q += acc[i, 1]
            acc[i, 0] = p
            acc[i, 1] = q
            return carry

        for i in range(spt):
            step(i, 0)

    def forward(j):
        for d in near_first:
            z_copy(j, d).wait_send()
            if j + 1 < per:
                z_copy(j + 1, d).start()
        for d in near_first:
            z_copy(j, d).wait_recv()
            for k in range(1, n_tm):
                x_copy(j, d, k).start()

    def arrive(j):
        for k in range(1, n_tm):
            x_copy(j, None, k).wait_recv()

    def others(j):
        return [(j, k) for k in range(1, n_tm)]

    last = per - 1
    for j in range(per):
        forward(j)
        units = [(j, 0)]
        if j > 0:
            arrive(j - 1)
            units += others(j - 1)
        accumulate(units, j == 0)
    arrive(last)
    gather(others(last))

    def lagged(i):
        p, q = products(others(last), i, [receivers(unit) for unit in others(last)])
        p, q = p + acc[i, 0], q + acc[i, 1]
        both = jnp.dot(p.astype(bf16), lag_ref[:WIN], preferred_element_type=f32)
        both += jnp.dot(q.astype(bf16), lag_ref[WIN:], preferred_element_type=f32)
        own_lag[i] = both[:, :LAGS] + both[:, LAGS:]

    def sub_copy(k, d):
        to = lax.rem(my_sub + d, n_sub)
        return pltpu.make_async_remote_copy(
            src_ref=own_lag.at[to * spd + k], dst_ref=sub_in.at[k, d - 1],
            send_sem=sub_send.at[k, d - 1], recv_sem=sub_recv.at[k, d - 1],
            device_id={"sub": to}, device_id_type=MESH)

    def r_copy(k, d):
        to = lax.rem(me + d, n_chan)
        return pltpu.make_async_remote_copy(
            src_ref=z_out.at[k, d - 1], dst_ref=z_in.at[k, d - 1], send_sem=r_send.at[k], recv_sem=r_recv.at[k],
            device_id={"chan": to}, device_id_type=MESH)

    def r_all(k):
        return pltpu.make_async_remote_copy(
            src_ref=z_out.at[k], dst_ref=z_in.at[k], send_sem=r_send.at[k], recv_sem=r_recv.at[k],
            device_id={"chan": lax.rem(me + 1, n_chan)}, device_id_type=MESH)

    def a_copy(k, d):
        here = done.at[now * spd + k]
        return pltpu.make_async_remote_copy(
            src_ref=here, dst_ref=here, send_sem=a_send.at[k], recv_sem=a_recv.at[k],
            device_id=at_time(d), device_id_type=MESH)

    def a_all(k):
        rest = done.at[pl.ds(0, n_time - 1)]
        return pltpu.make_async_remote_copy(
            src_ref=rest, dst_ref=rest, send_sem=a_send.at[k], recv_sem=a_recv.at[k],
            device_id=at_time(1), device_id_type=MESH)

    for d in range(1, n_sub):
        for k in range(spd):
            lagged(lax.rem(my_sub + d, n_sub) * spd + k)
            sub_copy(k, d).start()
    kept = []
    for k in range(spd):
        own = my_sub * spd + k
        lagged(own)
        for d in range(1, n_sub):
            sub_copy(k, d).wait_recv()

        def summed(q, own=own, k=k):
            here = pl.ds(q * channels, channels)
            value = own_lag[own, here]
            for d in range(1, n_sub):
                value += sub_in[k, d - 1, here]
            return value

        for d in far_first:
            to = lax.rem(me + d, n_chan)
            z_out[k, d - 1] = summed(to).astype(bf16)
            r_copy(k, d).start()
        kept.append(summed(me))
    picked = []
    for k in range(spd):
        pick = jnp.broadcast_to(pick_ref[pl.ds(now * spd + k, 1)], (LAGS, channels))
        picked.append(jnp.transpose(pick.astype(f32)).astype(jnp.int32))
    receiver = me * channels + lax.broadcasted_iota(jnp.int32, (channels, LAGS), 0)
    for k in range(spd):
        s = now * spd + k
        value = kept[k]
        r_all(k).wait_recv()
        for d in range(1, n_chan):
            value += z_in[k, d - 1].astype(f32)
        start = owner_ref[s] * channels + panel_ref[s] * P_SIZE
        far = jnp.abs(receiver - (start + picked[k])) > REACH
        done[s] = jnp.where(far, 0.0, value).astype(bf16)
        for d in range(1, n_time):
            a_copy(k, d).start()
    for k in range(spd):
        if n_time > 1:
            a_all(k).wait_recv()
    store = pltpu.make_async_copy(done, out_hbm, out_sem.at[0])
    store.start()
    for k, move in enumerate(moves):
        pl.when(exists(*move))(lambda k=k: copy(k).wait_send())
    pick_all().wait_send()
    for k in range(1, n_tm):
        for j in range(per):
            x_copy(j, None, k).wait_send()
    for k in range(spd):
        for d in range(1, n_sub):
            sub_copy(k, d).wait_send()
        r_all(k).wait_send()
        if n_time > 1:
            a_all(k).wait_send()
    store.wait()


VMEM = pl.BlockSpec(memory_space=pltpu.VMEM)


def relay(raw, fir_taps, spatial_taps, band_edges, source_owner, source_panel, source_pick):
    channels, samples = raw.shape
    margin = (fir_taps.shape[0] - 1) // 2
    side = spatial_taps.shape[0] // 2
    frames = samples // WIN
    steps = source_owner.shape[0]
    times = ("tm", "sub")
    count = lax.axis_size(times)
    n_chan = lax.axis_size("chan")
    n_tm, n_sub = lax.axis_size("tm"), lax.axis_size("sub")
    depth = WIN + 2 * LANES
    first = LANES - margin
    taps = jnp.pad(fir_taps.astype(jnp.float32), (first, depth - first - fir_taps.shape[0]))[None, :]
    total = frames * n_tm * n_sub
    lag_table = lag_tables(1.0 / math.sqrt(total * (WIN // 2)))
    chunks = steps * SPLIT
    flow = pltpu.VMEM((chunks, frames // SPLIT, P_SIZE, WIN), jnp.bfloat16)
    part = channels // n_sub
    dma = pltpu.SemaphoreType.DMA
    any_space = pl.BlockSpec(memory_space=pltpu.HBM)
    bf16, f32 = jnp.bfloat16, jnp.float32
    return pl.pallas_call(
        functools.partial(relay_kernel, frames, channels, side, steps, n_chan, n_tm, n_sub),
        out_shape=jax.ShapeDtypeStruct((steps, channels, LAGS), f32),
        in_specs=[any_space] * 9,
        out_specs=VMEM,
        scratch_shapes=[
            pltpu.SMEM(spatial_taps.shape, f32),
            pltpu.SMEM(band_edges.shape, jnp.int32),
            pltpu.SMEM(source_owner.shape, jnp.int32),
            pltpu.SMEM(source_panel.shape, jnp.int32),
            pltpu.VMEM(taps.shape, f32),
            pltpu.VMEM(source_pick.shape, jnp.int32),
            pltpu.VMEM(raw.shape, bf16),
            pltpu.VMEM((WIN, WIN), bf16),
            pltpu.VMEM((2 * WIN, LAGS), f32),
            pltpu.VMEM((2, channels + 16, WIN), f32),
            pltpu.VMEM((frames, channels, WIN), f32),
            pltpu.VMEM((channels + 16, samples + 2 * LANES), bf16),
            pltpu.VMEM((2, channels, LANES), bf16),
            pltpu.VMEM((2, side, samples), bf16),
            pltpu.VMEM((2, side, samples), bf16),
            pltpu.VMEM((4, side, LANES), bf16),
            pltpu.VMEM((4, side, LANES), bf16),
            dma((8,)), dma((8,)), dma((9,)),
            pltpu.VMEM((frames, channels, WIN), bf16),
            pltpu.VMEM((steps, frames, P_SIZE, WIN), bf16),
            pltpu.VMEM((steps, channels, P_SIZE), bf16),
            pltpu.VMEM((steps, channels, LANES), jnp.int32),
            pltpu.VMEM((frames, channels, WIN), f32),
            pltpu.VMEM((frames, channels, WIN), f32),
            flow, flow, flow, flow,
            pltpu.VMEM((steps, channels, LAGS), f32),
            pltpu.VMEM((steps, n_sub - 1, part, LAGS), f32),
            pltpu.VMEM((steps, n_tm, part, LAGS), f32),
            pltpu.VMEM((steps, channels, LAGS), f32),
            dma((chunks,)), dma((chunks,)), dma((chunks,)), dma((chunks,)),
            dma((steps, n_sub - 1)), dma((steps, n_sub - 1)),
            dma((steps, n_tm - 1)), dma((steps, n_tm - 1)),
            dma((steps, n_sub - 1)), dma((steps, n_sub - 1)),
        ],
        compiler_params=pltpu.CompilerParams(
            vmem_limit_bytes=64 * 2**20, collective_id=0, has_side_effects=True),
        name="correlate",
    )(spatial_taps, band_edges, source_owner, source_panel, taps, source_pick, raw, spectral_table(), lag_table)


def split(raw, fir_taps, spatial_taps, band_edges, source_owner, source_panel, source_pick):
    channels, samples = raw.shape
    side = spatial_taps.shape[0] // 2
    frames = samples // WIN
    steps = source_owner.shape[0]
    n_chan, n_tm, n_sub = lax.axis_size("chan"), lax.axis_size("tm"), lax.axis_size("sub")
    n_time = n_tm * n_sub
    depth = WIN + 2 * LANES
    lag_table = lag_pair(1.0 / math.sqrt(frames * n_time * (WIN // 2)))
    per, spd = frames // n_chan, steps // n_time
    spt = spd * n_sub
    panels, everyone = channels // P_SIZE, n_chan * channels
    dma, any_space = pltpu.SemaphoreType.DMA, pl.BlockSpec(memory_space=pltpu.HBM)
    bf16, f32 = jnp.bfloat16, jnp.float32
    return pl.pallas_call(
        functools.partial(split_kernel, frames, channels, side, steps, n_chan, n_tm, n_sub),
        out_shape=jax.ShapeDtypeStruct((steps, channels, LAGS), bf16),
        in_specs=[any_space] * 9,
        out_specs=any_space,
        scratch_shapes=[
            pltpu.SMEM(spatial_taps.shape, f32),
            pltpu.SMEM(band_edges.shape, jnp.int32),
            pltpu.SMEM(source_owner.shape, jnp.int32),
            pltpu.SMEM(source_panel.shape, jnp.int32),
            pltpu.VMEM(fir_taps.shape, bf16),
            pltpu.VMEM(source_pick.shape, jnp.int32),
            pltpu.VMEM(raw.shape, bf16),
            pltpu.VMEM((WIN, WIN), bf16),
            pltpu.VMEM(lag_table.shape, bf16),
            pltpu.VMEM((frames, channels, WIN), f32),
            pltpu.VMEM((2, frames + 2, channels, WIN), bf16),
            pltpu.VMEM((16, samples + 2 * LANES), bf16),
            pltpu.VMEM((frames, 16, depth), bf16),
            pltpu.VMEM((2, channels, WIN), f32),
            pltpu.VMEM((frames, 16, WIN), f32),
            pltpu.VMEM((channels, WIN), f32),
            pltpu.VMEM((2, channels, LANES), bf16),
            pltpu.VMEM((2, side, samples), bf16),
            pltpu.VMEM((2, side, samples), bf16),
            pltpu.VMEM((4, side, LANES), bf16),
            pltpu.VMEM((4, side, LANES), bf16),
            pltpu.VMEM((frames, panels, P_SIZE, WIN), bf16),
            pltpu.VMEM((n_chan, *source_pick.shape), jnp.int32),
            pltpu.VMEM((spt, everyone, P_SIZE), bf16),
            pltpu.VMEM((spt, n_tm, P_SIZE, 2 * WIN), bf16),
            pltpu.VMEM((spt, 2, everyone, WIN), f32),
            pltpu.VMEM((spt, everyone, LAGS), f32),
            pltpu.VMEM((spd, max(n_sub - 1, 1), everyone, LAGS), f32),
            pltpu.VMEM((spd, n_chan - 1, channels, LAGS), bf16),
            pltpu.VMEM((spd, n_chan - 1, channels, LAGS), bf16),
            pltpu.VMEM((steps, channels, LAGS), bf16),
            dma((9,)), dma((8,)), dma((8,)), pltpu.SemaphoreType.REGULAR((2,)),
            dma((1,)), dma((1,)), dma((n_chan - 1,)), dma((per, n_chan - 1)),
            dma((per, max(n_tm - 1, 1))), dma((per, max(n_tm - 1, 1))),
            dma((spd, max(n_sub - 1, 1))), dma((spd, max(n_sub - 1, 1))),
            dma((spd,)), dma((spd,)), dma((spd,)), dma((spd,)), dma((1,)),
        ] + [pltpu.VMEM((n_chan * panels, P_SIZE, WIN), bf16)] * per
        + [pltpu.VMEM((max(n_tm - 1, 1), n_chan * panels, P_SIZE, WIN), bf16)] * per,
        compiler_params=pltpu.CompilerParams(
            vmem_limit_bytes=60 * 2**20, collective_id=0, has_side_effects=True),
        name="correlate",
    )(spatial_taps, band_edges, source_owner, source_panel, fir_taps, source_pick, raw, spectral_table(), lag_table).astype(f32)


def shards(*blocks):
    frames, steps = blocks[0].shape[1] // WIN, blocks[4].shape[0]
    chans = lax.axis_size("chan")
    even = chans > 1 and frames % chans == 0 and frames % GROUP == 0 and steps % lax.axis_size(("tm", "sub")) == 0
    return (split if even else relay)(*blocks)


def solution(mesh):
    placed = (
        P(("grp", "chan"), ("tm", "sub")),
        P(),
        P(),
        P(),
        P("grp"),
        P(),
        P(None, ("grp", "chan")),
    )
    return jax.shard_map(
        shards,
        mesh=mesh,
        in_specs=placed,
        out_specs=P(None, ("grp", "chan"), None),
        check_vma=False,
    )
```

```python
import functools
import math

import jax
import jax.numpy as jnp
import numpy as np
from jax import lax
from jax.experimental import pallas as pl
from jax.experimental.pallas import tpu as pltpu
from jax.sharding import PartitionSpec as P

P_SIZE = 32
WIN = 256
LAGS = 128
REACH = 1000
HIGHEST = lax.Precision.HIGHEST


def column_maps():
    column = np.arange(WIN)
    quarter = WIN // 4
    bins = column // (2 * quarter) * quarter + column % quarter
    parts = column // quarter % 2
    return bins, parts


def spectral_table():
    bins, parts = column_maps()
    angle = 2.0 * np.pi * ((bins[None, :] * np.arange(WIN)[:, None]) % WIN) / WIN
    table = np.where(parts == 0, np.cos(angle), -np.sin(angle)) / math.sqrt(WIN)
    return jnp.asarray(table.astype(np.float32)).astype(jnp.bfloat16)


def bins_of(shape, axis):
    column = lax.broadcasted_iota(jnp.int32, shape, axis)
    quarter = WIN // 4
    return lax.div(column, 2 * quarter) * quarter + lax.rem(column, quarter)


def lag_tables(scale):
    bins, parts = column_maps()
    lag = np.arange(LAGS) - LAGS // 2
    angle = 2.0 * np.pi * ((bins[:, None] * lag[None, :]) % WIN) / WIN
    real = np.cos(angle) * scale
    imag = np.where(parts[:, None] == 0, -np.sin(angle), np.sin(angle)) * scale
    return jnp.asarray(np.concatenate([real, imag]).astype(np.float32))


def taper_row(edges_ref):
    bins = bins_of((1, WIN), 1).astype(jnp.float32)
    e0, e1, e2, e3 = [jnp.full((1, WIN), edges_ref[k]).astype(jnp.float32) for k in range(4)]
    rising = 0.5 - 0.5 * jnp.cos(math.pi * (bins - e0) / (e1 - e0))
    falling = 0.5 - 0.5 * jnp.cos(math.pi * (e3 - bins) / (e3 - e2))
    inner = jnp.where(bins < e3, falling, 0.0)
    inner = jnp.where(bins <= e2, 1.0, inner)
    inner = jnp.where(bins < e1, rising, inner)
    return jnp.where(bins <= e0, 0.0, inner)


LANES = 128
SPLIT = 2
LAG = 2
MESH = pl.DeviceIdType.MESH


def relay_kernel(frames, channels, side, steps, n_chan, n_tm, n_sub, sp_hbm, edges_hbm, owner_hbm, panel_hbm,
           taps_hbm, pick_hbm, raw_hbm, table_hbm, lag_hbm, out_ref,
           sp_ref, edges_ref, owner_ref, panel_ref, taps_ref, pick_ref, raw_ref, table_ref, lag_ref, filt, spec, ext, time_in, chan_out, chan_in, corner_out, corner_in, send_sem,
           recv_sem, load_sem, white_ref, own_ref, chosen, pick_wide, plain, swapped, in_low, in_high, to_high,
           to_low, own_lag, sub_in, tm_in, done, sem_high, sem_low, got_low, got_high, sub_send, sub_recv,
           tm_send, tm_recv, fin_send, fin_recv):
    my_tm = lax.axis_index("tm")
    my_sub = lax.axis_index("sub")
    loads = [
        pltpu.make_async_copy(source, target, load_sem.at[k])
        for k, (source, target) in enumerate([
            (raw_hbm, raw_ref), (taps_hbm, taps_ref), (pick_hbm, pick_ref), (sp_hbm, sp_ref),
            (edges_hbm, edges_ref), (owner_hbm, owner_ref), (panel_hbm, panel_ref),
            (table_hbm, table_ref), (lag_hbm, lag_ref),
        ])
    ]
    for load in loads:
        load.start()
    me = lax.axis_index("chan")
    n_time = n_tm * n_sub
    now = lax.axis_index("tm") * n_sub + lax.axis_index("sub")
    samples = frames * WIN
    depth = taps_ref.shape[1]

    def peer(dc, dt):
        at = lax.rem(now + dt + n_time, n_time)
        return {"chan": lax.rem(me + dc + n_chan, n_chan), "tm": lax.div(at, n_sub), "sub": lax.rem(at, n_sub)}

    moves = [(0, 1), (0, -1), (1, 0), (-1, 0), (1, 1), (1, -1), (-1, 1), (-1, -1)]
    barrier = pltpu.get_barrier_semaphore()
    peers = [peer(dc, dt) for dc, dt in moves]
    peers += [{"tm": lax.rem(my_tm + d, n_tm)} for d in range(1, n_tm)]
    peers += [{"sub": lax.rem(my_sub + d, n_sub)} for d in range(1, n_sub)]
    for to in peers:
        pl.semaphore_signal(barrier, inc=1, device_id=to, device_id_type=MESH)

    loads[0].wait()
    ends = (slice(channels - side, channels), slice(0, side))
    sides = (slice(samples - LANES, samples), slice(0, LANES))
    for k in range(2):
        chan_out[k] = raw_ref[ends[k]]
        for h in range(2):
            corner_out[2 * k + h] = raw_ref[ends[k], sides[h]]

    def exists(dc, dt):
        return (me + dc >= 0) & (me + dc < n_chan) & (now + dt >= 0) & (now + dt < n_time)

    def copy(k):
        dc, dt = moves[k]
        if k < 2:
            src, dst = raw_ref.at[:, sides[k]], time_in.at[k]
        elif k < 4:
            src, dst = chan_out.at[k - 2], chan_in.at[k - 2]
        else:
            src, dst = corner_out.at[k - 4], corner_in.at[k - 4]
        return pltpu.make_async_remote_copy(
            src_ref=src, dst_ref=dst, send_sem=send_sem.at[k], recv_sem=recv_sem.at[k],
            device_id=peer(dc, dt), device_id_type=MESH)

    pl.semaphore_wait(barrier, len(peers))
    for k in (2, 3, 0, 1, 4, 5, 6, 7):
        pl.when(exists(*moves[k]))(lambda k=k: copy(k).start())

    ext[:channels, LANES : LANES + samples] = raw_ref[...]
    for load in loads[1:]:
        load.wait()
    rolled = pltpu.roll(jnp.broadcast_to(taps_ref[...], (WIN, depth)), 0, 1, stride=1, stride_axis=0)
    fir_t = rolled.astype(jnp.bfloat16)
    near = (jnp.abs(bins_of((WIN, WIN), 0) - bins_of((WIN, WIN), 1)) <= 4).astype(jnp.float32)
    row_bins = bins_of((1, WIN), 1)
    count = jnp.minimum(row_bins + 4, WIN // 2 - 1) - jnp.maximum(row_bins - 4, 0) + 1
    turned = jnp.transpose(pick_ref[...].astype(jnp.float32))
    for s in range(steps):
        wide = jnp.broadcast_to(turned[:, s : s + 1], (channels, LANES)).astype(jnp.int32)
        pick_wide[s] = wide
        chosen[s] = (
            wide[:, :P_SIZE] == lax.broadcasted_iota(jnp.int32, (channels, P_SIZE), 1)
        ).astype(jnp.bfloat16)

    @pl.when(me == 0)
    def _():
        in_low[...] = jnp.zeros_like(in_low)

    @pl.when(me == n_chan - 1)
    def _():
        in_high[...] = jnp.zeros_like(in_high)

    for k, (dc, dt) in enumerate(moves):
        there = exists(-dc, -dt)
        pl.when(there)(lambda k=k: copy(k).wait_recv())
        buf, slot = (time_in, k) if k < 2 else (chan_in, k - 2) if k < 4 else (corner_in, k - 4)

        @pl.when(jnp.logical_not(there))
        def _():
            buf[slot] = jnp.zeros(buf.shape[1:], buf.dtype)

    def rows(low, high):
        width = low.shape[1]
        spare = jnp.zeros((16 - 2 * side, width), jnp.float32)
        both = [low.astype(jnp.float32), high.astype(jnp.float32), spare]
        return jnp.concatenate(both, axis=0).astype(jnp.bfloat16)

    high_at = LANES + samples
    ext[:channels, :LANES] = time_in[0]
    ext[:channels, high_at:] = time_in[1]
    ext[channels:, LANES:high_at] = rows(chan_in[0], chan_in[1])
    ext[channels:, :LANES] = rows(corner_in[0], corner_in[2])
    ext[channels:, high_at:] = rows(corner_in[1], corner_in[3])
    power = jnp.zeros((channels, WIN), jnp.float32)
    for w in range(frames):
        block = ext[:, w * WIN : w * WIN + depth]
        got = lax.dot_general(block, fir_t, (((1,), (1,)), ((), ())), preferred_element_type=jnp.float32)
        slot = w % 2
        filt[slot, 8 : 8 + channels] = got[:channels]
        filt[slot, 8 - side : 8] = got[channels : channels + side]
        filt[slot, 8 + channels : 8 + channels + side] = got[channels + side : channels + 2 * side]
        shaped = sp_ref[0] * filt[slot, 8 - side : 8 - side + channels]
        for m in range(1, 2 * side + 1):
            shaped += sp_ref[m] * filt[slot, 8 - side + m : 8 - side + m + channels]
        spectra = jnp.dot(shaped.astype(jnp.bfloat16), table_ref[...], preferred_element_type=jnp.float32)
        spec[w] = spectra
        power += spectra * spectra
    level = jnp.dot(power, near, precision=HIGHEST, preferred_element_type=jnp.float32)
    level = level / (count.astype(jnp.float32) * frames)
    factor = taper_row(edges_ref) / jnp.sqrt(level + 1e-06)
    for w in range(frames):
        white_ref[w] = (spec[w] * factor).astype(jnp.bfloat16)
    half = WIN // 2
    part = channels // n_sub
    group = frames // SPLIT
    chunks = steps * SPLIT

    def up(c):
        return pltpu.make_async_remote_copy(
            src_ref=to_high.at[c], dst_ref=in_low.at[c], send_sem=sem_high.at[c], recv_sem=got_low.at[c],
            device_id={"chan": lax.rem(me + 1, n_chan)}, device_id_type=MESH)

    def down(c):
        return pltpu.make_async_remote_copy(
            src_ref=to_low.at[c], dst_ref=in_high.at[c], send_sem=sem_low.at[c], recv_sem=got_high.at[c],
            device_id={"chan": lax.rem(me + n_chan - 1, n_chan)}, device_id_type=MESH)

    def sub_copy(s, d):
        to = lax.rem(my_sub + d, n_sub)
        return pltpu.make_async_remote_copy(
            src_ref=own_lag.at[s, pl.ds(to * part, part)], dst_ref=sub_in.at[s, d - 1],
            send_sem=sub_send.at[s, d - 1], recv_sem=sub_recv.at[s, d - 1],
            device_id={"sub": to}, device_id_type=MESH)

    def tm_copy(s, d):
        return pltpu.make_async_remote_copy(
            src_ref=tm_in.at[s, my_tm], dst_ref=tm_in.at[s, my_tm],
            send_sem=tm_send.at[s, d - 1], recv_sem=tm_recv.at[s, d - 1],
            device_id={"tm": lax.rem(my_tm + d, n_tm)}, device_id_type=MESH)

    def fin_copy(s, d):
        here = pl.ds(my_sub * part, part)
        return pltpu.make_async_remote_copy(
            src_ref=done.at[s, here], dst_ref=done.at[s, here],
            send_sem=fin_send.at[s, d - 1], recv_sem=fin_recv.at[s, d - 1],
            device_id={"sub": lax.rem(my_sub + d, n_sub)}, device_id_type=MESH)

    def own_panel(s):
        panel = jnp.full((P_SIZE, WIN), panel_ref[s], jnp.int32)
        for w in range(frames):
            value = white_ref[w, :P_SIZE]
            for k in range(1, channels // P_SIZE):
                value = jnp.where(panel == k, white_ref[w, k * P_SIZE : (k + 1) * P_SIZE], value)
            own_ref[s, w] = value

    def stage(c, arrived, leaving):
        s = lax.div(c, SPLIT)
        k = lax.rem(c, SPLIT)
        mine = jnp.full((P_SIZE, WIN), owner_ref[s], jnp.int32) == me
        for w in range(group):
            leaving[c, w] = jnp.where(mine, own_ref[s, k * group + w], arrived[c, w])

    def relay(t):
        c = t - LAG * me

        @pl.when((c >= 0) & (c < chunks))
        def _():
            @pl.when(me > 0)
            def _():
                up(c).wait_recv()

            @pl.when(me < n_chan - 1)
            def _():
                stage(c, in_low, to_high)
                up(c).start()

        e = t - LAG * (n_chan - 1 - me)

        @pl.when((e >= 0) & (e < chunks))
        def _():
            @pl.when(me < n_chan - 1)
            def _():
                down(e).wait_recv()

            @pl.when(me > 0)
            def _():
                stage(e, in_high, to_low)
                down(e).start()

    def compute(s):
        rows = channels // 2
        owner = owner_ref[s]
        where = jnp.full((P_SIZE, WIN), owner, jnp.int32)
        start = owner * channels + panel_ref[s] * P_SIZE
        for r in range(2):
            here = slice(r * rows, (r + 1) * rows)
            acc_p = jnp.zeros((rows, WIN), jnp.float32)
            acc_q = jnp.zeros((rows, WIN), jnp.float32)
            for w in range(frames):
                c = s * SPLIT + w // group
                value = jnp.where(where < me, in_low[c, w % group], in_high[c, w % group])
                value = jnp.where(where == me, own_ref[s, w], value)
                partner = jnp.dot(chosen[s, here], value, preferred_element_type=jnp.float32)
                acc_p += plain[w, here] * partner
                acc_q += swapped[w, here] * partner
            lagged = jnp.dot(acc_p, lag_ref[:WIN], precision=HIGHEST, preferred_element_type=jnp.float32)
            lagged += jnp.dot(acc_q, lag_ref[WIN:], precision=HIGHEST, preferred_element_type=jnp.float32)
            receiver = me * channels + r * rows + lax.broadcasted_iota(jnp.int32, (rows, LAGS), 0)
            far = jnp.abs(receiver - (start + pick_wide[s, here])) > REACH
            own_lag[s, here] = jnp.where(far, 0.0, lagged)
        for d in range(1, n_sub):
            sub_copy(s, d).start()

    def sub_sum(s):
        total = own_lag[s, pl.ds(my_sub * part, part)]
        for d in range(1, n_sub):
            sub_copy(s, d).wait_recv()
            total += sub_in[s, d - 1]
        tm_in[s, my_tm] = total
        for d in range(1, n_tm):
            tm_copy(s, d).start()

    def tm_sum(s):
        for d in range(1, n_tm):
            tm_copy(s, d).wait_recv()
        total = tm_in[s, 0]
        for k in range(1, n_tm):
            total += tm_in[s, k]
        done[s, pl.ds(my_sub * part, part)] = total
        for d in range(1, n_sub):
            fin_copy(s, d).start()

    def finish(s):
        for d in range(1, n_sub):
            fin_copy(s, d).wait_recv()
        out_ref[s] = done[s]

    delay = -(-(n_chan - 1) * LAG // SPLIT)

    def turn(u, carry):
        pl.when(u < steps)(functools.partial(own_panel, u))
        for k in range(SPLIT):
            relay(u * SPLIT + k)

        @pl.when(u == 0)
        def _():
            for w in range(frames):
                value = white_ref[w].astype(jnp.float32)
                plain[w] = value
                for h in range(2):
                    swapped[w, :, h * half : (h + 1) * half] = pltpu.roll(
                        value[:, h * half : (h + 1) * half], half // 2, 1)

        for late, work in enumerate((compute, sub_sum, tm_sum, finish)):
            s = u - delay - late
            pl.when((s >= 0) & (s < steps))(functools.partial(work, s))
        return carry

    lax.fori_loop(0, steps + delay + 3, turn, 0)

    def drain_chunk(c, carry):
        @pl.when(me < n_chan - 1)
        def _():
            up(c).wait_send()

        @pl.when(me > 0)
        def _():
            down(c).wait_send()
        return carry

    lax.fori_loop(0, chunks, drain_chunk, 0)
    for k, move in enumerate(moves):
        pl.when(exists(*move))(lambda k=k: copy(k).wait_send())

    def drain_step(s, carry):
        for d in range(1, n_sub):
            sub_copy(s, d).wait_send()
            fin_copy(s, d).wait_send()
        for d in range(1, n_tm):
            tm_copy(s, d).wait_send()
        return carry

    lax.fori_loop(0, steps, drain_step, 0)


def lag_pair(scale):
    bins, parts = column_maps()
    lag = np.arange(LAGS) - LAGS // 2
    angle = 2.0 * np.pi * ((bins[:, None] * lag[None, :]) % WIN) / WIN
    real = np.cos(angle) * scale
    imag = np.where(parts[:, None] == 0, np.sin(angle), -np.sin(angle)) * scale
    full = np.concatenate([real, imag]).astype(np.float32)
    high = jnp.asarray(full).astype(jnp.bfloat16)
    low = (jnp.asarray(full) - high.astype(jnp.float32)).astype(jnp.bfloat16)
    return jnp.concatenate([high, low], axis=1)


GROUP = 4
AHEAD = 1


def split_kernel(frames, channels, side, steps, n_chan, n_tm, n_sub, sp_hbm, edges_hbm, owner_hbm, panel_hbm,
                 taps_hbm, pick_hbm, raw_hbm, table_hbm, lag_hbm, out_hbm,
                 sp_ref, edges_ref, owner_ref, panel_ref, taps_ref, pick_ref, raw_ref, table_ref, lag_ref,
                 spec, mixed, halo_ext, halo_win, ends_ref, rim_ref, power_ref,
                 time_in, chan_out, chan_in, corner_out, corner_in, white_ref, picks, chosen, pan, acc,
                 own_lag, sub_out, sub_in, z_out, z_in, done,
                 load_sem, halo_send, halo_recv, far_sem, pick_send, pick_recv, z_send, z_recv, x_send, x_recv,
                 sub_send, sub_recv, r_send, r_recv, a_send, a_recv, out_sem, *white_in):
    f32, bf16 = jnp.float32, jnp.bfloat16
    me, my_tm, my_sub = lax.axis_index("chan"), lax.axis_index("tm"), lax.axis_index("sub")
    n_time = n_tm * n_sub
    now = my_tm * n_sub + my_sub
    samples = frames * WIN
    n_taps = taps_ref.shape[0]
    depth = WIN + 2 * LANES
    panels = channels // P_SIZE
    per = frames // n_chan
    spd = steps // n_time
    spt = spd * n_sub
    mine, theirs = white_in[:per], white_in[per:]
    loads = [
        pltpu.make_async_copy(source, target, load_sem.at[k])
        for k, (source, target) in enumerate([
            (raw_hbm, raw_ref), (taps_hbm, taps_ref), (pick_hbm, pick_ref), (sp_hbm, sp_ref),
            (edges_hbm, edges_ref), (owner_hbm, owner_ref), (panel_hbm, panel_ref),
            (table_hbm, table_ref), (lag_hbm, lag_ref),
        ])
    ]
    for load in loads[1:] + loads[:1]:
        load.start()

    def at_time(dt):
        at = lax.rem(now + dt + n_time, n_time)
        return {"tm": lax.div(at, n_sub), "sub": lax.rem(at, n_sub)}

    def peer(dc, dt):
        return {"chan": lax.rem(me + dc + n_chan, n_chan), **at_time(dt)}

    def exists(dc, dt):
        return (me + dc >= 0) & (me + dc < n_chan) & (now + dt >= 0) & (now + dt < n_time)

    moves = [(0, 1), (0, -1), (1, 0), (-1, 0), (1, 1), (1, -1), (-1, 1), (-1, -1)]
    barrier = pltpu.get_barrier_semaphore()
    for dt in range(1, n_time):
        pl.semaphore_signal(barrier, inc=1, device_id=at_time(dt), device_id_type=MESH)
    for move in moves[2:]:
        @pl.when(exists(*move))
        def _(move=move):
            pl.semaphore_signal(barrier, inc=1, device_id=peer(*move), device_id_type=MESH)

    for load in loads[1:]:
        load.wait()
    taps = taps_ref[...].astype(f32).reshape(1, n_taps)
    taps = jnp.concatenate([taps, jnp.zeros((1, depth - n_taps), f32)], axis=1)
    shift = LANES - (n_taps - 1) // 2
    rolled = pltpu.roll(jnp.broadcast_to(taps, (WIN, depth)), shift, 1, stride=1, stride_axis=0)
    fir_w = jnp.transpose(rolled).astype(bf16)
    parts = [fir_w[LANES : LANES + WIN]] * 2 + [fir_w[:LANES], fir_w[LANES + WIN :]] * 2
    fir_pair = jnp.concatenate(parts, axis=0)
    near = (jnp.abs(bins_of((WIN, WIN), 0) - bins_of((WIN, WIN), 1)) <= 4).astype(bf16)
    row_bins = bins_of((1, WIN), 1)
    count = jnp.minimum(row_bins + 4, WIN // 2 - 1) - jnp.maximum(row_bins - 4, 0) + 1
    taper = taper_row(edges_ref)

    def fir(block, first=0, last=depth):
        return jnp.dot(block, fir_w[first:last], preferred_element_type=f32)

    def taps_at(offset):
        total = jnp.zeros(offset.shape, f32)
        for m in range(2 * side + 1):
            total = jnp.where(offset == m - side, sp_ref[m], total)
        return total

    def two(value):
        high = value.astype(bf16)
        return high, (value - high.astype(f32)).astype(bf16)

    def across(matrix, value):
        m_high, m_low = matrix
        v_high, v_low = two(value)
        left = jnp.concatenate([m_high, m_low, m_high], axis=1)
        right = jnp.concatenate([v_high, v_high, v_low], axis=0)
        return jnp.dot(left, right, preferred_element_type=f32)

    def iota(shape, axis):
        return lax.broadcasted_iota(jnp.int32, shape, axis)

    square = (channels, channels)
    spatial = two(taps_at(iota(square, 1) - iota(square, 0)))
    rim = channels - 16
    stacked = jnp.concatenate(spatial, axis=0)
    row, column = iota((16, frames * 16), 0), iota((16, frames * 16), 1)
    row_channel = jnp.where(row < 8, row, row + rim)
    spot = lax.rem(column, 16)
    column_channel = jnp.where(spot < side, spot - side, jnp.where(spot < 2 * side, channels + spot - side, 4 * channels))
    base = taps_at(column_channel - row_channel)
    frame_of = lax.div(column, 16)
    rim_matrix = two(jnp.concatenate([jnp.where(frame_of == w, base, 0.0) for w in range(frames)], axis=0))
    for k in range(2):
        for at in (0, frames + 1):
            mixed[k, at] = jnp.zeros((channels, WIN), bf16)
    loads[0].wait()
    ends = (slice(channels - side, channels), slice(0, side))
    sides = (slice(samples - LANES, samples), slice(0, LANES))
    for k in range(2):
        chan_out[k] = raw_ref[ends[k]]
        for h in range(2):
            corner_out[2 * k + h] = raw_ref[ends[k], sides[h]]

    def copy(k):
        dc, dt = moves[k]
        if k < 2:
            src, dst = raw_ref.at[:, sides[k]], time_in.at[k]
        elif k < 4:
            src, dst = chan_out.at[k - 2], chan_in.at[k - 2]
        else:
            src, dst = corner_out.at[k - 4], corner_in.at[k - 4]
        return pltpu.make_async_remote_copy(
            src_ref=src, dst_ref=dst, send_sem=halo_send.at[k], recv_sem=halo_recv.at[k],
            device_id=peer(dc, dt), device_id_type=MESH)

    greeted = sum(exists(*move).astype(jnp.int32) for move in moves[2:])
    pl.semaphore_wait(barrier, n_time - 1 + greeted)
    for k in (2, 3, 0, 1, 4, 5, 6, 7):
        pl.when(exists(*moves[k]))(lambda k=k: copy(k).start())

    inner = (me > 0) & (me < n_chan - 1)

    def token(way):
        pl.semaphore_signal(far_sem.at[way], inc=1, device_id={"chan": me + 1 - 2 * way}, device_id_type=MESH)

    def relay_tokens(k):
        for way, distance in ((0, me), (1, n_chan - 1 - me)):
            @pl.when(distance >= k + 1)
            def _():
                pl.semaphore_wait(far_sem.at[way], 1)
            pl.when((distance >= k + 1) & inner)(lambda: token(way))

    for way in range(2):
        pl.when(inner)(lambda: token(way))

    def pick_copy(d):
        return pltpu.make_async_remote_copy(
            src_ref=pick_ref, dst_ref=picks.at[me], send_sem=pick_send.at[0], recv_sem=pick_recv.at[0],
            device_id={"chan": lax.rem(me + d, n_chan)}, device_id_type=MESH)

    def pick_all():
        rest = picks.at[pl.ds(0, n_chan - 1)]
        return pltpu.make_async_remote_copy(
            src_ref=rest, dst_ref=rest, send_sem=pick_send.at[0], recv_sem=pick_recv.at[0],
            device_id={"chan": lax.rem(me + 1, n_chan)}, device_id_type=MESH)

    for w in range(frames):
        got = jnp.dot(stacked, raw_ref[:, w * WIN : (w + 1) * WIN], preferred_element_type=f32)
        mixed[0, w + 1], mixed[1, w + 1] = two(got[:channels] + got[channels:])

    def filtered(g):
        sides = []
        for k in range(2):
            sides.append(mixed[k, g + 1 : g + 1 + GROUP])
        for k in range(2):
            sides += [mixed[k, g : g + GROUP, :, WIN - LANES :], mixed[k, g + 2 : g + 2 + GROUP, :, :LANES]]
        windows = jnp.concatenate(sides, axis=2).reshape(GROUP * channels, 2 * depth)
        return jnp.dot(windows, fir_pair, preferred_element_type=f32)

    power = jnp.zeros((channels, WIN), f32)
    ready = filtered(0)
    for g in range(0, frames, GROUP):
        part, ready = ready, filtered(g + GROUP) if g + GROUP < frames else None
        spectra = jnp.dot(part.astype(bf16), table_ref[...], preferred_element_type=f32)
        part, spectra = part.reshape(GROUP, channels, WIN), spectra.reshape(GROUP, channels, WIN)
        for k in range(GROUP):
            w = g + k
            if w in (0, frames - 1):
                ends_ref[min(w, 1)] = part[k]
                continue
            rim_ref[w, :8] = part[k, :8]
            rim_ref[w, 8:] = part[k, channels - 8 :]
            spec[w] = spectra[k]
            power += spectra[k] * spectra[k]
    power_ref[...] = power
    relay_tokens(1)

    for k, (dc, dt) in enumerate(moves):
        there = exists(-dc, -dt)
        pl.when(there)(lambda k=k: copy(k).wait_recv())
        buf, slot = (time_in, k) if k < 2 else (chan_in, k - 2) if k < 4 else (corner_in, k - 4)

        @pl.when(jnp.logical_not(there))
        def _():
            buf[slot] = jnp.zeros(buf.shape[1:], buf.dtype)

    def rows(low, high):
        width = low.shape[1]
        spare = jnp.zeros((16 - 2 * side, width), f32)
        both = [low.astype(f32), high.astype(f32), spare]
        return jnp.concatenate(both, axis=0).astype(bf16)

    halo_ext[:, LANES : LANES + samples] = rows(chan_in[0], chan_in[1])
    halo_ext[:, :LANES] = rows(corner_in[0], corner_in[2])
    halo_ext[:, LANES + samples :] = rows(corner_in[1], corner_in[3])
    for w in range(frames):
        halo_win[w] = halo_ext[:, w * WIN : w * WIN + depth]
    halo = fir(halo_win[...].reshape(frames * 16, depth))
    late = [fir(time_in[k], k * (depth - LANES), k * (depth - LANES) + LANES) for k in range(2)]
    rim_part = across(rim_matrix, halo).reshape(frames, 16, WIN)
    late = [across(spatial, value) for value in late]
    blocks = [rim_ref[1 : frames - 1] + rim_part[1 : frames - 1]]
    blocks[0] = blocks[0].reshape((frames - 2) * 16, WIN)
    for k, w in enumerate((0, frames - 1)):
        whole = ends_ref[k] + late[k]
        blocks += [whole[:8] + rim_part[w, :8], whole[8 : channels - 8], whole[channels - 8 :] + rim_part[w, 8:]]
    shaped = jnp.concatenate(blocks, axis=0).astype(bf16)
    spectra = jnp.dot(shaped, table_ref[...], preferred_element_type=f32)
    rims, whole = spectra[: (frames - 2) * 16].reshape(frames - 2, 16, WIN), spectra[(frames - 2) * 16 :]
    whole = whole.reshape(2, channels, WIN)
    for w in range(1, frames - 1):
        spec[w, :8] = rims[w - 1, :8]
        spec[w, channels - 8 :] = rims[w - 1, 8:]
    for k, w in enumerate((0, frames - 1)):
        spec[w] = whole[k]
    rims = jnp.sum(rims * rims, axis=0)
    inside = power_ref[8 : channels - 8]
    power = jnp.concatenate([rims[:8], inside, rims[8:]], axis=0) + jnp.sum(whole * whole, axis=0)
    for k in range(2, n_chan - 1):
        relay_tokens(k)
    for d in range(1, n_chan):
        pick_copy(d).start()
    level = jnp.dot(
        jnp.concatenate(two(power), axis=1), jnp.concatenate([near, near], axis=0), preferred_element_type=f32)
    level = level / (count.astype(f32) * frames)
    factor = taper / jnp.sqrt(level + 1e-06)

    def whiten(w):
        return (spec[w] * factor).astype(bf16).reshape(panels, P_SIZE, WIN)

    def block_of(q):
        return pl.ds(q * panels, panels)

    def z_copy(j, d):
        to = lax.rem(me + d, n_chan)
        return pltpu.make_async_remote_copy(
            src_ref=white_ref.at[to * per + j], dst_ref=mine[j].at[block_of(me)],
            send_sem=z_send.at[j % AHEAD, d - 1], recv_sem=z_recv.at[j, d - 1],
            device_id={"chan": to}, device_id_type=MESH)

    def x_copy(j, e, k):
        at = slice(None) if e is None else block_of(lax.rem(me - e + n_chan, n_chan))
        return pltpu.make_async_remote_copy(
            src_ref=mine[j].at[at], dst_ref=theirs[j].at[k - 1, at],
            send_sem=x_send.at[j, k - 1], recv_sem=x_recv.at[j, k - 1],
            device_id={"tm": lax.rem(my_tm + k, n_tm)}, device_id_type=MESH)

    near_first = sorted(range(1, n_chan), key=lambda d: (min(d, n_chan - d), d))
    far_first = near_first[::-1]
    for j in range(per):
        for d in far_first:
            w = lax.rem(me + d, n_chan) * per + j
            white_ref[w] = whiten(w)
            if j < AHEAD:
                z_copy(j, d).start()
        mine[j][block_of(me)] = whiten(me * per + j)
        for k in range(1, n_tm):
            x_copy(j, 0, k).start()
    picks[me] = pick_ref[...]
    pick_all().wait_recv()
    for i in range(spt):
        for q in range(n_chan):
            pick = jnp.broadcast_to(picks[q, pl.ds(my_tm * spt + i, 1)], (P_SIZE, channels))
            hit = (pick == iota((P_SIZE, channels), 0)).astype(f32)
            chosen[i, q * channels : (q + 1) * channels] = jnp.transpose(hit).astype(bf16)

    half = WIN // 2

    def source(unit):
        j, k = unit
        return mine[j] if k == 0 else theirs[j].at[k - 1]

    def gather(units):
        for i in range(spt):
            s = my_tm * spt + i
            at = owner_ref[s] * panels + panel_ref[s]
            for u, unit in enumerate(units):
                value = source(unit)[at]
                wide = value.astype(f32)
                turn = [pltpu.roll(wide[:, h * half : (h + 1) * half], half // 2, 1) for h in range(2)]
                pan[i, u, :, :WIN] = value
                pan[i, u, :, WIN:] = jnp.concatenate(turn, axis=1).astype(bf16)

    everyone = n_chan * channels

    def receivers(unit):
        return source(unit)[...].reshape(everyone, WIN).astype(f32)

    def products(units, i, values):
        p = q = None
        for u, value in enumerate(values):
            partner = jnp.dot(chosen[i], pan[i, u], preferred_element_type=f32)
            dp, dq = value * partner[:, :WIN], value * partner[:, WIN:]
            p, q = (dp, dq) if u == 0 else (p + dp, q + dq)
        return p, q

    def accumulate(units, first):
        gather(units)
        values = [receivers(unit) for unit in units]

        def step(i, carry):
            p, q = products(units, i, values)
            if not first:
                p += acc[i, 0]
                q += acc[i, 1]
            acc[i, 0] = p
            acc[i, 1] = q
            return carry

        for i in range(spt):
            step(i, 0)

    def forward(j):
        for d in near_first:
            z_copy(j, d).wait_send()
            if j + AHEAD < per:
                z_copy(j + AHEAD, d).start()
        for d in near_first:
            z_copy(j, d).wait_recv()
            for k in range(1, n_tm):
                x_copy(j, d, k).start()

    def arrive(j):
        for k in range(1, n_tm):
            x_copy(j, None, k).wait_recv()

    def others(j):
        return [(j, k) for k in range(1, n_tm)]

    last = per - 1
    for j in range(per):
        forward(j)
        units = [(j, 0)]
        if j > 0:
            arrive(j - 1)
            units += others(j - 1)
        accumulate(units, j == 0)
    arrive(last)
    gather(others(last))

    def summed_products(i):
        p, q = products(others(last), i, [receivers(unit) for unit in others(last)])
        return (p + acc[i, 0]).astype(bf16), (q + acc[i, 1]).astype(bf16)

    def lagged(both):
        lags = jnp.dot(both[0], lag_ref[:WIN], preferred_element_type=f32)
        lags += jnp.dot(both[1], lag_ref[WIN:], preferred_element_type=f32)
        return lags[:, :LAGS] + lags[:, LAGS:]

    def sub_copy(k, d):
        to = lax.rem(my_sub + d, n_sub)
        return pltpu.make_async_remote_copy(
            src_ref=sub_out.at[k, d - 1], dst_ref=sub_in.at[k, d - 1],
            send_sem=sub_send.at[k, d - 1], recv_sem=sub_recv.at[k, d - 1],
            device_id={"sub": to}, device_id_type=MESH)

    def r_copy(k, d):
        to = lax.rem(me + d, n_chan)
        return pltpu.make_async_remote_copy(
            src_ref=z_out.at[k, d - 1], dst_ref=z_in.at[k, d - 1], send_sem=r_send.at[k], recv_sem=r_recv.at[k],
            device_id={"chan": to}, device_id_type=MESH)

    def r_all(k):
        return pltpu.make_async_remote_copy(
            src_ref=z_out.at[k], dst_ref=z_in.at[k], send_sem=r_send.at[k], recv_sem=r_recv.at[k],
            device_id={"chan": lax.rem(me + 1, n_chan)}, device_id_type=MESH)

    def a_copy(k, d):
        return pltpu.make_async_remote_copy(
            src_ref=done.at[k], dst_ref=out_hbm.at[now * spd + k], send_sem=a_send.at[k], recv_sem=a_recv.at[k],
            device_id=at_time(d), device_id_type=MESH)

    def a_all(k):
        rest = out_hbm.at[pl.ds(0, n_time - 1)]
        return pltpu.make_async_remote_copy(
            src_ref=rest, dst_ref=rest, send_sem=a_send.at[k], recv_sem=a_recv.at[k],
            device_id=at_time(1), device_id_type=MESH)

    def store(k):
        return pltpu.make_async_copy(done.at[k], out_hbm.at[now * spd + k], out_sem.at[k])

    work = [(d, k) for d in [*range(1, n_sub), 0] for k in range(spd)]

    def at_step(d, k):
        return lax.rem(my_sub + d, n_sub) * spd + k

    kept = []
    coming = summed_products(at_step(*work[0]))
    for n, (d, k) in enumerate(work):
        current, coming = coming, summed_products(at_step(*work[n + 1])) if n + 1 < len(work) else None
        lags = lagged(current)
        if d > 0:
            sub_out[k, d - 1] = lags.astype(bf16)
            sub_copy(k, d).start()
            continue
        own_lag[k] = lags
        for other in range(1, n_sub):
            sub_copy(k, other).wait_recv()

        def summed(q, k=k):
            here = pl.ds(q * channels, channels)
            value = own_lag[k, here]
            for other in range(1, n_sub):
                value += sub_in[k, other - 1, here].astype(f32)
            return value

        for way in far_first:
            z_out[k, way - 1] = summed(lax.rem(me + way, n_chan)).astype(bf16)
            r_copy(k, way).start()
        kept.append(summed(me))
    picked = []
    for k in range(spd):
        pick = jnp.broadcast_to(pick_ref[pl.ds(now * spd + k, 1)], (LAGS, channels))
        picked.append(jnp.transpose(pick.astype(f32)).astype(jnp.int32))
    receiver = me * channels + lax.broadcasted_iota(jnp.int32, (channels, LAGS), 0)
    for k in range(spd):
        s = now * spd + k
        value = kept[k]
        r_all(k).wait_recv()
        for d in range(1, n_chan):
            value += z_in[k, d - 1].astype(f32)
        start = owner_ref[s] * channels + panel_ref[s] * P_SIZE
        far = jnp.abs(receiver - (start + picked[k])) > REACH
        done[k] = jnp.where(far, 0.0, value).astype(bf16)
        for d in range(1, n_time):
            a_copy(k, d).start()
        store(k).start()
    for k in range(spd):
        if n_time > 1:
            a_all(k).wait_recv()
    for k, move in enumerate(moves):
        pl.when(exists(*move))(lambda k=k: copy(k).wait_send())
    pick_all().wait_send()
    for k in range(1, n_tm):
        for j in range(per):
            x_copy(j, None, k).wait_send()
    for k in range(spd):
        for d in range(1, n_sub):
            sub_copy(k, d).wait_send()
        r_all(k).wait_send()
        if n_time > 1:
            a_all(k).wait_send()
    for k in range(spd):
        store(k).wait()


VMEM = pl.BlockSpec(memory_space=pltpu.VMEM)


def relay(raw, fir_taps, spatial_taps, band_edges, source_owner, source_panel, source_pick):
    channels, samples = raw.shape
    margin = (fir_taps.shape[0] - 1) // 2
    side = spatial_taps.shape[0] // 2
    frames = samples // WIN
    steps = source_owner.shape[0]
    times = ("tm", "sub")
    count = lax.axis_size(times)
    n_chan = lax.axis_size("chan")
    n_tm, n_sub = lax.axis_size("tm"), lax.axis_size("sub")
    depth = WIN + 2 * LANES
    first = LANES - margin
    taps = jnp.pad(fir_taps.astype(jnp.float32), (first, depth - first - fir_taps.shape[0]))[None, :]
    total = frames * n_tm * n_sub
    lag_table = lag_tables(1.0 / math.sqrt(total * (WIN // 2)))
    chunks = steps * SPLIT
    flow = pltpu.VMEM((chunks, frames // SPLIT, P_SIZE, WIN), jnp.bfloat16)
    part = channels // n_sub
    dma = pltpu.SemaphoreType.DMA
    any_space = pl.BlockSpec(memory_space=pltpu.HBM)
    bf16, f32 = jnp.bfloat16, jnp.float32
    return pl.pallas_call(
        functools.partial(relay_kernel, frames, channels, side, steps, n_chan, n_tm, n_sub),
        out_shape=jax.ShapeDtypeStruct((steps, channels, LAGS), f32),
        in_specs=[any_space] * 9,
        out_specs=VMEM,
        scratch_shapes=[
            pltpu.SMEM(spatial_taps.shape, f32),
            pltpu.SMEM(band_edges.shape, jnp.int32),
            pltpu.SMEM(source_owner.shape, jnp.int32),
            pltpu.SMEM(source_panel.shape, jnp.int32),
            pltpu.VMEM(taps.shape, f32),
            pltpu.VMEM(source_pick.shape, jnp.int32),
            pltpu.VMEM(raw.shape, bf16),
            pltpu.VMEM((WIN, WIN), bf16),
            pltpu.VMEM((2 * WIN, LAGS), f32),
            pltpu.VMEM((2, channels + 16, WIN), f32),
            pltpu.VMEM((frames, channels, WIN), f32),
            pltpu.VMEM((channels + 16, samples + 2 * LANES), bf16),
            pltpu.VMEM((2, channels, LANES), bf16),
            pltpu.VMEM((2, side, samples), bf16),
            pltpu.VMEM((2, side, samples), bf16),
            pltpu.VMEM((4, side, LANES), bf16),
            pltpu.VMEM((4, side, LANES), bf16),
            dma((8,)), dma((8,)), dma((9,)),
            pltpu.VMEM((frames, channels, WIN), bf16),
            pltpu.VMEM((steps, frames, P_SIZE, WIN), bf16),
            pltpu.VMEM((steps, channels, P_SIZE), bf16),
            pltpu.VMEM((steps, channels, LANES), jnp.int32),
            pltpu.VMEM((frames, channels, WIN), f32),
            pltpu.VMEM((frames, channels, WIN), f32),
            flow, flow, flow, flow,
            pltpu.VMEM((steps, channels, LAGS), f32),
            pltpu.VMEM((steps, n_sub - 1, part, LAGS), f32),
            pltpu.VMEM((steps, n_tm, part, LAGS), f32),
            pltpu.VMEM((steps, channels, LAGS), f32),
            dma((chunks,)), dma((chunks,)), dma((chunks,)), dma((chunks,)),
            dma((steps, n_sub - 1)), dma((steps, n_sub - 1)),
            dma((steps, n_tm - 1)), dma((steps, n_tm - 1)),
            dma((steps, n_sub - 1)), dma((steps, n_sub - 1)),
        ],
        compiler_params=pltpu.CompilerParams(
            vmem_limit_bytes=64 * 2**20, collective_id=0, has_side_effects=True),
        name="correlate",
    )(spatial_taps, band_edges, source_owner, source_panel, taps, source_pick, raw, spectral_table(), lag_table)


def split(raw, fir_taps, spatial_taps, band_edges, source_owner, source_panel, source_pick):
    channels, samples = raw.shape
    side = spatial_taps.shape[0] // 2
    frames = samples // WIN
    steps = source_owner.shape[0]
    n_chan, n_tm, n_sub = lax.axis_size("chan"), lax.axis_size("tm"), lax.axis_size("sub")
    n_time = n_tm * n_sub
    depth = WIN + 2 * LANES
    lag_table = lag_pair(1.0 / math.sqrt(frames * n_time * (WIN // 2)))
    per, spd = frames // n_chan, steps // n_time
    spt = spd * n_sub
    panels, everyone = channels // P_SIZE, n_chan * channels
    dma, any_space = pltpu.SemaphoreType.DMA, pl.BlockSpec(memory_space=pltpu.HBM)
    bf16, f32 = jnp.bfloat16, jnp.float32
    return pl.pallas_call(
        functools.partial(split_kernel, frames, channels, side, steps, n_chan, n_tm, n_sub),
        out_shape=jax.ShapeDtypeStruct((steps, channels, LAGS), bf16),
        in_specs=[any_space] * 9,
        out_specs=any_space,
        scratch_shapes=[
            pltpu.SMEM(spatial_taps.shape, f32),
            pltpu.SMEM(band_edges.shape, jnp.int32),
            pltpu.SMEM(source_owner.shape, jnp.int32),
            pltpu.SMEM(source_panel.shape, jnp.int32),
            pltpu.VMEM(fir_taps.shape, bf16),
            pltpu.VMEM(source_pick.shape, jnp.int32),
            pltpu.VMEM(raw.shape, bf16),
            pltpu.VMEM((WIN, WIN), bf16),
            pltpu.VMEM(lag_table.shape, bf16),
            pltpu.VMEM((frames, channels, WIN), f32),
            pltpu.VMEM((2, frames + 2, channels, WIN), bf16),
            pltpu.VMEM((16, samples + 2 * LANES), bf16),
            pltpu.VMEM((frames, 16, depth), bf16),
            pltpu.VMEM((2, channels, WIN), f32),
            pltpu.VMEM((frames, 16, WIN), f32),
            pltpu.VMEM((channels, WIN), f32),
            pltpu.VMEM((2, channels, LANES), bf16),
            pltpu.VMEM((2, side, samples), bf16),
            pltpu.VMEM((2, side, samples), bf16),
            pltpu.VMEM((4, side, LANES), bf16),
            pltpu.VMEM((4, side, LANES), bf16),
            pltpu.VMEM((frames, panels, P_SIZE, WIN), bf16),
            pltpu.VMEM((n_chan, *source_pick.shape), jnp.int32),
            pltpu.VMEM((spt, everyone, P_SIZE), bf16),
            pltpu.VMEM((spt, n_tm, P_SIZE, 2 * WIN), bf16),
            pltpu.VMEM((spt, 2, everyone, WIN), f32),
            pltpu.VMEM((spd, everyone, LAGS), f32),
            pltpu.VMEM((spd, max(n_sub - 1, 1), everyone, LAGS), bf16),
            pltpu.VMEM((spd, max(n_sub - 1, 1), everyone, LAGS), bf16),
            pltpu.VMEM((spd, n_chan - 1, channels, LAGS), bf16),
            pltpu.VMEM((spd, n_chan - 1, channels, LAGS), bf16),
            pltpu.VMEM((spd, channels, LAGS), bf16),
            dma((9,)), dma((8,)), dma((8,)), pltpu.SemaphoreType.REGULAR((2,)),
            dma((1,)), dma((1,)), dma((AHEAD, n_chan - 1)), dma((per, n_chan - 1)),
            dma((per, max(n_tm - 1, 1))), dma((per, max(n_tm - 1, 1))),
            dma((spd, max(n_sub - 1, 1))), dma((spd, max(n_sub - 1, 1))),
            dma((spd,)), dma((spd,)), dma((spd,)), dma((spd,)), dma((spd,)),
        ] + [pltpu.VMEM((n_chan * panels, P_SIZE, WIN), bf16)] * per
        + [pltpu.VMEM((max(n_tm - 1, 1), n_chan * panels, P_SIZE, WIN), bf16)] * per,
        compiler_params=pltpu.CompilerParams(
            vmem_limit_bytes=60 * 2**20, collective_id=0, has_side_effects=True),
        name="correlate",
    )(spatial_taps, band_edges, source_owner, source_panel, fir_taps, source_pick, raw, spectral_table(), lag_table).astype(f32)


def shards(*blocks):
    frames, steps = blocks[0].shape[1] // WIN, blocks[4].shape[0]
    chans = lax.axis_size("chan")
    even = chans > 1 and frames % chans == 0 and frames % GROUP == 0 and steps % lax.axis_size(("tm", "sub")) == 0
    return (split if even else relay)(*blocks)


def solution(mesh):
    placed = (
        P(("grp", "chan"), ("tm", "sub")),
        P(),
        P(),
        P(),
        P("grp"),
        P(),
        P(None, ("grp", "chan")),
    )
    return jax.shard_map(
        shards,
        mesh=mesh,
        in_specs=placed,
        out_specs=P(None, ("grp", "chan"), None),
        check_vma=False,
    )
```

```python
import functools
import math

import jax
import jax.numpy as jnp
import numpy as np
from jax import lax
from jax.experimental import pallas as pl
from jax.experimental.pallas import tpu as pltpu
from jax.sharding import PartitionSpec as P

P_SIZE = 32
WIN = 256
LAGS = 128
REACH = 1000
HIGHEST = lax.Precision.HIGHEST


def column_maps():
    column = np.arange(WIN)
    quarter = WIN // 4
    bins = column // (2 * quarter) * quarter + column % quarter
    parts = column // quarter % 2
    return bins, parts


def spectral_table():
    bins, parts = column_maps()
    angle = 2.0 * np.pi * ((bins[None, :] * np.arange(WIN)[:, None]) % WIN) / WIN
    table = np.where(parts == 0, np.cos(angle), -np.sin(angle)) / math.sqrt(WIN)
    return jnp.asarray(table.astype(np.float32)).astype(jnp.bfloat16)


def bins_of(shape, axis):
    column = lax.broadcasted_iota(jnp.int32, shape, axis)
    quarter = WIN // 4
    return lax.div(column, 2 * quarter) * quarter + lax.rem(column, quarter)


def lag_tables(scale):
    bins, parts = column_maps()
    lag = np.arange(LAGS) - LAGS // 2
    angle = 2.0 * np.pi * ((bins[:, None] * lag[None, :]) % WIN) / WIN
    real = np.cos(angle) * scale
    imag = np.where(parts[:, None] == 0, -np.sin(angle), np.sin(angle)) * scale
    return jnp.asarray(np.concatenate([real, imag]).astype(np.float32))


def taper_row(edges_ref):
    bins = bins_of((1, WIN), 1).astype(jnp.float32)
    e0, e1, e2, e3 = [jnp.full((1, WIN), edges_ref[k]).astype(jnp.float32) for k in range(4)]
    rising = 0.5 - 0.5 * jnp.cos(math.pi * (bins - e0) / (e1 - e0))
    falling = 0.5 - 0.5 * jnp.cos(math.pi * (e3 - bins) / (e3 - e2))
    inner = jnp.where(bins < e3, falling, 0.0)
    inner = jnp.where(bins <= e2, 1.0, inner)
    inner = jnp.where(bins < e1, rising, inner)
    return jnp.where(bins <= e0, 0.0, inner)


LANES = 128
SPLIT = 2
LAG = 2
MESH = pl.DeviceIdType.MESH


def relay_kernel(frames, channels, side, steps, n_chan, n_tm, n_sub, sp_hbm, edges_hbm, owner_hbm, panel_hbm,
           taps_hbm, pick_hbm, raw_hbm, table_hbm, lag_hbm, out_ref,
           sp_ref, edges_ref, owner_ref, panel_ref, taps_ref, pick_ref, raw_ref, table_ref, lag_ref, filt, spec, ext, time_in, chan_out, chan_in, corner_out, corner_in, send_sem,
           recv_sem, load_sem, white_ref, own_ref, chosen, pick_wide, plain, swapped, in_low, in_high, to_high,
           to_low, own_lag, sub_in, tm_in, done, sem_high, sem_low, got_low, got_high, sub_send, sub_recv,
           tm_send, tm_recv, fin_send, fin_recv):
    my_tm = lax.axis_index("tm")
    my_sub = lax.axis_index("sub")
    loads = [
        pltpu.make_async_copy(source, target, load_sem.at[k])
        for k, (source, target) in enumerate([
            (raw_hbm, raw_ref), (taps_hbm, taps_ref), (pick_hbm, pick_ref), (sp_hbm, sp_ref),
            (edges_hbm, edges_ref), (owner_hbm, owner_ref), (panel_hbm, panel_ref),
            (table_hbm, table_ref), (lag_hbm, lag_ref),
        ])
    ]
    for load in loads:
        load.start()
    me = lax.axis_index("chan")
    n_time = n_tm * n_sub
    now = lax.axis_index("tm") * n_sub + lax.axis_index("sub")
    samples = frames * WIN
    depth = taps_ref.shape[1]

    def peer(dc, dt):
        at = lax.rem(now + dt + n_time, n_time)
        return {"chan": lax.rem(me + dc + n_chan, n_chan), "tm": lax.div(at, n_sub), "sub": lax.rem(at, n_sub)}

    moves = [(0, 1), (0, -1), (1, 0), (-1, 0), (1, 1), (1, -1), (-1, 1), (-1, -1)]
    barrier = pltpu.get_barrier_semaphore()
    peers = [peer(dc, dt) for dc, dt in moves]
    peers += [{"tm": lax.rem(my_tm + d, n_tm)} for d in range(1, n_tm)]
    peers += [{"sub": lax.rem(my_sub + d, n_sub)} for d in range(1, n_sub)]
    for to in peers:
        pl.semaphore_signal(barrier, inc=1, device_id=to, device_id_type=MESH)

    loads[0].wait()
    ends = (slice(channels - side, channels), slice(0, side))
    sides = (slice(samples - LANES, samples), slice(0, LANES))
    for k in range(2):
        chan_out[k] = raw_ref[ends[k]]
        for h in range(2):
            corner_out[2 * k + h] = raw_ref[ends[k], sides[h]]

    def exists(dc, dt):
        return (me + dc >= 0) & (me + dc < n_chan) & (now + dt >= 0) & (now + dt < n_time)

    def copy(k):
        dc, dt = moves[k]
        if k < 2:
            src, dst = raw_ref.at[:, sides[k]], time_in.at[k]
        elif k < 4:
            src, dst = chan_out.at[k - 2], chan_in.at[k - 2]
        else:
            src, dst = corner_out.at[k - 4], corner_in.at[k - 4]
        return pltpu.make_async_remote_copy(
            src_ref=src, dst_ref=dst, send_sem=send_sem.at[k], recv_sem=recv_sem.at[k],
            device_id=peer(dc, dt), device_id_type=MESH)

    pl.semaphore_wait(barrier, len(peers))
    for k in (2, 3, 0, 1, 4, 5, 6, 7):
        pl.when(exists(*moves[k]))(lambda k=k: copy(k).start())

    ext[:channels, LANES : LANES + samples] = raw_ref[...]
    for load in loads[1:]:
        load.wait()
    rolled = pltpu.roll(jnp.broadcast_to(taps_ref[...], (WIN, depth)), 0, 1, stride=1, stride_axis=0)
    fir_t = rolled.astype(jnp.bfloat16)
    near = (jnp.abs(bins_of((WIN, WIN), 0) - bins_of((WIN, WIN), 1)) <= 4).astype(jnp.float32)
    row_bins = bins_of((1, WIN), 1)
    count = jnp.minimum(row_bins + 4, WIN // 2 - 1) - jnp.maximum(row_bins - 4, 0) + 1
    turned = jnp.transpose(pick_ref[...].astype(jnp.float32))
    for s in range(steps):
        wide = jnp.broadcast_to(turned[:, s : s + 1], (channels, LANES)).astype(jnp.int32)
        pick_wide[s] = wide
        chosen[s] = (
            wide[:, :P_SIZE] == lax.broadcasted_iota(jnp.int32, (channels, P_SIZE), 1)
        ).astype(jnp.bfloat16)

    @pl.when(me == 0)
    def _():
        in_low[...] = jnp.zeros_like(in_low)

    @pl.when(me == n_chan - 1)
    def _():
        in_high[...] = jnp.zeros_like(in_high)

    for k, (dc, dt) in enumerate(moves):
        there = exists(-dc, -dt)
        pl.when(there)(lambda k=k: copy(k).wait_recv())
        buf, slot = (time_in, k) if k < 2 else (chan_in, k - 2) if k < 4 else (corner_in, k - 4)

        @pl.when(jnp.logical_not(there))
        def _():
            buf[slot] = jnp.zeros(buf.shape[1:], buf.dtype)

    def rows(low, high):
        width = low.shape[1]
        spare = jnp.zeros((16 - 2 * side, width), jnp.float32)
        both = [low.astype(jnp.float32), high.astype(jnp.float32), spare]
        return jnp.concatenate(both, axis=0).astype(jnp.bfloat16)

    high_at = LANES + samples
    ext[:channels, :LANES] = time_in[0]
    ext[:channels, high_at:] = time_in[1]
    ext[channels:, LANES:high_at] = rows(chan_in[0], chan_in[1])
    ext[channels:, :LANES] = rows(corner_in[0], corner_in[2])
    ext[channels:, high_at:] = rows(corner_in[1], corner_in[3])
    power = jnp.zeros((channels, WIN), jnp.float32)
    for w in range(frames):
        block = ext[:, w * WIN : w * WIN + depth]
        got = lax.dot_general(block, fir_t, (((1,), (1,)), ((), ())), preferred_element_type=jnp.float32)
        slot = w % 2
        filt[slot, 8 : 8 + channels] = got[:channels]
        filt[slot, 8 - side : 8] = got[channels : channels + side]
        filt[slot, 8 + channels : 8 + channels + side] = got[channels + side : channels + 2 * side]
        shaped = sp_ref[0] * filt[slot, 8 - side : 8 - side + channels]
        for m in range(1, 2 * side + 1):
            shaped += sp_ref[m] * filt[slot, 8 - side + m : 8 - side + m + channels]
        spectra = jnp.dot(shaped.astype(jnp.bfloat16), table_ref[...], preferred_element_type=jnp.float32)
        spec[w] = spectra
        power += spectra * spectra
    level = jnp.dot(power, near, precision=HIGHEST, preferred_element_type=jnp.float32)
    level = level / (count.astype(jnp.float32) * frames)
    factor = taper_row(edges_ref) / jnp.sqrt(level + 1e-06)
    for w in range(frames):
        white_ref[w] = (spec[w] * factor).astype(jnp.bfloat16)
    half = WIN // 2
    part = channels // n_sub
    group = frames // SPLIT
    chunks = steps * SPLIT

    def up(c):
        return pltpu.make_async_remote_copy(
            src_ref=to_high.at[c], dst_ref=in_low.at[c], send_sem=sem_high.at[c], recv_sem=got_low.at[c],
            device_id={"chan": lax.rem(me + 1, n_chan)}, device_id_type=MESH)

    def down(c):
        return pltpu.make_async_remote_copy(
            src_ref=to_low.at[c], dst_ref=in_high.at[c], send_sem=sem_low.at[c], recv_sem=got_high.at[c],
            device_id={"chan": lax.rem(me + n_chan - 1, n_chan)}, device_id_type=MESH)

    def sub_copy(s, d):
        to = lax.rem(my_sub + d, n_sub)
        return pltpu.make_async_remote_copy(
            src_ref=own_lag.at[s, pl.ds(to * part, part)], dst_ref=sub_in.at[s, d - 1],
            send_sem=sub_send.at[s, d - 1], recv_sem=sub_recv.at[s, d - 1],
            device_id={"sub": to}, device_id_type=MESH)

    def tm_copy(s, d):
        return pltpu.make_async_remote_copy(
            src_ref=tm_in.at[s, my_tm], dst_ref=tm_in.at[s, my_tm],
            send_sem=tm_send.at[s, d - 1], recv_sem=tm_recv.at[s, d - 1],
            device_id={"tm": lax.rem(my_tm + d, n_tm)}, device_id_type=MESH)

    def fin_copy(s, d):
        here = pl.ds(my_sub * part, part)
        return pltpu.make_async_remote_copy(
            src_ref=done.at[s, here], dst_ref=done.at[s, here],
            send_sem=fin_send.at[s, d - 1], recv_sem=fin_recv.at[s, d - 1],
            device_id={"sub": lax.rem(my_sub + d, n_sub)}, device_id_type=MESH)

    def own_panel(s):
        panel = jnp.full((P_SIZE, WIN), panel_ref[s], jnp.int32)
        for w in range(frames):
            value = white_ref[w, :P_SIZE]
            for k in range(1, channels // P_SIZE):
                value = jnp.where(panel == k, white_ref[w, k * P_SIZE : (k + 1) * P_SIZE], value)
            own_ref[s, w] = value

    def stage(c, arrived, leaving):
        s = lax.div(c, SPLIT)
        k = lax.rem(c, SPLIT)
        mine = jnp.full((P_SIZE, WIN), owner_ref[s], jnp.int32) == me
        for w in range(group):
            leaving[c, w] = jnp.where(mine, own_ref[s, k * group + w], arrived[c, w])

    def relay(t):
        c = t - LAG * me

        @pl.when((c >= 0) & (c < chunks))
        def _():
            @pl.when(me > 0)
            def _():
                up(c).wait_recv()

            @pl.when(me < n_chan - 1)
            def _():
                stage(c, in_low, to_high)
                up(c).start()

        e = t - LAG * (n_chan - 1 - me)

        @pl.when((e >= 0) & (e < chunks))
        def _():
            @pl.when(me < n_chan - 1)
            def _():
                down(e).wait_recv()

            @pl.when(me > 0)
            def _():
                stage(e, in_high, to_low)
                down(e).start()

    def compute(s):
        rows = channels // 2
        owner = owner_ref[s]
        where = jnp.full((P_SIZE, WIN), owner, jnp.int32)
        start = owner * channels + panel_ref[s] * P_SIZE
        for r in range(2):
            here = slice(r * rows, (r + 1) * rows)
            acc_p = jnp.zeros((rows, WIN), jnp.float32)
            acc_q = jnp.zeros((rows, WIN), jnp.float32)
            for w in range(frames):
                c = s * SPLIT + w // group
                value = jnp.where(where < me, in_low[c, w % group], in_high[c, w % group])
                value = jnp.where(where == me, own_ref[s, w], value)
                partner = jnp.dot(chosen[s, here], value, preferred_element_type=jnp.float32)
                acc_p += plain[w, here] * partner
                acc_q += swapped[w, here] * partner
            lagged = jnp.dot(acc_p, lag_ref[:WIN], precision=HIGHEST, preferred_element_type=jnp.float32)
            lagged += jnp.dot(acc_q, lag_ref[WIN:], precision=HIGHEST, preferred_element_type=jnp.float32)
            receiver = me * channels + r * rows + lax.broadcasted_iota(jnp.int32, (rows, LAGS), 0)
            far = jnp.abs(receiver - (start + pick_wide[s, here])) > REACH
            own_lag[s, here] = jnp.where(far, 0.0, lagged)
        for d in range(1, n_sub):
            sub_copy(s, d).start()

    def sub_sum(s):
        total = own_lag[s, pl.ds(my_sub * part, part)]
        for d in range(1, n_sub):
            sub_copy(s, d).wait_recv()
            total += sub_in[s, d - 1]
        tm_in[s, my_tm] = total
        for d in range(1, n_tm):
            tm_copy(s, d).start()

    def tm_sum(s):
        for d in range(1, n_tm):
            tm_copy(s, d).wait_recv()
        total = tm_in[s, 0]
        for k in range(1, n_tm):
            total += tm_in[s, k]
        done[s, pl.ds(my_sub * part, part)] = total
        for d in range(1, n_sub):
            fin_copy(s, d).start()

    def finish(s):
        for d in range(1, n_sub):
            fin_copy(s, d).wait_recv()
        out_ref[s] = done[s]

    delay = -(-(n_chan - 1) * LAG // SPLIT)

    def turn(u, carry):
        pl.when(u < steps)(functools.partial(own_panel, u))
        for k in range(SPLIT):
            relay(u * SPLIT + k)

        @pl.when(u == 0)
        def _():
            for w in range(frames):
                value = white_ref[w].astype(jnp.float32)
                plain[w] = value
                for h in range(2):
                    swapped[w, :, h * half : (h + 1) * half] = pltpu.roll(
                        value[:, h * half : (h + 1) * half], half // 2, 1)

        for late, work in enumerate((compute, sub_sum, tm_sum, finish)):
            s = u - delay - late
            pl.when((s >= 0) & (s < steps))(functools.partial(work, s))
        return carry

    lax.fori_loop(0, steps + delay + 3, turn, 0)

    def drain_chunk(c, carry):
        @pl.when(me < n_chan - 1)
        def _():
            up(c).wait_send()

        @pl.when(me > 0)
        def _():
            down(c).wait_send()
        return carry

    lax.fori_loop(0, chunks, drain_chunk, 0)
    for k, move in enumerate(moves):
        pl.when(exists(*move))(lambda k=k: copy(k).wait_send())

    def drain_step(s, carry):
        for d in range(1, n_sub):
            sub_copy(s, d).wait_send()
            fin_copy(s, d).wait_send()
        for d in range(1, n_tm):
            tm_copy(s, d).wait_send()
        return carry

    lax.fori_loop(0, steps, drain_step, 0)


def lag_pair(scale):
    bins, parts = column_maps()
    lag = np.arange(LAGS) - LAGS // 2
    angle = 2.0 * np.pi * ((bins[:, None] * lag[None, :]) % WIN) / WIN
    real = np.cos(angle) * scale
    imag = np.where(parts[:, None] == 0, np.sin(angle), -np.sin(angle)) * scale
    full = np.concatenate([real, imag]).astype(np.float32)
    high = jnp.asarray(full).astype(jnp.bfloat16)
    low = (jnp.asarray(full) - high.astype(jnp.float32)).astype(jnp.bfloat16)
    return jnp.concatenate([high, low], axis=1)


GROUP = 4
AHEAD = 1


def split_kernel(frames, channels, side, steps, n_chan, n_tm, n_sub, sp_hbm, edges_hbm, owner_hbm, panel_hbm,
                 taps_hbm, pick_hbm, raw_hbm, table_hbm, lag_hbm, out_hbm,
                 sp_ref, edges_ref, owner_ref, panel_ref, taps_ref, pick_ref, raw_ref, table_ref, lag_ref,
                 spec, mixed, halo_ext, halo_win, ends_ref, rim_ref, power_ref,
                 time_in, chan_out, chan_in, corner_out, corner_in, white_ref, picks, chosen, pan, acc,
                 own_lag, sub_out, sub_in, z_out, z_in, done,
                 load_sem, halo_send, halo_recv, far_sem, pick_send, pick_recv, z_send, z_recv, x_send, x_recv,
                 sub_send, sub_recv, r_send, r_recv, a_send, a_recv, out_sem, *white_in):
    f32, bf16 = jnp.float32, jnp.bfloat16
    me, my_tm, my_sub = lax.axis_index("chan"), lax.axis_index("tm"), lax.axis_index("sub")
    n_time = n_tm * n_sub
    now = my_tm * n_sub + my_sub
    samples = frames * WIN
    n_taps = taps_ref.shape[0]
    depth = WIN + 2 * LANES
    panels = channels // P_SIZE
    per = frames // n_chan
    spd = steps // n_time
    spt = spd * n_sub
    mine, theirs = white_in[:per], white_in[per:]
    loads = [
        pltpu.make_async_copy(source, target, load_sem.at[k])
        for k, (source, target) in enumerate([
            (raw_hbm, raw_ref), (taps_hbm, taps_ref), (pick_hbm, pick_ref), (sp_hbm, sp_ref),
            (edges_hbm, edges_ref), (owner_hbm, owner_ref), (panel_hbm, panel_ref),
            (table_hbm, table_ref), (lag_hbm, lag_ref),
        ])
    ]
    for load in loads[1:] + loads[:1]:
        load.start()

    def at_time(dt):
        at = lax.rem(now + dt + n_time, n_time)
        return {"tm": lax.div(at, n_sub), "sub": lax.rem(at, n_sub)}

    def peer(dc, dt):
        return {"chan": lax.rem(me + dc + n_chan, n_chan), **at_time(dt)}

    def exists(dc, dt):
        return (me + dc >= 0) & (me + dc < n_chan) & (now + dt >= 0) & (now + dt < n_time)

    moves = [(0, 1), (0, -1), (1, 0), (-1, 0), (1, 1), (1, -1), (-1, 1), (-1, -1)]
    barrier = pltpu.get_barrier_semaphore()
    for dt in range(1, n_time):
        pl.semaphore_signal(barrier, inc=1, device_id=at_time(dt), device_id_type=MESH)
    for move in moves[2:]:
        @pl.when(exists(*move))
        def _(move=move):
            pl.semaphore_signal(barrier, inc=1, device_id=peer(*move), device_id_type=MESH)

    for load in loads[1:]:
        load.wait()
    taps = taps_ref[...].astype(f32).reshape(1, n_taps)
    taps = jnp.concatenate([taps, jnp.zeros((1, depth - n_taps), f32)], axis=1)
    shift = LANES - (n_taps - 1) // 2
    rolled = pltpu.roll(jnp.broadcast_to(taps, (WIN, depth)), shift, 1, stride=1, stride_axis=0)
    fir_w = jnp.transpose(rolled).astype(bf16)
    parts = [fir_w[LANES : LANES + WIN]] * 2 + [fir_w[:LANES], fir_w[LANES + WIN :]] * 2
    fir_pair = jnp.concatenate(parts, axis=0)
    near = (jnp.abs(bins_of((WIN, WIN), 0) - bins_of((WIN, WIN), 1)) <= 4).astype(bf16)
    row_bins = bins_of((1, WIN), 1)
    count = jnp.minimum(row_bins + 4, WIN // 2 - 1) - jnp.maximum(row_bins - 4, 0) + 1
    taper = taper_row(edges_ref)

    def fir(block, first=0, last=depth):
        return jnp.dot(block, fir_w[first:last], preferred_element_type=f32)

    def taps_at(offset):
        total = jnp.zeros(offset.shape, f32)
        for m in range(2 * side + 1):
            total = jnp.where(offset == m - side, sp_ref[m], total)
        return total

    def two(value):
        high = value.astype(bf16)
        return high, (value - high.astype(f32)).astype(bf16)

    def across(matrix, value):
        m_high, m_low = matrix
        v_high, v_low = two(value)
        left = jnp.concatenate([m_high, m_low, m_high], axis=1)
        right = jnp.concatenate([v_high, v_high, v_low], axis=0)
        return jnp.dot(left, right, preferred_element_type=f32)

    def iota(shape, axis):
        return lax.broadcasted_iota(jnp.int32, shape, axis)

    square = (channels, channels)
    spatial = two(taps_at(iota(square, 1) - iota(square, 0)))
    rim = channels - 16
    stacked = jnp.concatenate(spatial, axis=0)
    row, column = iota((16, frames * 16), 0), iota((16, frames * 16), 1)
    row_channel = jnp.where(row < 8, row, row + rim)
    spot = lax.rem(column, 16)
    column_channel = jnp.where(spot < side, spot - side, jnp.where(spot < 2 * side, channels + spot - side, 4 * channels))
    base = taps_at(column_channel - row_channel)
    frame_of = lax.div(column, 16)
    rim_matrix = two(jnp.concatenate([jnp.where(frame_of == w, base, 0.0) for w in range(frames)], axis=0))
    for k in range(2):
        for at in (0, frames + 1):
            mixed[k, at] = jnp.zeros((channels, WIN), bf16)
    loads[0].wait()
    ends = (slice(channels - side, channels), slice(0, side))
    sides = (slice(samples - LANES, samples), slice(0, LANES))
    for k in range(2):
        chan_out[k] = raw_ref[ends[k]]
        for h in range(2):
            corner_out[2 * k + h] = raw_ref[ends[k], sides[h]]

    def copy(k):
        dc, dt = moves[k]
        if k < 2:
            src, dst = raw_ref.at[:, sides[k]], time_in.at[k]
        elif k < 4:
            src, dst = chan_out.at[k - 2], chan_in.at[k - 2]
        else:
            src, dst = corner_out.at[k - 4], corner_in.at[k - 4]
        return pltpu.make_async_remote_copy(
            src_ref=src, dst_ref=dst, send_sem=halo_send.at[k], recv_sem=halo_recv.at[k],
            device_id=peer(dc, dt), device_id_type=MESH)

    greeted = sum(exists(*move).astype(jnp.int32) for move in moves[2:])
    pl.semaphore_wait(barrier, n_time - 1 + greeted)
    for k in (2, 3, 0, 1, 4, 5, 6, 7):
        pl.when(exists(*moves[k]))(lambda k=k: copy(k).start())

    inner = (me > 0) & (me < n_chan - 1)

    def token(way):
        pl.semaphore_signal(far_sem.at[way], inc=1, device_id={"chan": me + 1 - 2 * way}, device_id_type=MESH)

    def relay_tokens(k):
        for way, distance in ((0, me), (1, n_chan - 1 - me)):
            @pl.when(distance >= k + 1)
            def _():
                pl.semaphore_wait(far_sem.at[way], 1)
            pl.when((distance >= k + 1) & inner)(lambda: token(way))

    for way in range(2):
        pl.when(inner)(lambda: token(way))

    def pick_copy(d):
        return pltpu.make_async_remote_copy(
            src_ref=pick_ref, dst_ref=picks.at[me], send_sem=pick_send.at[0], recv_sem=pick_recv.at[0],
            device_id={"chan": lax.rem(me + d, n_chan)}, device_id_type=MESH)

    def pick_all():
        rest = picks.at[pl.ds(0, n_chan - 1)]
        return pltpu.make_async_remote_copy(
            src_ref=rest, dst_ref=rest, send_sem=pick_send.at[0], recv_sem=pick_recv.at[0],
            device_id={"chan": lax.rem(me + 1, n_chan)}, device_id_type=MESH)

    for w in range(frames):
        got = jnp.dot(stacked, raw_ref[:, w * WIN : (w + 1) * WIN], preferred_element_type=f32)
        mixed[0, w + 1], mixed[1, w + 1] = two(got[:channels] + got[channels:])

    def filtered(g):
        sides = []
        for k in range(2):
            sides.append(mixed[k, g + 1 : g + 1 + GROUP])
        for k in range(2):
            sides += [mixed[k, g : g + GROUP, :, WIN - LANES :], mixed[k, g + 2 : g + 2 + GROUP, :, :LANES]]
        windows = jnp.concatenate(sides, axis=2).reshape(GROUP * channels, 2 * depth)
        return jnp.dot(windows, fir_pair, preferred_element_type=f32)

    power = jnp.zeros((channels, WIN), f32)
    ready = filtered(0)
    for g in range(0, frames, GROUP):
        part, ready = ready, filtered(g + GROUP) if g + GROUP < frames else None
        spectra = jnp.dot(part.astype(bf16), table_ref[...], preferred_element_type=f32)
        part, spectra = part.reshape(GROUP, channels, WIN), spectra.reshape(GROUP, channels, WIN)
        for k in range(GROUP):
            w = g + k
            if w in (0, frames - 1):
                ends_ref[min(w, 1)] = part[k]
                continue
            rim_ref[w, :8] = part[k, :8]
            rim_ref[w, 8:] = part[k, channels - 8 :]
            spec[w] = spectra[k]
            power += spectra[k] * spectra[k]
    power_ref[...] = power
    relay_tokens(1)

    for k, (dc, dt) in enumerate(moves):
        there = exists(-dc, -dt)
        pl.when(there)(lambda k=k: copy(k).wait_recv())
        buf, slot = (time_in, k) if k < 2 else (chan_in, k - 2) if k < 4 else (corner_in, k - 4)

        @pl.when(jnp.logical_not(there))
        def _():
            buf[slot] = jnp.zeros(buf.shape[1:], buf.dtype)

    def rows(low, high):
        width = low.shape[1]
        spare = jnp.zeros((16 - 2 * side, width), f32)
        both = [low.astype(f32), high.astype(f32), spare]
        return jnp.concatenate(both, axis=0).astype(bf16)

    halo_ext[:, LANES : LANES + samples] = rows(chan_in[0], chan_in[1])
    halo_ext[:, :LANES] = rows(corner_in[0], corner_in[2])
    halo_ext[:, LANES + samples :] = rows(corner_in[1], corner_in[3])
    for w in range(frames):
        halo_win[w] = halo_ext[:, w * WIN : w * WIN + depth]
    halo = fir(halo_win[...].reshape(frames * 16, depth))
    late = [fir(time_in[k], k * (depth - LANES), k * (depth - LANES) + LANES) for k in range(2)]
    rim_part = across(rim_matrix, halo).reshape(frames, 16, WIN)
    late = [across(spatial, value) for value in late]
    blocks = [rim_ref[1 : frames - 1] + rim_part[1 : frames - 1]]
    blocks[0] = blocks[0].reshape((frames - 2) * 16, WIN)
    for k, w in enumerate((0, frames - 1)):
        whole = ends_ref[k] + late[k]
        blocks += [whole[:8] + rim_part[w, :8], whole[8 : channels - 8], whole[channels - 8 :] + rim_part[w, 8:]]
    shaped = jnp.concatenate(blocks, axis=0).astype(bf16)
    spectra = jnp.dot(shaped, table_ref[...], preferred_element_type=f32)
    rims, whole = spectra[: (frames - 2) * 16].reshape(frames - 2, 16, WIN), spectra[(frames - 2) * 16 :]
    whole = whole.reshape(2, channels, WIN)
    for w in range(1, frames - 1):
        spec[w, :8] = rims[w - 1, :8]
        spec[w, channels - 8 :] = rims[w - 1, 8:]
    for k, w in enumerate((0, frames - 1)):
        spec[w] = whole[k]
    rims = jnp.sum(rims * rims, axis=0)
    inside = power_ref[8 : channels - 8]
    power = jnp.concatenate([rims[:8], inside, rims[8:]], axis=0) + jnp.sum(whole * whole, axis=0)
    for k in range(2, n_chan - 1):
        relay_tokens(k)
    for d in range(1, n_chan):
        pick_copy(d).start()
    level = jnp.dot(
        jnp.concatenate(two(power), axis=1), jnp.concatenate([near, near], axis=0), preferred_element_type=f32)
    level = level / (count.astype(f32) * frames)
    factor = taper / jnp.sqrt(level + 1e-06)

    def whiten(w):
        return (spec[w] * factor).astype(bf16).reshape(panels, P_SIZE, WIN)

    def block_of(q):
        return pl.ds(q * panels, panels)

    def z_copy(j, d):
        to = lax.rem(me + d, n_chan)
        return pltpu.make_async_remote_copy(
            src_ref=white_ref.at[to * per + j], dst_ref=mine[j].at[block_of(me)],
            send_sem=z_send.at[j % AHEAD, d - 1], recv_sem=z_recv.at[j, d - 1],
            device_id={"chan": to}, device_id_type=MESH)

    def x_copy(j, e, k):
        at = slice(None) if e is None else block_of(lax.rem(me - e + n_chan, n_chan))
        return pltpu.make_async_remote_copy(
            src_ref=mine[j].at[at], dst_ref=theirs[j].at[k - 1, at],
            send_sem=x_send.at[j, k - 1], recv_sem=x_recv.at[j, k - 1],
            device_id={"tm": lax.rem(my_tm + k, n_tm)}, device_id_type=MESH)

    near_first = sorted(range(1, n_chan), key=lambda d: (min(d, n_chan - d), d))
    far_first = near_first[::-1]
    for j in range(per):
        for d in far_first:
            w = lax.rem(me + d, n_chan) * per + j
            white_ref[w] = whiten(w)
            if j < AHEAD:
                z_copy(j, d).start()
        mine[j][block_of(me)] = whiten(me * per + j)
        for k in range(1, n_tm):
            x_copy(j, 0, k).start()
    def choose():
        picks[me] = pick_ref[...]
        pick_all().wait_recv()
        for i in range(spt):
            for q in range(n_chan):
                pick = jnp.broadcast_to(picks[q, pl.ds(my_tm * spt + i, 1)], (P_SIZE, channels))
                hit = (pick == iota((P_SIZE, channels), 0)).astype(f32)
                chosen[i, q * channels : (q + 1) * channels] = jnp.transpose(hit).astype(bf16)

    half = WIN // 2

    def source(unit):
        j, k = unit
        return mine[j] if k == 0 else theirs[j].at[k - 1]

    def gather(units):
        for i in range(spt):
            s = my_tm * spt + i
            at = owner_ref[s] * panels + panel_ref[s]
            for u, unit in enumerate(units):
                value = source(unit)[at]
                wide = value.astype(f32)
                turn = [pltpu.roll(wide[:, h * half : (h + 1) * half], half // 2, 1) for h in range(2)]
                pan[i, u, :, :WIN] = value
                pan[i, u, :, WIN:] = jnp.concatenate(turn, axis=1).astype(bf16)

    everyone = n_chan * channels

    def receivers(unit):
        return source(unit)[...].reshape(everyone, WIN).astype(f32)

    def products(units, i, values):
        p = q = None
        for u, value in enumerate(values):
            partner = jnp.dot(chosen[i], pan[i, u], preferred_element_type=f32)
            dp, dq = value * partner[:, :WIN], value * partner[:, WIN:]
            p, q = (dp, dq) if u == 0 else (p + dp, q + dq)
        return p, q

    def accumulate(units, first):
        gather(units)
        values = [receivers(unit) for unit in units]

        def step(i, carry):
            p, q = products(units, i, values)
            if not first:
                p += acc[i, 0]
                q += acc[i, 1]
            acc[i, 0] = p
            acc[i, 1] = q
            return carry

        for i in range(spt):
            step(i, 0)

    def forward(j):
        for d in near_first:
            z_copy(j, d).wait_send()
            if j + AHEAD < per:
                z_copy(j + AHEAD, d).start()
            z_copy(j, d).wait_recv()
            for k in range(1, n_tm):
                x_copy(j, d, k).start()

    def arrive(j):
        for k in range(1, n_tm):
            x_copy(j, None, k).wait_recv()

    def others(j):
        return [(j, k) for k in range(1, n_tm)]

    last = per - 1
    for j in range(per):
        forward(j)
        if j == 0:
            choose()
        units = [(j, 0)]
        if j > 0:
            arrive(j - 1)
            units += others(j - 1)
        accumulate(units, j == 0)
    arrive(last)
    gather(others(last))

    def summed_products(i):
        p, q = products(others(last), i, [receivers(unit) for unit in others(last)])
        return (p + acc[i, 0]).astype(bf16), (q + acc[i, 1]).astype(bf16)

    def lagged(both):
        lags = jnp.dot(both[0], lag_ref[:WIN], preferred_element_type=f32)
        lags += jnp.dot(both[1], lag_ref[WIN:], preferred_element_type=f32)
        return lags[:, :LAGS] + lags[:, LAGS:]

    def sub_copy(k, d):
        to = lax.rem(my_sub + d, n_sub)
        return pltpu.make_async_remote_copy(
            src_ref=sub_out.at[k, d - 1], dst_ref=sub_in.at[k, d - 1],
            send_sem=sub_send.at[k, d - 1], recv_sem=sub_recv.at[k, d - 1],
            device_id={"sub": to}, device_id_type=MESH)

    def r_copy(k, d):
        to = lax.rem(me + d, n_chan)
        return pltpu.make_async_remote_copy(
            src_ref=z_out.at[k, d - 1], dst_ref=z_in.at[k, d - 1], send_sem=r_send.at[k], recv_sem=r_recv.at[k],
            device_id={"chan": to}, device_id_type=MESH)

    def r_all(k):
        return pltpu.make_async_remote_copy(
            src_ref=z_out.at[k], dst_ref=z_in.at[k], send_sem=r_send.at[k], recv_sem=r_recv.at[k],
            device_id={"chan": lax.rem(me + 1, n_chan)}, device_id_type=MESH)

    def a_copy(k, d):
        return pltpu.make_async_remote_copy(
            src_ref=done.at[k], dst_ref=out_hbm.at[now * spd + k], send_sem=a_send.at[k], recv_sem=a_recv.at[k],
            device_id=at_time(d), device_id_type=MESH)

    def a_all(k):
        rest = out_hbm.at[pl.ds(0, n_time - 1)]
        return pltpu.make_async_remote_copy(
            src_ref=rest, dst_ref=rest, send_sem=a_send.at[k], recv_sem=a_recv.at[k],
            device_id=at_time(1), device_id_type=MESH)

    def store(k):
        return pltpu.make_async_copy(done.at[k], out_hbm.at[now * spd + k], out_sem.at[k])

    work = [(d, k) for d in [*range(1, n_sub), 0] for k in range(spd)]

    def at_step(d, k):
        return lax.rem(my_sub + d, n_sub) * spd + k

    kept = []
    coming = summed_products(at_step(*work[0]))
    for n, (d, k) in enumerate(work):
        current, coming = coming, summed_products(at_step(*work[n + 1])) if n + 1 < len(work) else None
        lags = lagged(current)
        if d > 0:
            sub_out[k, d - 1] = lags.astype(bf16)
            sub_copy(k, d).start()
            continue
        own_lag[k] = lags
        for other in range(1, n_sub):
            sub_copy(k, other).wait_recv()

        def summed(q, k=k):
            here = pl.ds(q * channels, channels)
            value = own_lag[k, here]
            for other in range(1, n_sub):
                value += sub_in[k, other - 1, here].astype(f32)
            return value

        for way in far_first:
            z_out[k, way - 1] = summed(lax.rem(me + way, n_chan)).astype(bf16)
            r_copy(k, way).start()
        kept.append(summed(me))
    picked = []
    for k in range(spd):
        pick = jnp.broadcast_to(pick_ref[pl.ds(now * spd + k, 1)], (LAGS, channels))
        picked.append(jnp.transpose(pick.astype(f32)).astype(jnp.int32))
    receiver = me * channels + lax.broadcasted_iota(jnp.int32, (channels, LAGS), 0)
    for k in range(spd):
        s = now * spd + k
        value = kept[k]
        r_all(k).wait_recv()
        for d in range(1, n_chan):
            value += z_in[k, d - 1].astype(f32)
        start = owner_ref[s] * channels + panel_ref[s] * P_SIZE
        far = jnp.abs(receiver - (start + picked[k])) > REACH
        done[k] = jnp.where(far, 0.0, value).astype(bf16)
        for d in range(1, n_time):
            a_copy(k, d).start()
        store(k).start()
    for k in range(spd):
        if n_time > 1:
            a_all(k).wait_recv()
    for k, move in enumerate(moves):
        pl.when(exists(*move))(lambda k=k: copy(k).wait_send())
    pick_all().wait_send()
    for k in range(1, n_tm):
        for j in range(per):
            x_copy(j, None, k).wait_send()
    for k in range(spd):
        for d in range(1, n_sub):
            sub_copy(k, d).wait_send()
        r_all(k).wait_send()
        if n_time > 1:
            a_all(k).wait_send()
    for k in range(spd):
        store(k).wait()


VMEM = pl.BlockSpec(memory_space=pltpu.VMEM)


def relay(raw, fir_taps, spatial_taps, band_edges, source_owner, source_panel, source_pick):
    channels, samples = raw.shape
    margin = (fir_taps.shape[0] - 1) // 2
    side = spatial_taps.shape[0] // 2
    frames = samples // WIN
    steps = source_owner.shape[0]
    times = ("tm", "sub")
    count = lax.axis_size(times)
    n_chan = lax.axis_size("chan")
    n_tm, n_sub = lax.axis_size("tm"), lax.axis_size("sub")
    depth = WIN + 2 * LANES
    first = LANES - margin
    taps = jnp.pad(fir_taps.astype(jnp.float32), (first, depth - first - fir_taps.shape[0]))[None, :]
    total = frames * n_tm * n_sub
    lag_table = lag_tables(1.0 / math.sqrt(total * (WIN // 2)))
    chunks = steps * SPLIT
    flow = pltpu.VMEM((chunks, frames // SPLIT, P_SIZE, WIN), jnp.bfloat16)
    part = channels // n_sub
    dma = pltpu.SemaphoreType.DMA
    any_space = pl.BlockSpec(memory_space=pltpu.HBM)
    bf16, f32 = jnp.bfloat16, jnp.float32
    return pl.pallas_call(
        functools.partial(relay_kernel, frames, channels, side, steps, n_chan, n_tm, n_sub),
        out_shape=jax.ShapeDtypeStruct((steps, channels, LAGS), f32),
        in_specs=[any_space] * 9,
        out_specs=VMEM,
        scratch_shapes=[
            pltpu.SMEM(spatial_taps.shape, f32),
            pltpu.SMEM(band_edges.shape, jnp.int32),
            pltpu.SMEM(source_owner.shape, jnp.int32),
            pltpu.SMEM(source_panel.shape, jnp.int32),
            pltpu.VMEM(taps.shape, f32),
            pltpu.VMEM(source_pick.shape, jnp.int32),
            pltpu.VMEM(raw.shape, bf16),
            pltpu.VMEM((WIN, WIN), bf16),
            pltpu.VMEM((2 * WIN, LAGS), f32),
            pltpu.VMEM((2, channels + 16, WIN), f32),
            pltpu.VMEM((frames, channels, WIN), f32),
            pltpu.VMEM((channels + 16, samples + 2 * LANES), bf16),
            pltpu.VMEM((2, channels, LANES), bf16),
            pltpu.VMEM((2, side, samples), bf16),
            pltpu.VMEM((2, side, samples), bf16),
            pltpu.VMEM((4, side, LANES), bf16),
            pltpu.VMEM((4, side, LANES), bf16),
            dma((8,)), dma((8,)), dma((9,)),
            pltpu.VMEM((frames, channels, WIN), bf16),
            pltpu.VMEM((steps, frames, P_SIZE, WIN), bf16),
            pltpu.VMEM((steps, channels, P_SIZE), bf16),
            pltpu.VMEM((steps, channels, LANES), jnp.int32),
            pltpu.VMEM((frames, channels, WIN), f32),
            pltpu.VMEM((frames, channels, WIN), f32),
            flow, flow, flow, flow,
            pltpu.VMEM((steps, channels, LAGS), f32),
            pltpu.VMEM((steps, n_sub - 1, part, LAGS), f32),
            pltpu.VMEM((steps, n_tm, part, LAGS), f32),
            pltpu.VMEM((steps, channels, LAGS), f32),
            dma((chunks,)), dma((chunks,)), dma((chunks,)), dma((chunks,)),
            dma((steps, n_sub - 1)), dma((steps, n_sub - 1)),
            dma((steps, n_tm - 1)), dma((steps, n_tm - 1)),
            dma((steps, n_sub - 1)), dma((steps, n_sub - 1)),
        ],
        compiler_params=pltpu.CompilerParams(
            vmem_limit_bytes=64 * 2**20, collective_id=0, has_side_effects=True),
        name="correlate",
    )(spatial_taps, band_edges, source_owner, source_panel, taps, source_pick, raw, spectral_table(), lag_table)


def split(raw, fir_taps, spatial_taps, band_edges, source_owner, source_panel, source_pick):
    channels, samples = raw.shape
    side = spatial_taps.shape[0] // 2
    frames = samples // WIN
    steps = source_owner.shape[0]
    n_chan, n_tm, n_sub = lax.axis_size("chan"), lax.axis_size("tm"), lax.axis_size("sub")
    n_time = n_tm * n_sub
    depth = WIN + 2 * LANES
    lag_table = lag_pair(1.0 / math.sqrt(frames * n_time * (WIN // 2)))
    per, spd = frames // n_chan, steps // n_time
    spt = spd * n_sub
    panels, everyone = channels // P_SIZE, n_chan * channels
    dma, any_space = pltpu.SemaphoreType.DMA, pl.BlockSpec(memory_space=pltpu.HBM)
    bf16, f32 = jnp.bfloat16, jnp.float32
    return pl.pallas_call(
        functools.partial(split_kernel, frames, channels, side, steps, n_chan, n_tm, n_sub),
        out_shape=jax.ShapeDtypeStruct((steps, channels, LAGS), bf16),
        in_specs=[any_space] * 9,
        out_specs=any_space,
        scratch_shapes=[
            pltpu.SMEM(spatial_taps.shape, f32),
            pltpu.SMEM(band_edges.shape, jnp.int32),
            pltpu.SMEM(source_owner.shape, jnp.int32),
            pltpu.SMEM(source_panel.shape, jnp.int32),
            pltpu.VMEM(fir_taps.shape, bf16),
            pltpu.VMEM(source_pick.shape, jnp.int32),
            pltpu.VMEM(raw.shape, bf16),
            pltpu.VMEM((WIN, WIN), bf16),
            pltpu.VMEM(lag_table.shape, bf16),
            pltpu.VMEM((frames, channels, WIN), f32),
            pltpu.VMEM((2, frames + 2, channels, WIN), bf16),
            pltpu.VMEM((16, samples + 2 * LANES), bf16),
            pltpu.VMEM((frames, 16, depth), bf16),
            pltpu.VMEM((2, channels, WIN), f32),
            pltpu.VMEM((frames, 16, WIN), f32),
            pltpu.VMEM((channels, WIN), f32),
            pltpu.VMEM((2, channels, LANES), bf16),
            pltpu.VMEM((2, side, samples), bf16),
            pltpu.VMEM((2, side, samples), bf16),
            pltpu.VMEM((4, side, LANES), bf16),
            pltpu.VMEM((4, side, LANES), bf16),
            pltpu.VMEM((frames, panels, P_SIZE, WIN), bf16),
            pltpu.VMEM((n_chan, *source_pick.shape), jnp.int32),
            pltpu.VMEM((spt, everyone, P_SIZE), bf16),
            pltpu.VMEM((spt, n_tm, P_SIZE, 2 * WIN), bf16),
            pltpu.VMEM((spt, 2, everyone, WIN), f32),
            pltpu.VMEM((spd, everyone, LAGS), f32),
            pltpu.VMEM((spd, max(n_sub - 1, 1), everyone, LAGS), bf16),
            pltpu.VMEM((spd, max(n_sub - 1, 1), everyone, LAGS), bf16),
            pltpu.VMEM((spd, n_chan - 1, channels, LAGS), bf16),
            pltpu.VMEM((spd, n_chan - 1, channels, LAGS), bf16),
            pltpu.VMEM((spd, channels, LAGS), bf16),
            dma((9,)), dma((8,)), dma((8,)), pltpu.SemaphoreType.REGULAR((2,)),
            dma((1,)), dma((1,)), dma((AHEAD, n_chan - 1)), dma((per, n_chan - 1)),
            dma((per, max(n_tm - 1, 1))), dma((per, max(n_tm - 1, 1))),
            dma((spd, max(n_sub - 1, 1))), dma((spd, max(n_sub - 1, 1))),
            dma((spd,)), dma((spd,)), dma((spd,)), dma((spd,)), dma((spd,)),
        ] + [pltpu.VMEM((n_chan * panels, P_SIZE, WIN), bf16)] * per
        + [pltpu.VMEM((max(n_tm - 1, 1), n_chan * panels, P_SIZE, WIN), bf16)] * per,
        compiler_params=pltpu.CompilerParams(
            vmem_limit_bytes=60 * 2**20, collective_id=0, has_side_effects=True),
        name="correlate",
    )(spatial_taps, band_edges, source_owner, source_panel, fir_taps, source_pick, raw, spectral_table(), lag_table).astype(f32)


def shards(*blocks):
    frames, steps = blocks[0].shape[1] // WIN, blocks[4].shape[0]
    chans = lax.axis_size("chan")
    even = chans > 1 and frames % chans == 0 and frames % GROUP == 0 and steps % lax.axis_size(("tm", "sub")) == 0
    return (split if even else relay)(*blocks)


def solution(mesh):
    placed = (
        P(("grp", "chan"), ("tm", "sub")),
        P(),
        P(),
        P(),
        P("grp"),
        P(),
        P(None, ("grp", "chan")),
    )
    return jax.shard_map(
        shards,
        mesh=mesh,
        in_specs=placed,
        out_specs=P(None, ("grp", "chan"), None),
        check_vma=False,
    )
```

```python
import functools
import math

import jax
import jax.numpy as jnp
import numpy as np
from jax import lax
from jax.experimental import pallas as pl
from jax.experimental.pallas import tpu as pltpu
from jax.sharding import PartitionSpec as P

P_SIZE = 32
WIN = 256
LAGS = 128
REACH = 1000
HIGHEST = lax.Precision.HIGHEST


def column_maps():
    column = np.arange(WIN)
    quarter = WIN // 4
    bins = column // (2 * quarter) * quarter + column % quarter
    parts = column // quarter % 2
    return bins, parts


def spectral_table():
    bins, parts = column_maps()
    angle = 2.0 * np.pi * ((bins[None, :] * np.arange(WIN)[:, None]) % WIN) / WIN
    table = np.where(parts == 0, np.cos(angle), -np.sin(angle)) / math.sqrt(WIN)
    return jnp.asarray(table.astype(np.float32)).astype(jnp.bfloat16)


def bins_of(shape, axis):
    column = lax.broadcasted_iota(jnp.int32, shape, axis)
    quarter = WIN // 4
    return lax.div(column, 2 * quarter) * quarter + lax.rem(column, quarter)


def lag_tables(scale):
    bins, parts = column_maps()
    lag = np.arange(LAGS) - LAGS // 2
    angle = 2.0 * np.pi * ((bins[:, None] * lag[None, :]) % WIN) / WIN
    real = np.cos(angle) * scale
    imag = np.where(parts[:, None] == 0, -np.sin(angle), np.sin(angle)) * scale
    return jnp.asarray(np.concatenate([real, imag]).astype(np.float32))


def taper_row(edges_ref):
    bins = bins_of((1, WIN), 1).astype(jnp.float32)
    e0, e1, e2, e3 = [jnp.full((1, WIN), edges_ref[k]).astype(jnp.float32) for k in range(4)]
    rising = 0.5 - 0.5 * jnp.cos(math.pi * (bins - e0) / (e1 - e0))
    falling = 0.5 - 0.5 * jnp.cos(math.pi * (e3 - bins) / (e3 - e2))
    inner = jnp.where(bins < e3, falling, 0.0)
    inner = jnp.where(bins <= e2, 1.0, inner)
    inner = jnp.where(bins < e1, rising, inner)
    return jnp.where(bins <= e0, 0.0, inner)


LANES = 128
SPLIT = 2
LAG = 2
MESH = pl.DeviceIdType.MESH


def relay_kernel(frames, channels, side, steps, n_chan, n_tm, n_sub, sp_hbm, edges_hbm, owner_hbm, panel_hbm,
           taps_hbm, pick_hbm, raw_hbm, table_hbm, lag_hbm, out_ref,
           sp_ref, edges_ref, owner_ref, panel_ref, taps_ref, pick_ref, raw_ref, table_ref, lag_ref, filt, spec, ext, time_in, chan_out, chan_in, corner_out, corner_in, send_sem,
           recv_sem, load_sem, white_ref, own_ref, chosen, pick_wide, plain, swapped, in_low, in_high, to_high,
           to_low, own_lag, sub_in, tm_in, done, sem_high, sem_low, got_low, got_high, sub_send, sub_recv,
           tm_send, tm_recv, fin_send, fin_recv):
    my_tm = lax.axis_index("tm")
    my_sub = lax.axis_index("sub")
    loads = [
        pltpu.make_async_copy(source, target, load_sem.at[k])
        for k, (source, target) in enumerate([
            (raw_hbm, raw_ref), (taps_hbm, taps_ref), (pick_hbm, pick_ref), (sp_hbm, sp_ref),
            (edges_hbm, edges_ref), (owner_hbm, owner_ref), (panel_hbm, panel_ref),
            (table_hbm, table_ref), (lag_hbm, lag_ref),
        ])
    ]
    for load in loads:
        load.start()
    me = lax.axis_index("chan")
    n_time = n_tm * n_sub
    now = lax.axis_index("tm") * n_sub + lax.axis_index("sub")
    samples = frames * WIN
    depth = taps_ref.shape[1]

    def peer(dc, dt):
        at = lax.rem(now + dt + n_time, n_time)
        return {"chan": lax.rem(me + dc + n_chan, n_chan), "tm": lax.div(at, n_sub), "sub": lax.rem(at, n_sub)}

    moves = [(0, 1), (0, -1), (1, 0), (-1, 0), (1, 1), (1, -1), (-1, 1), (-1, -1)]
    barrier = pltpu.get_barrier_semaphore()
    peers = [peer(dc, dt) for dc, dt in moves]
    peers += [{"tm": lax.rem(my_tm + d, n_tm)} for d in range(1, n_tm)]
    peers += [{"sub": lax.rem(my_sub + d, n_sub)} for d in range(1, n_sub)]
    for to in peers:
        pl.semaphore_signal(barrier, inc=1, device_id=to, device_id_type=MESH)

    loads[0].wait()
    ends = (slice(channels - side, channels), slice(0, side))
    sides = (slice(samples - LANES, samples), slice(0, LANES))
    for k in range(2):
        chan_out[k] = raw_ref[ends[k]]
        for h in range(2):
            corner_out[2 * k + h] = raw_ref[ends[k], sides[h]]

    def exists(dc, dt):
        return (me + dc >= 0) & (me + dc < n_chan) & (now + dt >= 0) & (now + dt < n_time)

    def copy(k):
        dc, dt = moves[k]
        if k < 2:
            src, dst = raw_ref.at[:, sides[k]], time_in.at[k]
        elif k < 4:
            src, dst = chan_out.at[k - 2], chan_in.at[k - 2]
        else:
            src, dst = corner_out.at[k - 4], corner_in.at[k - 4]
        return pltpu.make_async_remote_copy(
            src_ref=src, dst_ref=dst, send_sem=send_sem.at[k], recv_sem=recv_sem.at[k],
            device_id=peer(dc, dt), device_id_type=MESH)

    pl.semaphore_wait(barrier, len(peers))
    for k in (2, 3, 0, 1, 4, 5, 6, 7):
        pl.when(exists(*moves[k]))(lambda k=k: copy(k).start())

    ext[:channels, LANES : LANES + samples] = raw_ref[...]
    for load in loads[1:]:
        load.wait()
    rolled = pltpu.roll(jnp.broadcast_to(taps_ref[...], (WIN, depth)), 0, 1, stride=1, stride_axis=0)
    fir_t = rolled.astype(jnp.bfloat16)
    near = (jnp.abs(bins_of((WIN, WIN), 0) - bins_of((WIN, WIN), 1)) <= 4).astype(jnp.float32)
    row_bins = bins_of((1, WIN), 1)
    count = jnp.minimum(row_bins + 4, WIN // 2 - 1) - jnp.maximum(row_bins - 4, 0) + 1
    turned = jnp.transpose(pick_ref[...].astype(jnp.float32))
    for s in range(steps):
        wide = jnp.broadcast_to(turned[:, s : s + 1], (channels, LANES)).astype(jnp.int32)
        pick_wide[s] = wide
        chosen[s] = (
            wide[:, :P_SIZE] == lax.broadcasted_iota(jnp.int32, (channels, P_SIZE), 1)
        ).astype(jnp.bfloat16)

    @pl.when(me == 0)
    def _():
        in_low[...] = jnp.zeros_like(in_low)

    @pl.when(me == n_chan - 1)
    def _():
        in_high[...] = jnp.zeros_like(in_high)

    for k, (dc, dt) in enumerate(moves):
        there = exists(-dc, -dt)
        pl.when(there)(lambda k=k: copy(k).wait_recv())
        buf, slot = (time_in, k) if k < 2 else (chan_in, k - 2) if k < 4 else (corner_in, k - 4)

        @pl.when(jnp.logical_not(there))
        def _():
            buf[slot] = jnp.zeros(buf.shape[1:], buf.dtype)

    def rows(low, high):
        width = low.shape[1]
        spare = jnp.zeros((16 - 2 * side, width), jnp.float32)
        both = [low.astype(jnp.float32), high.astype(jnp.float32), spare]
        return jnp.concatenate(both, axis=0).astype(jnp.bfloat16)

    high_at = LANES + samples
    ext[:channels, :LANES] = time_in[0]
    ext[:channels, high_at:] = time_in[1]
    ext[channels:, LANES:high_at] = rows(chan_in[0], chan_in[1])
    ext[channels:, :LANES] = rows(corner_in[0], corner_in[2])
    ext[channels:, high_at:] = rows(corner_in[1], corner_in[3])
    power = jnp.zeros((channels, WIN), jnp.float32)
    for w in range(frames):
        block = ext[:, w * WIN : w * WIN + depth]
        got = lax.dot_general(block, fir_t, (((1,), (1,)), ((), ())), preferred_element_type=jnp.float32)
        slot = w % 2
        filt[slot, 8 : 8 + channels] = got[:channels]
        filt[slot, 8 - side : 8] = got[channels : channels + side]
        filt[slot, 8 + channels : 8 + channels + side] = got[channels + side : channels + 2 * side]
        shaped = sp_ref[0] * filt[slot, 8 - side : 8 - side + channels]
        for m in range(1, 2 * side + 1):
            shaped += sp_ref[m] * filt[slot, 8 - side + m : 8 - side + m + channels]
        spectra = jnp.dot(shaped.astype(jnp.bfloat16), table_ref[...], preferred_element_type=jnp.float32)
        spec[w] = spectra
        power += spectra * spectra
    level = jnp.dot(power, near, precision=HIGHEST, preferred_element_type=jnp.float32)
    level = level / (count.astype(jnp.float32) * frames)
    factor = taper_row(edges_ref) / jnp.sqrt(level + 1e-06)
    for w in range(frames):
        white_ref[w] = (spec[w] * factor).astype(jnp.bfloat16)
    half = WIN // 2
    part = channels // n_sub
    group = frames // SPLIT
    chunks = steps * SPLIT

    def up(c):
        return pltpu.make_async_remote_copy(
            src_ref=to_high.at[c], dst_ref=in_low.at[c], send_sem=sem_high.at[c], recv_sem=got_low.at[c],
            device_id={"chan": lax.rem(me + 1, n_chan)}, device_id_type=MESH)

    def down(c):
        return pltpu.make_async_remote_copy(
            src_ref=to_low.at[c], dst_ref=in_high.at[c], send_sem=sem_low.at[c], recv_sem=got_high.at[c],
            device_id={"chan": lax.rem(me + n_chan - 1, n_chan)}, device_id_type=MESH)

    def sub_copy(s, d):
        to = lax.rem(my_sub + d, n_sub)
        return pltpu.make_async_remote_copy(
            src_ref=own_lag.at[s, pl.ds(to * part, part)], dst_ref=sub_in.at[s, d - 1],
            send_sem=sub_send.at[s, d - 1], recv_sem=sub_recv.at[s, d - 1],
            device_id={"sub": to}, device_id_type=MESH)

    def tm_copy(s, d):
        return pltpu.make_async_remote_copy(
            src_ref=tm_in.at[s, my_tm], dst_ref=tm_in.at[s, my_tm],
            send_sem=tm_send.at[s, d - 1], recv_sem=tm_recv.at[s, d - 1],
            device_id={"tm": lax.rem(my_tm + d, n_tm)}, device_id_type=MESH)

    def fin_copy(s, d):
        here = pl.ds(my_sub * part, part)
        return pltpu.make_async_remote_copy(
            src_ref=done.at[s, here], dst_ref=done.at[s, here],
            send_sem=fin_send.at[s, d - 1], recv_sem=fin_recv.at[s, d - 1],
            device_id={"sub": lax.rem(my_sub + d, n_sub)}, device_id_type=MESH)

    def own_panel(s):
        panel = jnp.full((P_SIZE, WIN), panel_ref[s], jnp.int32)
        for w in range(frames):
            value = white_ref[w, :P_SIZE]
            for k in range(1, channels // P_SIZE):
                value = jnp.where(panel == k, white_ref[w, k * P_SIZE : (k + 1) * P_SIZE], value)
            own_ref[s, w] = value

    def stage(c, arrived, leaving):
        s = lax.div(c, SPLIT)
        k = lax.rem(c, SPLIT)
        mine = jnp.full((P_SIZE, WIN), owner_ref[s], jnp.int32) == me
        for w in range(group):
            leaving[c, w] = jnp.where(mine, own_ref[s, k * group + w], arrived[c, w])

    def relay(t):
        c = t - LAG * me

        @pl.when((c >= 0) & (c < chunks))
        def _():
            @pl.when(me > 0)
            def _():
                up(c).wait_recv()

            @pl.when(me < n_chan - 1)
            def _():
                stage(c, in_low, to_high)
                up(c).start()

        e = t - LAG * (n_chan - 1 - me)

        @pl.when((e >= 0) & (e < chunks))
        def _():
            @pl.when(me < n_chan - 1)
            def _():
                down(e).wait_recv()

            @pl.when(me > 0)
            def _():
                stage(e, in_high, to_low)
                down(e).start()

    def compute(s):
        rows = channels // 2
        owner = owner_ref[s]
        where = jnp.full((P_SIZE, WIN), owner, jnp.int32)
        start = owner * channels + panel_ref[s] * P_SIZE
        for r in range(2):
            here = slice(r * rows, (r + 1) * rows)
            acc_p = jnp.zeros((rows, WIN), jnp.float32)
            acc_q = jnp.zeros((rows, WIN), jnp.float32)
            for w in range(frames):
                c = s * SPLIT + w // group
                value = jnp.where(where < me, in_low[c, w % group], in_high[c, w % group])
                value = jnp.where(where == me, own_ref[s, w], value)
                partner = jnp.dot(chosen[s, here], value, preferred_element_type=jnp.float32)
                acc_p += plain[w, here] * partner
                acc_q += swapped[w, here] * partner
            lagged = jnp.dot(acc_p, lag_ref[:WIN], precision=HIGHEST, preferred_element_type=jnp.float32)
            lagged += jnp.dot(acc_q, lag_ref[WIN:], precision=HIGHEST, preferred_element_type=jnp.float32)
            receiver = me * channels + r * rows + lax.broadcasted_iota(jnp.int32, (rows, LAGS), 0)
            far = jnp.abs(receiver - (start + pick_wide[s, here])) > REACH
            own_lag[s, here] = jnp.where(far, 0.0, lagged)
        for d in range(1, n_sub):
            sub_copy(s, d).start()

    def sub_sum(s):
        total = own_lag[s, pl.ds(my_sub * part, part)]
        for d in range(1, n_sub):
            sub_copy(s, d).wait_recv()
            total += sub_in[s, d - 1]
        tm_in[s, my_tm] = total
        for d in range(1, n_tm):
            tm_copy(s, d).start()

    def tm_sum(s):
        for d in range(1, n_tm):
            tm_copy(s, d).wait_recv()
        total = tm_in[s, 0]
        for k in range(1, n_tm):
            total += tm_in[s, k]
        done[s, pl.ds(my_sub * part, part)] = total
        for d in range(1, n_sub):
            fin_copy(s, d).start()

    def finish(s):
        for d in range(1, n_sub):
            fin_copy(s, d).wait_recv()
        out_ref[s] = done[s]

    delay = -(-(n_chan - 1) * LAG // SPLIT)

    def turn(u, carry):
        pl.when(u < steps)(functools.partial(own_panel, u))
        for k in range(SPLIT):
            relay(u * SPLIT + k)

        @pl.when(u == 0)
        def _():
            for w in range(frames):
                value = white_ref[w].astype(jnp.float32)
                plain[w] = value
                for h in range(2):
                    swapped[w, :, h * half : (h + 1) * half] = pltpu.roll(
                        value[:, h * half : (h + 1) * half], half // 2, 1)

        for late, work in enumerate((compute, sub_sum, tm_sum, finish)):
            s = u - delay - late
            pl.when((s >= 0) & (s < steps))(functools.partial(work, s))
        return carry

    lax.fori_loop(0, steps + delay + 3, turn, 0)

    def drain_chunk(c, carry):
        @pl.when(me < n_chan - 1)
        def _():
            up(c).wait_send()

        @pl.when(me > 0)
        def _():
            down(c).wait_send()
        return carry

    lax.fori_loop(0, chunks, drain_chunk, 0)
    for k, move in enumerate(moves):
        pl.when(exists(*move))(lambda k=k: copy(k).wait_send())

    def drain_step(s, carry):
        for d in range(1, n_sub):
            sub_copy(s, d).wait_send()
            fin_copy(s, d).wait_send()
        for d in range(1, n_tm):
            tm_copy(s, d).wait_send()
        return carry

    lax.fori_loop(0, steps, drain_step, 0)


def lag_pair(scale):
    bins, parts = column_maps()
    lag = np.arange(LAGS) - LAGS // 2
    angle = 2.0 * np.pi * ((bins[:, None] * lag[None, :]) % WIN) / WIN
    real = np.cos(angle) * scale
    imag = np.where(parts[:, None] == 0, np.sin(angle), -np.sin(angle)) * scale
    full = np.concatenate([real, imag]).astype(np.float32)
    return jnp.asarray(full).astype(jnp.bfloat16)


GROUP = 4
AHEAD = 1


def split_kernel(frames, channels, side, steps, n_chan, n_tm, n_sub, sp_hbm, edges_hbm, owner_hbm, panel_hbm,
                 taps_hbm, pick_hbm, raw_hbm, table_hbm, lag_hbm, out_hbm,
                 sp_ref, edges_ref, owner_ref, panel_ref, taps_ref, pick_ref, raw_ref, table_ref, lag_ref,
                 spec, mixed, halo_ext, halo_win, ends_ref, rim_ref, power_ref,
                 time_in, chan_out, chan_in, corner_out, corner_in, white_ref, picks, chosen, pan, acc,
                 own_lag, sub_out, sub_in, z_out, z_in, done,
                 load_sem, halo_send, halo_recv, far_sem, pick_send, pick_recv, z_send, z_recv, x_send, x_recv,
                 sub_send, sub_recv, r_send, r_recv, a_send, a_recv, out_sem, *white_in):
    f32, bf16 = jnp.float32, jnp.bfloat16
    me, my_tm, my_sub = lax.axis_index("chan"), lax.axis_index("tm"), lax.axis_index("sub")
    n_time = n_tm * n_sub
    now = my_tm * n_sub + my_sub
    samples = frames * WIN
    n_taps = taps_ref.shape[0]
    depth = WIN + 2 * LANES
    panels = channels // P_SIZE
    per = frames // n_chan
    spd = steps // n_time
    spt = spd * n_sub
    mine, theirs = white_in[:per], white_in[per:]
    loads = [
        pltpu.make_async_copy(source, target, load_sem.at[k])
        for k, (source, target) in enumerate([
            (raw_hbm, raw_ref), (taps_hbm, taps_ref), (pick_hbm, pick_ref), (sp_hbm, sp_ref),
            (edges_hbm, edges_ref), (owner_hbm, owner_ref), (panel_hbm, panel_ref),
            (table_hbm, table_ref), (lag_hbm, lag_ref),
        ])
    ]
    for load in loads[1:] + loads[:1]:
        load.start()

    def at_time(dt):
        at = lax.rem(now + dt + n_time, n_time)
        return {"tm": lax.div(at, n_sub), "sub": lax.rem(at, n_sub)}

    def peer(dc, dt):
        return {"chan": lax.rem(me + dc + n_chan, n_chan), **at_time(dt)}

    def exists(dc, dt):
        return (me + dc >= 0) & (me + dc < n_chan) & (now + dt >= 0) & (now + dt < n_time)

    moves = [(0, 1), (0, -1), (1, 0), (-1, 0), (1, 1), (1, -1), (-1, 1), (-1, -1)]
    barrier = pltpu.get_barrier_semaphore()
    for dt in range(1, n_time):
        pl.semaphore_signal(barrier, inc=1, device_id=at_time(dt), device_id_type=MESH)
    for move in moves[2:]:
        @pl.when(exists(*move))
        def _(move=move):
            pl.semaphore_signal(barrier, inc=1, device_id=peer(*move), device_id_type=MESH)

    for load in loads[1:]:
        load.wait()
    taps = taps_ref[...].astype(f32).reshape(1, n_taps)
    taps = jnp.concatenate([taps, jnp.zeros((1, depth - n_taps), f32)], axis=1)
    shift = LANES - (n_taps - 1) // 2
    rolled = pltpu.roll(jnp.broadcast_to(taps, (WIN, depth)), shift, 1, stride=1, stride_axis=0)
    fir_w = jnp.transpose(rolled).astype(bf16)
    parts = [fir_w[LANES : LANES + WIN]] * 2 + [fir_w[:LANES], fir_w[LANES + WIN :]] * 2
    fir_pair = jnp.concatenate(parts, axis=0)
    near = (jnp.abs(bins_of((WIN, WIN), 0) - bins_of((WIN, WIN), 1)) <= 4).astype(bf16)
    row_bins = bins_of((1, WIN), 1)
    count = jnp.minimum(row_bins + 4, WIN // 2 - 1) - jnp.maximum(row_bins - 4, 0) + 1
    taper = taper_row(edges_ref)

    def fir(block, first=0, last=depth):
        return jnp.dot(block, fir_w[first:last], preferred_element_type=f32)

    def taps_at(offset):
        total = jnp.zeros(offset.shape, f32)
        for m in range(2 * side + 1):
            total = jnp.where(offset == m - side, sp_ref[m], total)
        return total

    def two(value):
        high = value.astype(bf16)
        return high, (value - high.astype(f32)).astype(bf16)

    def across(matrix, value):
        m_high, m_low = matrix
        v_high, v_low = two(value)
        left = jnp.concatenate([m_high, m_low, m_high], axis=1)
        right = jnp.concatenate([v_high, v_high, v_low], axis=0)
        return jnp.dot(left, right, preferred_element_type=f32)

    def iota(shape, axis):
        return lax.broadcasted_iota(jnp.int32, shape, axis)

    square = (channels, channels)
    spatial = two(taps_at(iota(square, 1) - iota(square, 0)))
    rim = channels - 16
    stacked = jnp.concatenate(spatial, axis=0)
    row, column = iota((16, frames * 16), 0), iota((16, frames * 16), 1)
    row_channel = jnp.where(row < 8, row, row + rim)
    spot = lax.rem(column, 16)
    column_channel = jnp.where(spot < side, spot - side, jnp.where(spot < 2 * side, channels + spot - side, 4 * channels))
    base = taps_at(column_channel - row_channel)
    frame_of = lax.div(column, 16)
    rim_matrix = two(jnp.concatenate([jnp.where(frame_of == w, base, 0.0) for w in range(frames)], axis=0))
    for k in range(2):
        for at in (0, frames + 1):
            mixed[k, at] = jnp.zeros((channels, WIN), bf16)
    loads[0].wait()
    ends = (slice(channels - side, channels), slice(0, side))
    sides = (slice(samples - LANES, samples), slice(0, LANES))
    for k in range(2):
        chan_out[k] = raw_ref[ends[k]]
        for h in range(2):
            corner_out[2 * k + h] = raw_ref[ends[k], sides[h]]

    def copy(k):
        dc, dt = moves[k]
        if k < 2:
            src, dst = raw_ref.at[:, sides[k]], time_in.at[k]
        elif k < 4:
            src, dst = chan_out.at[k - 2], chan_in.at[k - 2]
        else:
            src, dst = corner_out.at[k - 4], corner_in.at[k - 4]
        return pltpu.make_async_remote_copy(
            src_ref=src, dst_ref=dst, send_sem=halo_send.at[k], recv_sem=halo_recv.at[k],
            device_id=peer(dc, dt), device_id_type=MESH)

    greeted = sum(exists(*move).astype(jnp.int32) for move in moves[2:])
    pl.semaphore_wait(barrier, n_time - 1 + greeted)
    for k in (2, 3, 0, 1, 4, 5, 6, 7):
        pl.when(exists(*moves[k]))(lambda k=k: copy(k).start())

    inner = (me > 0) & (me < n_chan - 1)

    def token(way):
        pl.semaphore_signal(far_sem.at[way], inc=1, device_id={"chan": me + 1 - 2 * way}, device_id_type=MESH)

    def relay_tokens(k):
        for way, distance in ((0, me), (1, n_chan - 1 - me)):
            @pl.when(distance >= k + 1)
            def _():
                pl.semaphore_wait(far_sem.at[way], 1)
            pl.when((distance >= k + 1) & inner)(lambda: token(way))

    for way in range(2):
        pl.when(inner)(lambda: token(way))

    def pick_copy(d):
        return pltpu.make_async_remote_copy(
            src_ref=pick_ref, dst_ref=picks.at[me], send_sem=pick_send.at[0], recv_sem=pick_recv.at[0],
            device_id={"chan": lax.rem(me + d, n_chan)}, device_id_type=MESH)

    def pick_all():
        rest = picks.at[pl.ds(0, n_chan - 1)]
        return pltpu.make_async_remote_copy(
            src_ref=rest, dst_ref=rest, send_sem=pick_send.at[0], recv_sem=pick_recv.at[0],
            device_id={"chan": lax.rem(me + 1, n_chan)}, device_id_type=MESH)

    for w in range(frames):
        got = jnp.dot(stacked, raw_ref[:, w * WIN : (w + 1) * WIN], preferred_element_type=f32)
        mixed[0, w + 1], mixed[1, w + 1] = two(got[:channels] + got[channels:])

    def filtered(g):
        sides = []
        for k in range(2):
            sides.append(mixed[k, g + 1 : g + 1 + GROUP])
        for k in range(2):
            sides += [mixed[k, g : g + GROUP, :, WIN - LANES :], mixed[k, g + 2 : g + 2 + GROUP, :, :LANES]]
        windows = jnp.concatenate(sides, axis=2).reshape(GROUP * channels, 2 * depth)
        return jnp.dot(windows, fir_pair, preferred_element_type=f32)

    power = jnp.zeros((channels, WIN), f32)
    ready = filtered(0)
    for g in range(0, frames, GROUP):
        part, ready = ready, filtered(g + GROUP) if g + GROUP < frames else None
        spectra = jnp.dot(part.astype(bf16), table_ref[...], preferred_element_type=f32)
        part, spectra = part.reshape(GROUP, channels, WIN), spectra.reshape(GROUP, channels, WIN)
        for k in range(GROUP):
            w = g + k
            if w in (0, frames - 1):
                ends_ref[min(w, 1)] = part[k]
                continue
            rim_ref[w, :8] = part[k, :8]
            rim_ref[w, 8:] = part[k, channels - 8 :]
            spec[w] = spectra[k]
            power += spectra[k] * spectra[k]
    power_ref[...] = power
    relay_tokens(1)

    for k, (dc, dt) in enumerate(moves):
        there = exists(-dc, -dt)
        pl.when(there)(lambda k=k: copy(k).wait_recv())
        buf, slot = (time_in, k) if k < 2 else (chan_in, k - 2) if k < 4 else (corner_in, k - 4)

        @pl.when(jnp.logical_not(there))
        def _():
            buf[slot] = jnp.zeros(buf.shape[1:], buf.dtype)

    def rows(low, high):
        width = low.shape[1]
        spare = jnp.zeros((16 - 2 * side, width), f32)
        both = [low.astype(f32), high.astype(f32), spare]
        return jnp.concatenate(both, axis=0).astype(bf16)

    halo_ext[:, LANES : LANES + samples] = rows(chan_in[0], chan_in[1])
    halo_ext[:, :LANES] = rows(corner_in[0], corner_in[2])
    halo_ext[:, LANES + samples :] = rows(corner_in[1], corner_in[3])
    for w in range(frames):
        halo_win[w] = halo_ext[:, w * WIN : w * WIN + depth]
    halo = fir(halo_win[...].reshape(frames * 16, depth))
    late = [fir(time_in[k], k * (depth - LANES), k * (depth - LANES) + LANES) for k in range(2)]
    rim_part = across(rim_matrix, halo).reshape(frames, 16, WIN)
    late = [across(spatial, value) for value in late]
    blocks = [rim_ref[1 : frames - 1] + rim_part[1 : frames - 1]]
    blocks[0] = blocks[0].reshape((frames - 2) * 16, WIN)
    for k, w in enumerate((0, frames - 1)):
        whole = ends_ref[k] + late[k]
        blocks += [whole[:8] + rim_part[w, :8], whole[8 : channels - 8], whole[channels - 8 :] + rim_part[w, 8:]]
    shaped = jnp.concatenate(blocks, axis=0).astype(bf16)
    spectra = jnp.dot(shaped, table_ref[...], preferred_element_type=f32)
    rims, whole = spectra[: (frames - 2) * 16].reshape(frames - 2, 16, WIN), spectra[(frames - 2) * 16 :]
    whole = whole.reshape(2, channels, WIN)
    for w in range(1, frames - 1):
        spec[w, :8] = rims[w - 1, :8]
        spec[w, channels - 8 :] = rims[w - 1, 8:]
    for k, w in enumerate((0, frames - 1)):
        spec[w] = whole[k]
    rims = jnp.sum(rims * rims, axis=0)
    inside = power_ref[8 : channels - 8]
    power = jnp.concatenate([rims[:8], inside, rims[8:]], axis=0) + jnp.sum(whole * whole, axis=0)
    for k in range(2, n_chan - 1):
        relay_tokens(k)
    for d in range(1, n_chan):
        pick_copy(d).start()
    level = jnp.dot(
        jnp.concatenate(two(power), axis=1), jnp.concatenate([near, near], axis=0), preferred_element_type=f32)
    level = level / (count.astype(f32) * frames)
    factor = taper / jnp.sqrt(level + 1e-06)

    def whiten(w):
        return (spec[w] * factor).astype(bf16).reshape(panels, P_SIZE, WIN)

    def block_of(q):
        return pl.ds(q * panels, panels)

    def z_copy(j, d):
        to = lax.rem(me + d, n_chan)
        return pltpu.make_async_remote_copy(
            src_ref=white_ref.at[to * per + j], dst_ref=mine[j].at[block_of(me)],
            send_sem=z_send.at[j % AHEAD, d - 1], recv_sem=z_recv.at[j, d - 1],
            device_id={"chan": to}, device_id_type=MESH)

    def x_copy(j, e, k):
        at = slice(None) if e is None else block_of(lax.rem(me - e + n_chan, n_chan))
        return pltpu.make_async_remote_copy(
            src_ref=mine[j].at[at], dst_ref=theirs[j].at[k - 1, at],
            send_sem=x_send.at[j, k - 1], recv_sem=x_recv.at[j, k - 1],
            device_id={"tm": lax.rem(my_tm + k, n_tm)}, device_id_type=MESH)

    near_first = sorted(range(1, n_chan), key=lambda d: (min(d, n_chan - d), d))
    far_first = near_first[::-1]
    for j in range(per):
        for d in far_first:
            w = lax.rem(me + d, n_chan) * per + j
            white_ref[w] = whiten(w)
            if j < AHEAD:
                z_copy(j, d).start()
        mine[j][block_of(me)] = whiten(me * per + j)
        for k in range(1, n_tm):
            x_copy(j, 0, k).start()
    def choose():
        picks[me] = pick_ref[...]
        pick_all().wait_recv()
        for i in range(spt):
            for q in range(n_chan):
                pick = jnp.broadcast_to(picks[q, pl.ds(my_tm * spt + i, 1)], (P_SIZE, channels))
                hit = (pick == iota((P_SIZE, channels), 0)).astype(f32)
                chosen[i, q * channels : (q + 1) * channels] = jnp.transpose(hit).astype(bf16)

    half = WIN // 2

    def source(unit):
        j, k = unit
        return mine[j] if k == 0 else theirs[j].at[k - 1]

    def gather(units):
        for i in range(spt):
            s = my_tm * spt + i
            at = owner_ref[s] * panels + panel_ref[s]
            for u, unit in enumerate(units):
                value = source(unit)[at]
                wide = value.astype(f32)
                turn = [pltpu.roll(wide[:, h * half : (h + 1) * half], half // 2, 1) for h in range(2)]
                pan[i, u, :, :WIN] = value
                pan[i, u, :, WIN:] = jnp.concatenate(turn, axis=1).astype(bf16)

    everyone = n_chan * channels

    def receivers(unit):
        return source(unit)[...].reshape(everyone, WIN).astype(f32)

    def products(units, i, values):
        p = q = None
        for u, value in enumerate(values):
            partner = jnp.dot(chosen[i], pan[i, u], preferred_element_type=f32)
            dp, dq = value * partner[:, :WIN], value * partner[:, WIN:]
            p, q = (dp, dq) if u == 0 else (p + dp, q + dq)
        return p, q

    def accumulate(units, first):
        gather(units)
        values = [receivers(unit) for unit in units]

        def step(i, carry):
            p, q = products(units, i, values)
            if not first:
                p += acc[i, 0]
                q += acc[i, 1]
            acc[i, 0] = p
            acc[i, 1] = q
            return carry

        for i in range(spt):
            step(i, 0)

    def forward(j):
        for d in near_first:
            z_copy(j, d).wait_send()
            if j + AHEAD < per:
                z_copy(j + AHEAD, d).start()
            z_copy(j, d).wait_recv()
            for k in range(1, n_tm):
                x_copy(j, d, k).start()

    def arrive(j):
        for k in range(1, n_tm):
            x_copy(j, None, k).wait_recv()

    def others(j):
        return [(j, k) for k in range(1, n_tm)]

    last = per - 1
    for j in range(per):
        forward(j)
        if j == 0:
            choose()
        units = [(j, 0)]
        if j > 0:
            arrive(j - 1)
            units += others(j - 1)
        accumulate(units, j == 0)
    arrive(last)
    gather(others(last))

    def summed_products(i):
        p, q = products(others(last), i, [receivers(unit) for unit in others(last)])
        return (p + acc[i, 0]).astype(bf16), (q + acc[i, 1]).astype(bf16)

    def lagged(both):
        lags = jnp.dot(both[0], lag_ref[:WIN], preferred_element_type=f32)
        lags += jnp.dot(both[1], lag_ref[WIN:], preferred_element_type=f32)
        return lags

    def sub_copy(k, d):
        to = lax.rem(my_sub + d, n_sub)
        return pltpu.make_async_remote_copy(
            src_ref=sub_out.at[k, d - 1], dst_ref=sub_in.at[k, d - 1],
            send_sem=sub_send.at[k, d - 1], recv_sem=sub_recv.at[k, d - 1],
            device_id={"sub": to}, device_id_type=MESH)

    def r_copy(k, d):
        to = lax.rem(me + d, n_chan)
        return pltpu.make_async_remote_copy(
            src_ref=z_out.at[k, d - 1], dst_ref=z_in.at[k, d - 1], send_sem=r_send.at[k], recv_sem=r_recv.at[k],
            device_id={"chan": to}, device_id_type=MESH)

    def r_all(k):
        return pltpu.make_async_remote_copy(
            src_ref=z_out.at[k], dst_ref=z_in.at[k], send_sem=r_send.at[k], recv_sem=r_recv.at[k],
            device_id={"chan": lax.rem(me + 1, n_chan)}, device_id_type=MESH)

    def a_copy(k, d):
        return pltpu.make_async_remote_copy(
            src_ref=done.at[k], dst_ref=out_hbm.at[now * spd + k], send_sem=a_send.at[k], recv_sem=a_recv.at[k],
            device_id=at_time(d), device_id_type=MESH)

    def a_all(k):
        rest = out_hbm.at[pl.ds(0, n_time - 1)]
        return pltpu.make_async_remote_copy(
            src_ref=rest, dst_ref=rest, send_sem=a_send.at[k], recv_sem=a_recv.at[k],
            device_id=at_time(1), device_id_type=MESH)

    def store(k):
        return pltpu.make_async_copy(done.at[k], out_hbm.at[now * spd + k], out_sem.at[k])

    work = [(d, k) for d in [*range(1, n_sub), 0] for k in range(spd)]

    def at_step(d, k):
        return lax.rem(my_sub + d, n_sub) * spd + k

    kept = []
    coming = summed_products(at_step(*work[0]))
    for n, (d, k) in enumerate(work):
        current, coming = coming, summed_products(at_step(*work[n + 1])) if n + 1 < len(work) else None
        lags = lagged(current)
        if d > 0:
            sub_out[k, d - 1] = lags.astype(bf16)
            sub_copy(k, d).start()
            continue
        own_lag[k] = lags
        for other in range(1, n_sub):
            sub_copy(k, other).wait_recv()

        def summed(q, k=k):
            here = pl.ds(q * channels, channels)
            value = own_lag[k, here]
            for other in range(1, n_sub):
                value += sub_in[k, other - 1, here].astype(f32)
            return value

        for way in far_first:
            z_out[k, way - 1] = summed(lax.rem(me + way, n_chan)).astype(bf16)
            r_copy(k, way).start()
        kept.append(summed(me))
    picked = []
    for k in range(spd):
        pick = jnp.broadcast_to(pick_ref[pl.ds(now * spd + k, 1)], (LAGS, channels))
        picked.append(jnp.transpose(pick.astype(f32)).astype(jnp.int32))
    receiver = me * channels + lax.broadcasted_iota(jnp.int32, (channels, LAGS), 0)
    for k in range(spd):
        s = now * spd + k
        value = kept[k]
        r_all(k).wait_recv()
        for d in range(1, n_chan):
            value += z_in[k, d - 1].astype(f32)
        start = owner_ref[s] * channels + panel_ref[s] * P_SIZE
        far = jnp.abs(receiver - (start + picked[k])) > REACH
        done[k] = jnp.where(far, 0.0, value).astype(bf16)
        for d in range(1, n_time):
            a_copy(k, d).start()
        store(k).start()
    for k in range(spd):
        if n_time > 1:
            a_all(k).wait_recv()
    for k, move in enumerate(moves):
        pl.when(exists(*move))(lambda k=k: copy(k).wait_send())
    pick_all().wait_send()
    for k in range(1, n_tm):
        for j in range(per):
            x_copy(j, None, k).wait_send()
    for k in range(spd):
        for d in range(1, n_sub):
            sub_copy(k, d).wait_send()
        r_all(k).wait_send()
        if n_time > 1:
            a_all(k).wait_send()
    for k in range(spd):
        store(k).wait()


VMEM = pl.BlockSpec(memory_space=pltpu.VMEM)


def relay(raw, fir_taps, spatial_taps, band_edges, source_owner, source_panel, source_pick):
    channels, samples = raw.shape
    margin = (fir_taps.shape[0] - 1) // 2
    side = spatial_taps.shape[0] // 2
    frames = samples // WIN
    steps = source_owner.shape[0]
    times = ("tm", "sub")
    count = lax.axis_size(times)
    n_chan = lax.axis_size("chan")
    n_tm, n_sub = lax.axis_size("tm"), lax.axis_size("sub")
    depth = WIN + 2 * LANES
    first = LANES - margin
    taps = jnp.pad(fir_taps.astype(jnp.float32), (first, depth - first - fir_taps.shape[0]))[None, :]
    total = frames * n_tm * n_sub
    lag_table = lag_tables(1.0 / math.sqrt(total * (WIN // 2)))
    chunks = steps * SPLIT
    flow = pltpu.VMEM((chunks, frames // SPLIT, P_SIZE, WIN), jnp.bfloat16)
    part = channels // n_sub
    dma = pltpu.SemaphoreType.DMA
    any_space = pl.BlockSpec(memory_space=pltpu.HBM)
    bf16, f32 = jnp.bfloat16, jnp.float32
    return pl.pallas_call(
        functools.partial(relay_kernel, frames, channels, side, steps, n_chan, n_tm, n_sub),
        out_shape=jax.ShapeDtypeStruct((steps, channels, LAGS), f32),
        in_specs=[any_space] * 9,
        out_specs=VMEM,
        scratch_shapes=[
            pltpu.SMEM(spatial_taps.shape, f32),
            pltpu.SMEM(band_edges.shape, jnp.int32),
            pltpu.SMEM(source_owner.shape, jnp.int32),
            pltpu.SMEM(source_panel.shape, jnp.int32),
            pltpu.VMEM(taps.shape, f32),
            pltpu.VMEM(source_pick.shape, jnp.int32),
            pltpu.VMEM(raw.shape, bf16),
            pltpu.VMEM((WIN, WIN), bf16),
            pltpu.VMEM((2 * WIN, LAGS), f32),
            pltpu.VMEM((2, channels + 16, WIN), f32),
            pltpu.VMEM((frames, channels, WIN), f32),
            pltpu.VMEM((channels + 16, samples + 2 * LANES), bf16),
            pltpu.VMEM((2, channels, LANES), bf16),
            pltpu.VMEM((2, side, samples), bf16),
            pltpu.VMEM((2, side, samples), bf16),
            pltpu.VMEM((4, side, LANES), bf16),
            pltpu.VMEM((4, side, LANES), bf16),
            dma((8,)), dma((8,)), dma((9,)),
            pltpu.VMEM((frames, channels, WIN), bf16),
            pltpu.VMEM((steps, frames, P_SIZE, WIN), bf16),
            pltpu.VMEM((steps, channels, P_SIZE), bf16),
            pltpu.VMEM((steps, channels, LANES), jnp.int32),
            pltpu.VMEM((frames, channels, WIN), f32),
            pltpu.VMEM((frames, channels, WIN), f32),
            flow, flow, flow, flow,
            pltpu.VMEM((steps, channels, LAGS), f32),
            pltpu.VMEM((steps, n_sub - 1, part, LAGS), f32),
            pltpu.VMEM((steps, n_tm, part, LAGS), f32),
            pltpu.VMEM((steps, channels, LAGS), f32),
            dma((chunks,)), dma((chunks,)), dma((chunks,)), dma((chunks,)),
            dma((steps, n_sub - 1)), dma((steps, n_sub - 1)),
            dma((steps, n_tm - 1)), dma((steps, n_tm - 1)),
            dma((steps, n_sub - 1)), dma((steps, n_sub - 1)),
        ],
        compiler_params=pltpu.CompilerParams(
            vmem_limit_bytes=64 * 2**20, collective_id=0, has_side_effects=True),
        name="correlate",
    )(spatial_taps, band_edges, source_owner, source_panel, taps, source_pick, raw, spectral_table(), lag_table)


def split(raw, fir_taps, spatial_taps, band_edges, source_owner, source_panel, source_pick):
    channels, samples = raw.shape
    side = spatial_taps.shape[0] // 2
    frames = samples // WIN
    steps = source_owner.shape[0]
    n_chan, n_tm, n_sub = lax.axis_size("chan"), lax.axis_size("tm"), lax.axis_size("sub")
    n_time = n_tm * n_sub
    depth = WIN + 2 * LANES
    lag_table = lag_pair(1.0 / math.sqrt(frames * n_time * (WIN // 2)))
    per, spd = frames // n_chan, steps // n_time
    spt = spd * n_sub
    panels, everyone = channels // P_SIZE, n_chan * channels
    dma, any_space = pltpu.SemaphoreType.DMA, pl.BlockSpec(memory_space=pltpu.HBM)
    bf16, f32 = jnp.bfloat16, jnp.float32
    return pl.pallas_call(
        functools.partial(split_kernel, frames, channels, side, steps, n_chan, n_tm, n_sub),
        out_shape=jax.ShapeDtypeStruct((steps, channels, LAGS), bf16),
        in_specs=[any_space] * 9,
        out_specs=any_space,
        scratch_shapes=[
            pltpu.SMEM(spatial_taps.shape, f32),
            pltpu.SMEM(band_edges.shape, jnp.int32),
            pltpu.SMEM(source_owner.shape, jnp.int32),
            pltpu.SMEM(source_panel.shape, jnp.int32),
            pltpu.VMEM(fir_taps.shape, bf16),
            pltpu.VMEM(source_pick.shape, jnp.int32),
            pltpu.VMEM(raw.shape, bf16),
            pltpu.VMEM((WIN, WIN), bf16),
            pltpu.VMEM(lag_table.shape, bf16),
            pltpu.VMEM((frames, channels, WIN), f32),
            pltpu.VMEM((2, frames + 2, channels, WIN), bf16),
            pltpu.VMEM((16, samples + 2 * LANES), bf16),
            pltpu.VMEM((frames, 16, depth), bf16),
            pltpu.VMEM((2, channels, WIN), f32),
            pltpu.VMEM((frames, 16, WIN), f32),
            pltpu.VMEM((channels, WIN), f32),
            pltpu.VMEM((2, channels, LANES), bf16),
            pltpu.VMEM((2, side, samples), bf16),
            pltpu.VMEM((2, side, samples), bf16),
            pltpu.VMEM((4, side, LANES), bf16),
            pltpu.VMEM((4, side, LANES), bf16),
            pltpu.VMEM((frames, panels, P_SIZE, WIN), bf16),
            pltpu.VMEM((n_chan, *source_pick.shape), jnp.int32),
            pltpu.VMEM((spt, everyone, P_SIZE), bf16),
            pltpu.VMEM((spt, n_tm, P_SIZE, 2 * WIN), bf16),
            pltpu.VMEM((spt, 2, everyone, WIN), f32),
            pltpu.VMEM((spd, everyone, LAGS), f32),
            pltpu.VMEM((spd, max(n_sub - 1, 1), everyone, LAGS), bf16),
            pltpu.VMEM((spd, max(n_sub - 1, 1), everyone, LAGS), bf16),
            pltpu.VMEM((spd, n_chan - 1, channels, LAGS), bf16),
            pltpu.VMEM((spd, n_chan - 1, channels, LAGS), bf16),
            pltpu.VMEM((spd, channels, LAGS), bf16),
            dma((9,)), dma((8,)), dma((8,)), pltpu.SemaphoreType.REGULAR((2,)),
            dma((1,)), dma((1,)), dma((AHEAD, n_chan - 1)), dma((per, n_chan - 1)),
            dma((per, max(n_tm - 1, 1))), dma((per, max(n_tm - 1, 1))),
            dma((spd, max(n_sub - 1, 1))), dma((spd, max(n_sub - 1, 1))),
            dma((spd,)), dma((spd,)), dma((spd,)), dma((spd,)), dma((spd,)),
        ] + [pltpu.VMEM((n_chan * panels, P_SIZE, WIN), bf16)] * per
        + [pltpu.VMEM((max(n_tm - 1, 1), n_chan * panels, P_SIZE, WIN), bf16)] * per,
        compiler_params=pltpu.CompilerParams(
            vmem_limit_bytes=60 * 2**20, collective_id=0, has_side_effects=True),
        name="correlate",
    )(spatial_taps, band_edges, source_owner, source_panel, fir_taps, source_pick, raw, spectral_table(), lag_table).astype(f32)


def shards(*blocks):
    frames, steps = blocks[0].shape[1] // WIN, blocks[4].shape[0]
    chans = lax.axis_size("chan")
    even = chans > 1 and frames % chans == 0 and frames % GROUP == 0 and steps % lax.axis_size(("tm", "sub")) == 0
    return (split if even else relay)(*blocks)


def solution(mesh):
    placed = (
        P(("grp", "chan"), ("tm", "sub")),
        P(),
        P(),
        P(),
        P("grp"),
        P(),
        P(None, ("grp", "chan")),
    )
    return jax.shard_map(
        shards,
        mesh=mesh,
        in_specs=placed,
        out_specs=P(None, ("grp", "chan"), None),
        check_vma=False,
    )
```
